32 devices in a mesh: dp: 16 (over z, x, core), tensor: 2 (over y).
Axes of the slice: x: 2, y: 2, z: 4, core: 2. Of those that a mesh axis runs over, the one named last changes fastest.
Arguments:
- inputs: float32 [64, 320, 1024], P(('dp', 'tensor')), may hold values from -6 to 6
- key_mask: int32 [64, 256], P('dp'), may hold values 0 or 1
- ln1_gain: float32 [1024], P('dp'), may hold values from 0.1 to 1.9
- ln1_bias: float32 [1024], P('dp'), may hold values from -1.8 to 1.8
- w_qkv: float32 [3, 1024, 1024], P(None, 'dp', 'tensor'), may hold values from -0.1875 to 0.1875
- qv_bias: float32 [2, 1024], P(None, 'dp'), may hold values from -0.6 to 0.6
- w_proj: float32 [1024, 1024], P('tensor', 'dp'), may hold values from -3.5 to 3.5
- proj_bias: float32 [1024], P('dp'), may hold values from -1.8 to 1.8
- ln2_gain: float32 [1024], P('dp'), may hold values from 0.1 to 1.9
- ln2_bias: float32 [1024], P('dp'), may hold values from -1.8 to 1.8
- w_fc1: float32 [1024, 4096], P('dp', 'tensor'), may hold values from -0.1875 to 0.1875
- fc1_bias: float32 [4096], P('dp'), may hold values from -3 to 3
- w_fc2: float32 [4096, 1024], P('tensor', 'dp'), may hold values from -0.09375 to 0.09375
- fc2_bias: float32 [1024], P('dp'), may hold values from -1.8 to 1.8
- out_grad: float32 [64, 320, 1024], P(('dp', 'tensor')), may hold values from -6 to 6
Outputs:
- activations: float32 [64, 320, 1024], P(('dp', 'tensor'))
- input_grad: float32 [64, 320, 1024], P(('dp', 'tensor'))
- ln1_gain_grad: float32 [1024], P('dp')
- ln1_bias_grad: float32 [1024], P('dp')
- w_qkv_grad: float32 [3, 1024, 1024], P(None, 'dp', 'tensor')
- qv_bias_grad: float32 [2, 1024], P(None, 'dp')
- w_proj_grad: float32 [1024, 1024], P('tensor', 'dp')
- proj_bias_grad: float32 [1024], P('dp')
- ln2_gain_grad: float32 [1024], P('dp')
- ln2_bias_grad: float32 [1024], P('dp')
- w_fc1_grad: float32 [1024, 4096], P('dp', 'tensor')
- fc1_bias_grad: float32 [4096], P('dp')
- w_fc2_grad: float32 [4096, 1024], P('tensor', 'dp')
- fc2_bias_grad: float32 [1024], P('dp')
The draws below stay inside these ranges and needn't reach their ends.
All inputs are finite; a program needn't handle non-finite values. No bound on the sum of `key_mask` on one device may be relied on, other than what follows from the above.
Results may differ from the reference program's by a relative error of at most 0.015.
Values may be sent and summed in bfloat16 or wider, within the bound.
No kernel may reach another device: no remote copies, remote signals or barrier semaphores. Data moves between devices by JAX's collectives and lax.ppermute only.
A program may use at most 192 MiB of HBM per device.

```python
import jax
import jax.numpy as jnp
from jax import lax

D = 1024
HEADS = 16
HEAD_DIM = 64
FF = 4096
BUF = 64
IMG_TOK = 256
SEQ = 320
IMAGES = 64


def set_ends(result, rng, low, high):
    place = [jax.random.randint(jax.random.fold_in(rng, axis), (), 0, length) for axis, length in enumerate(result.shape)]
    main_axis = result.shape.index(max(result.shape))
    neighbour = place[:main_axis] + [(place[main_axis] + 1) % result.shape[main_axis]] + place[main_axis + 1:]
    return result.at[tuple(place)].set(low).at[tuple(neighbour)].set(high)


def spiked(drawn, key, source, target, shards_of, factor):
    owner, partner = [(jnp.arange(drawn.shape[axis_at]) // (drawn.shape[axis_at] // shards_of)).reshape([-1 if axis == axis_at else 1 for axis in range(drawn.ndim)]) for axis_at in (source, target)]
    chosen = jax.random.permutation(key, shards_of)[partner]
    strong = (owner == chosen) | (owner == (partner + shards_of // 2) % shards_of)
    return jnp.where(strong, factor * drawn, drawn)


def level_of(rng, extent, shards, least, largest):
    factor_of, own = 1.0, jax.random.fold_in(rng, 6)
    for position, blocks in shards:
        heights = jnp.exp(jax.random.uniform(jax.random.fold_in(own, position), (blocks,), jnp.float32, least / len(shards), largest / len(shards)))
        factor_of = factor_of * jnp.repeat(heights, extent[position] // blocks).reshape([-1 if axis == position else 1 for axis in range(len(extent))])
    return factor_of


def noise(rng, shape, deviation, bound, shards=(), held_as=jnp.bfloat16):
    factor_of = level_of(rng, shape, shards, -0.22, 0.18) if shards else 1.0
    drawn = jax.random.normal(rng, shape, jnp.float32) * deviation * factor_of
    return jnp.minimum(jnp.maximum(drawn, -bound), bound).astype(held_as)


def gaussian_with(stream_key, dims, width, limit, cuts, heavy, kind=jnp.bfloat16):
    array = width * jax.random.normal(stream_key, dims, jnp.float32)
    if cuts:
        array = array * level_of(stream_key, dims, cuts, -0.22, 0.18)
    return jnp.clip(spiked(array, jax.random.fold_in(stream_key, 3), *heavy), -limit, limit).astype(kind)


def setup_inputs(seed: int = 0) -> dict:
    seeds = jax.random.split(jax.random.key(seed), 16)
    inputs = noise(seeds[0], (IMAGES, SEQ, D), 1.0, 6.0, ((0, 32),), jnp.float32)
    key_mask = set_ends((jax.random.randint(seeds[1], (IMAGES, IMG_TOK), 0, 4) < 3).astype(jnp.int32), jax.random.fold_in(seeds[1], 1), 0, 1)
    ln1_gain = jnp.clip(1.0 + 0.18 * jax.random.normal(seeds[2], (D,), jnp.float32), 0.1, 1.9)
    ln1_bias = noise(seeds[3], (D,), 0.3, 1.8, ((0, 16),), jnp.float32)
    w_qkv = noise(seeds[4], (3, D, D), D ** -0.5, 0.1875, ((1, 16), (2, 2)), jnp.float32)
    qv_bias = noise(seeds[5], (2, D), 0.1, 0.6, ((1, 16),), jnp.float32)
    w_proj = noise(seeds[6], (D, D), (D // SEQ) ** -0.5, 3.5, ((0, 2), (1, 16)), jnp.float32)
    proj_bias = noise(seeds[7], (D,), 0.3, 1.8, ((0, 16),), jnp.float32)
    ln2_gain = jnp.clip(1.0 + 0.18 * jax.random.normal(seeds[8], (D,), jnp.float32), 0.1, 1.9)
    ln2_bias = noise(seeds[9], (D,), 0.3, 1.8, ((0, 16),), jnp.float32)
    w_fc1 = noise(seeds[10], (D, FF), D ** -0.5, 0.1875, ((0, 16), (1, 2)), jnp.float32)
    fc1_bias = noise(seeds[11], (FF,), 0.5, 3.0, ((0, 16),), jnp.float32)
    w_fc2 = noise(seeds[12], (FF, D), FF ** -0.5, 0.09375, ((0, 2), (1, 16)), jnp.float32)
    fc2_bias = noise(seeds[13], (D,), 0.3, 1.8, ((0, 16),), jnp.float32)
    out_grad = gaussian_with(seeds[14], (IMAGES, SEQ, D), 1.0, 6.0, ((0, 32),), (0, 2, 32, 2.75), jnp.float32)
    return {"inputs": inputs, "key_mask": key_mask, "ln1_gain": ln1_gain, "ln1_bias": ln1_bias, "w_qkv": w_qkv, "qv_bias": qv_bias, "w_proj": w_proj, "proj_bias": proj_bias, "ln2_gain": ln2_gain, "ln2_bias": ln2_bias, "w_fc1": w_fc1, "fc1_bias": fc1_bias, "w_fc2": w_fc2, "fc2_bias": fc2_bias, "out_grad": out_grad}


norm_eps = 1e-06
masked_score = -1e+30

@jax.custom_vjp
def low(v):
    return lax.optimization_barrier(v.astype(jnp.bfloat16)).astype(jnp.float32)

@jax.custom_vjp
def low_back(v):
    return v

def low_keep(v):
    return (low(v), None)

def low_pass(kept, grad):
    return (grad,)

def back_keep(v):
    return (v, None)

def back_low(kept, grad):
    return (low(grad),)
low.defvjp(low_keep, low_pass)
low_back.defvjp(back_keep, back_low)

def layer_norm(row_data, gain_vec, shift_vec):
    center = row_data - lax.optimization_barrier(jnp.mean(row_data, axis=-1, keepdims=True))
    spread = lax.optimization_barrier(jnp.mean(center * center, axis=-1, keepdims=True))
    return center * lax.rsqrt(spread + norm_eps) * gain_vec + shift_vec

def matmul_hi(left, right):
    return jnp.matmul(left, right, precision=lax.Precision.HIGHEST)

def forward(inputs, visible, parameters):
    gain_one, bias_one, qkv_w, qv_b, proj_w, proj_b, gain_two, bias_two, fc1_w, fc1_b, fc2_w, fc2_b = [low(parameter) for parameter in parameters]
    groups, seq_len = (inputs.shape[0], inputs.shape[1])
    normed_one = low(layer_norm(inputs, gain_one, bias_one))
    queries = low(low_back(matmul_hi(normed_one, qkv_w[0])) + qv_b[0])
    key_rows = low(low_back(matmul_hi(normed_one, qkv_w[1])))
    value_rows = low(low_back(matmul_hi(normed_one, qkv_w[2])) + qv_b[1])
    head_shape = (groups, seq_len, HEADS, HEAD_DIM)
    scores = low_back(HEAD_DIM ** (-0.5) * jnp.einsum('gqhd,gkhd->ghqk', queries.reshape(head_shape), key_rows.reshape(head_shape), precision=lax.Precision.HIGHEST))
    scores = jnp.where(visible[:, None, None, :], scores, masked_score)
    highest = lax.optimization_barrier(jnp.max(scores, axis=-1, keepdims=True))
    exp_scores = jnp.exp(scores - highest)
    probs_low = low(exp_scores / lax.optimization_barrier(jnp.sum(exp_scores, axis=-1, keepdims=True)))
    mixed_heads = jnp.einsum('ghqk,gkhd->gqhd', probs_low, value_rows.reshape(head_shape), precision=lax.Precision.HIGHEST)
    mixed_rows = low(low_back(mixed_heads)).reshape(groups, seq_len, HEADS * HEAD_DIM)
    middle = inputs + (low_back(matmul_hi(mixed_rows, proj_w)) + proj_b)
    normed_two = low(layer_norm(middle, gain_two, bias_two))
    hidden_pre = low_back(matmul_hi(normed_two, fc1_w)) + fc1_b
    hidden = low(jax.nn.gelu(hidden_pre, approximate=False))
    return middle + (low_back(matmul_hi(hidden, fc2_w)) + fc2_b)

def reference(inputs, key_mask, ln1_gain, ln1_bias, w_qkv, qv_bias, w_proj, proj_bias, ln2_gain, ln2_bias, w_fc1, fc1_bias, w_fc2, fc2_bias, out_grad):
    parameters = (ln1_gain, ln1_bias, w_qkv, qv_bias, w_proj, proj_bias, ln2_gain, ln2_bias, w_fc1, fc1_bias, w_fc2, fc2_bias)
    group_size = 8
    steps_count = IMAGES // group_size
    visible = jnp.concatenate([jnp.ones((IMAGES, BUF), jnp.int32), key_mask], axis=1) > 0
    input_blocks = inputs.reshape(steps_count, group_size, SEQ, D)
    seen_blocks = visible.reshape(steps_count, group_size, SEQ)
    grad_blocks = out_grad.reshape(steps_count, group_size, SEQ, D)

    def one_group(running, pieces):
        input_part, seen_part, grad_part = pieces

        def local_forward(row_data, params_in):
            return forward(row_data, seen_part, params_in)
        outputs, pullback = jax.vjp(local_forward, input_part, parameters)
        input_grad, param_grads = pullback(grad_part)
        running = tuple((old_grad + new_grad for old_grad, new_grad in zip(running, param_grads)))
        return (running, (outputs, input_grad))
    zero_grads = tuple((jnp.zeros_like(parameter) for parameter in parameters))
    running, (outputs, input_grads) = lax.scan(one_group, zero_grads, (input_blocks, seen_blocks, grad_blocks))
    return (outputs.reshape(IMAGES, SEQ, D), input_grads.reshape(IMAGES, SEQ, D), running[0], running[1], running[2], running[3], running[4], running[5], running[6], running[7], running[8], running[9], running[10], running[11])
```

```python
import jax
import jax.numpy as jnp
from jax import lax
from jax.experimental import pallas as pl
from jax.experimental.pallas import tpu as pltpu
from jax.sharding import PartitionSpec as P

HEAD_DIM = 64
norm_eps = 1e-06
masked_score = -1e30
AXES = ("dp", "tensor")
LOW = jnp.bfloat16
F32 = jnp.float32
TILE = 128
Y_BIT, CORE_BIT, X_BIT, Z_SHIFT = 1, 2, 4, 3
ANY = pl.BlockSpec(memory_space=pl.ANY)


def mm(left, right):
    return lax.dot_general(left, right, (((1,), (0,)), ((), ())), preferred_element_type=F32)


def mm_nt(left, right):
    return lax.dot_general(left, right, (((1,), (1,)), ((), ())), preferred_element_type=F32)


def mm_tn(left, right):
    return lax.dot_general(left, right, (((0,), (0,)), ((), ())), preferred_element_type=F32)


def whole(*shape):
    return pl.BlockSpec(shape, lambda t, me: (0,) * len(shape))


def call(body, grid, ins, outs, shapes, scratch, flops, moved, name):
    return pl.pallas_call(
        body,
        grid_spec=pltpu.PrefetchScalarGridSpec(
            num_scalar_prefetch=1,
            grid=grid,
            in_specs=ins,
            out_specs=outs,
            scratch_shapes=scratch,
        ),
        out_shape=shapes,
        compiler_params=pltpu.CompilerParams(
            dimension_semantics=("arbitrary",) * len(grid), vmem_limit_bytes=60 << 20
        ),
        cost_estimate=pl.CostEstimate(flops=flops, bytes_accessed=moved, transcendentals=0),
        name=name,
    )


def places(me, core_flip, first, second):
    owner = ((me >> 1) & 1) ^ core_flip
    off_y = jnp.where(owner == 0, first, second)
    off_x = jnp.where(owner == 0, second, first)
    return off_y, off_x


def dp_of(me, core_flip, off_x, off_z):
    core = ((me >> 1) & 1) ^ core_flip
    return (((me >> Z_SHIFT) ^ off_z) << 2) | ((((me >> 2) & 1) ^ off_x) << 1) | core


def fetch(me, pieces, store, sems, start, width):
    for index, piece in enumerate(pieces):
        core_flip, first, second = index >> 2, (index >> 1) & 1, index & 1
        off_y, off_x = places(me, core_flip, first, second)
        y_at = (me & 1) ^ off_y
        depth, rows, _ = piece.shape
        for off_z in range(depth):
            row = pl.multiple_of(dp_of(me, core_flip, off_x, off_z) * rows, rows)
            pltpu.make_async_copy(
                piece.at[off_z, :, pl.ds(start, width)],
                store.at[y_at, pl.ds(row, rows), :],
                sems.at[y_at],
            ).start()


def arrived(store, sems, y_at):
    pltpu.make_async_copy(store.at[y_at], store.at[y_at], sems.at[y_at]).wait()


def normed(rows, gain, shift):
    center = rows - jnp.mean(rows, axis=-1, keepdims=True)
    spread = jnp.mean(center * center, axis=-1, keepdims=True)
    return center * lax.rsqrt(spread + norm_eps) * gain + shift


def qkv_call(me, rows_in, table, bias, pieces):
    count, width = rows_in.shape
    half = width // 2
    span = 3 * half

    def body(me_ref, x_ref, table_ref, bias_ref, *refs):
        parts, (norm_ref, turn_ref, out_ref, store, sems) = refs[:8], refs[8:]
        step = pl.program_id(0)

        @pl.when(step == 0)
        def _():
            fetch(me_ref[0], parts, store, sems, 0, span)

            @pl.loop(0, count // TILE)
            def _(i):
                at = pl.ds(pl.multiple_of(i * TILE, TILE), TILE)
                value = normed(x_ref[at, :], table_ref[0:1, :], table_ref[1:2, :])
                norm_ref[at, :] = value.astype(LOW)
                turn_ref[:, at] = value.T.astype(LOW)

        for y_at in range(2):

            @pl.when(step == 3 * y_at)
            def _():
                arrived(store, sems, y_at)

        y_at, col = step // 3, pl.multiple_of(step % 3 * half, half)
        product = mm(norm_ref[...], store[y_at, :, pl.ds(col, half)])
        out_ref[...] = (product + bias_ref[...]).astype(LOW)

    return call(
        body,
        (6,),
        [whole(count, width), whole(*table.shape), pl.BlockSpec((1, half), lambda t, me: (0, t))]
        + [ANY] * 8,
        [
            whole(count, width),
            whole(width, count),
            pl.BlockSpec((count, half), lambda t, me: (0, t)),
        ],
        [
            jax.ShapeDtypeStruct((count, width), LOW),
            jax.ShapeDtypeStruct((width, count), LOW),
            jax.ShapeDtypeStruct((count, 2 * span), LOW),
        ],
        [pltpu.VMEM((2, width, span), LOW), pltpu.SemaphoreType.DMA((2,))],
        2 * count * width * 2 * span,
        count * width * 16 + width * span * 4,
        "qkv",
    )(me, rows_in, table, bias, *pieces)


def head_halves(shape):
    lane = lax.broadcasted_iota(jnp.int32, shape, 1)
    return lane < HEAD_DIM, lane >= HEAD_DIM


def soft(query, key, seen):
    scores = jnp.where(seen, mm_nt(query, key) * HEAD_DIM**-0.5, masked_score)
    exps = jnp.exp(scores - jnp.max(scores, axis=-1, keepdims=True))
    return exps / jnp.sum(exps, axis=-1, keepdims=True)


def attend_call(me, qkv, visible):
    images, _, seq = visible.shape
    count, full = qkv.shape
    half = full // 6

    def body(me_ref, qkv_ref, seen_ref, out_ref):
        seen = seen_ref[0] > 0

        @pl.loop(0, half // TILE)
        def _(pair):
            col = pl.multiple_of(pair * TILE, TILE)
            query = qkv_ref[:, pl.ds(col, TILE)]
            key = qkv_ref[:, pl.ds(half + col, TILE)]
            value = qkv_ref[:, pl.ds(2 * half + col, TILE)]
            lanes = head_halves(query.shape)
            mixed = []
            for keep in lanes:
                probs = soft(jnp.where(keep, query, 0), key, seen)
                mixed.append(mm(probs.astype(LOW), value))
            out_ref[:, pl.ds(col, TILE)] = jnp.where(lanes[0], mixed[0], mixed[1]).astype(LOW)

    return call(
        body,
        (images, 2),
        [
            pl.BlockSpec((seq, 3 * half), lambda i, y, me: (i, y)),
            pl.BlockSpec((1, 1, seq), lambda i, y, me: (i, 0, 0)),
        ],
        pl.BlockSpec((seq, half), lambda i, y, me: (i, y)),
        jax.ShapeDtypeStruct((count, 2 * half), LOW),
        [],
        4 * count * seq * 2 * half * 4,
        count * full * 3,
        "attend",
    )(me, qkv, visible)


def project_call(me, mixed, rows_in, table, pieces):
    count, width = rows_in.shape
    half = width // 2

    def body(me_ref, mixed_ref, x_ref, table_ref, *refs):
        parts, (mid_ref, norm_ref, turn_ref, store, sems) = refs[:8], refs[8:]
        fetch(me_ref[0], parts, store, sems, 3 * half, half)
        arrived(store, sems, 0)
        mid_ref[...] = mm_nt(mixed_ref[:, :half], store[0])
        arrived(store, sems, 1)
        mid_ref[...] += mm_nt(mixed_ref[:, half:], store[1])

        @pl.loop(0, count // TILE)
        def _(i):
            at = pl.ds(pl.multiple_of(i * TILE, TILE), TILE)
            middle = x_ref[at, :] + (mid_ref[at, :] + table_ref[4:5, :])
            mid_ref[at, :] = middle
            value = normed(middle, table_ref[5:6, :], table_ref[6:7, :])
            norm_ref[at, :] = value.astype(LOW)
            turn_ref[:, at] = value.T.astype(LOW)

    return call(
        body,
        (1,),
        [whole(count, width), whole(count, width), whole(*table.shape)] + [ANY] * 8,
        [whole(count, width), whole(count, width), whole(width, count)],
        [
            jax.ShapeDtypeStruct((count, width), F32),
            jax.ShapeDtypeStruct((count, width), LOW),
            jax.ShapeDtypeStruct((width, count), LOW),
        ],
        [pltpu.VMEM((2, width, half), LOW), pltpu.SemaphoreType.DMA((2,))],
        2 * count * width * width,
        count * width * 14 + width * width * 2,
        "project",
    )(me, mixed, rows_in, table, *pieces)


def expand_call(me, normed_two, bias, pieces):
    count, width = normed_two.shape
    span = bias.shape[1] // 2
    chunk = span // 4

    def body(me_ref, norm_ref, bias_ref, *refs):
        parts, (hid_ref, slope_ref, store, sems) = refs[:8], refs[8:]
        step = pl.program_id(0)

        @pl.when(step == 0)
        def _():
            fetch(me_ref[0], parts, store, sems, 0, span)

        for y_at in range(2):

            @pl.when(step == 4 * y_at)
            def _():
                arrived(store, sems, y_at)

        y_at, col = step // 4, pl.multiple_of(step % 4 * chunk, chunk)
        pre = mm(norm_ref[...], store[y_at, :, pl.ds(col, chunk)]) + bias_ref[...]
        below = 0.5 + 0.5 * lax.erf(pre * 0.5**0.5)
        hid_ref[...] = (pre * below).astype(LOW)
        slope_ref[...] = (below + pre * jnp.exp(pre * pre * -0.5) * 0.3989422804014327).astype(LOW)

    out = pl.BlockSpec((count, chunk), lambda t, me: (0, t))
    return call(
        body,
        (8,),
        [whole(count, width), pl.BlockSpec((1, chunk), lambda t, me: (0, t))] + [ANY] * 8,
        [out, out],
        [jax.ShapeDtypeStruct((count, 2 * span), LOW)] * 2,
        [pltpu.VMEM((2, width, span), LOW), pltpu.SemaphoreType.DMA((2,))],
        2 * count * width * 2 * span,
        count * span * 8 + width * span * 4,
        "expand",
    )(me, normed_two, bias, *pieces)


def contract_call(me, hidden, slope, out_low, middle, table, pieces):
    count, width = middle.shape
    span = hidden.shape[1] // 2
    chunk = span // 4

    def body(me_ref, hid_ref, slope_ref, low_ref, mid_ref, table_ref, *refs):
        parts, (act_ref, pre_ref, sum_ref, store, sems) = refs[:8], refs[8:]
        step = pl.program_id(0)

        @pl.when(step == 0)
        def _():
            fetch(me_ref[0], parts, store, sems, 0, span)
            act_ref[...] = mid_ref[...] + table_ref[7:8, :]

        for y_at in range(2):

            @pl.when(step == 4 * y_at)
            def _():
                arrived(store, sems, y_at)

        y_at, col = step // 4, pl.multiple_of(step % 4 * chunk, chunk)
        weight = store[y_at, :, pl.ds(col, chunk)]
        act_ref[...] += mm_nt(hid_ref[...], weight)
        pre = mm(low_ref[...], weight) * slope_ref[...].astype(F32)
        pre_ref[...] = pre.astype(LOW)
        sum_ref[...] = jnp.sum(pre, axis=0, keepdims=True)

    part = pl.BlockSpec((count, chunk), lambda t, me: (0, t))
    return call(
        body,
        (8,),
        [part, part, whole(count, width), whole(count, width), whole(*table.shape)] + [ANY] * 8,
        [whole(count, width), part, pl.BlockSpec((1, chunk), lambda t, me: (0, t))],
        [
            jax.ShapeDtypeStruct((count, width), F32),
            jax.ShapeDtypeStruct((count, 2 * span), LOW),
            jax.ShapeDtypeStruct((1, 2 * span), F32),
        ],
        [pltpu.VMEM((2, width, span), LOW), pltpu.SemaphoreType.DMA((2,))],
        4 * count * width * 2 * span,
        count * span * 12 + width * span * 4,
        "contract",
    )(me, hidden, slope, out_low, middle, table, *pieces)


def norm_back_call(me, low, start, gain_row, rows_in, base, table, pieces, keep_low, name):
    count, width = rows_in.shape
    span = low.shape[1] // 2
    chunk = span // 2

    def body(me_ref, low_ref, x_ref, base_ref, table_ref, *refs):
        parts, outs = refs[:8], refs[8:]
        if keep_low:
            grad_ref, vec_ref, out_low_ref, turn_ref, store, sems = outs
        else:
            grad_ref, vec_ref, store, sems = outs
        step = pl.program_id(0)

        @pl.when(step == 0)
        def _():
            fetch(me_ref[0], parts, store, sems, start, span)

        for y_at in range(2):

            @pl.when(step == 2 * y_at)
            def _():
                arrived(store, sems, y_at)

        y_at, col = step // 2, pl.multiple_of(step % 2 * chunk, chunk)
        product = mm_nt(low_ref[...], store[y_at, :, pl.ds(col, chunk)])

        @pl.when(step == 0)
        def _():
            grad_ref[...] = product

        @pl.when(step > 0)
        def _():
            grad_ref[...] += product

        @pl.when(step == 3)
        def _():
            vec_ref[...] = jnp.zeros_like(vec_ref)

            @pl.loop(0, count // TILE)
            def _(i):
                at = pl.ds(pl.multiple_of(i * TILE, TILE), TILE)
                back = grad_ref[at, :]
                rows = x_ref[at, :]
                center = rows - jnp.mean(rows, axis=-1, keepdims=True)
                spread = jnp.mean(center * center, axis=-1, keepdims=True)
                scale = lax.rsqrt(spread + norm_eps)
                unit = center * scale
                inner = back * table_ref[gain_row : gain_row + 1, :]
                along = jnp.mean(inner * unit, axis=-1, keepdims=True)
                level = jnp.mean(inner, axis=-1, keepdims=True)
                grad = base_ref[at, :] + scale * (inner - level - unit * along)
                grad_ref[at, :] = grad
                vec_ref[0:1, :] += jnp.sum(back * unit, axis=0, keepdims=True)
                vec_ref[1:2, :] += jnp.sum(back, axis=0, keepdims=True)
                vec_ref[2:3, :] += jnp.sum(grad, axis=0, keepdims=True)
                if keep_low:
                    out_low_ref[at, :] = grad.astype(LOW)
                    turn_ref[:, at] = grad.T.astype(LOW)

    outs = [whole(count, width), whole(8, width)]
    shapes = [jax.ShapeDtypeStruct((count, width), F32), jax.ShapeDtypeStruct((8, width), F32)]
    if keep_low:
        outs += [whole(count, width), whole(width, count)]
        shapes += [
            jax.ShapeDtypeStruct((count, width), LOW),
            jax.ShapeDtypeStruct((width, count), LOW),
        ]
    return call(
        body,
        (4,),
        [
            pl.BlockSpec((count, chunk), lambda t, me: (0, t)),
            whole(count, width),
            whole(count, width),
            whole(*table.shape),
        ]
        + [ANY] * 8,
        outs,
        shapes,
        [pltpu.VMEM((2, width, span), LOW), pltpu.SemaphoreType.DMA((2,))],
        2 * count * width * 2 * span,
        count * width * 16 + width * span * 4 + count * span * 4,
        name,
    )(me, low, rows_in, base, table, *pieces)


def mixed_back_call(me, middle_low, pieces):
    count, width = middle_low.shape
    half = width // 2

    def body(me_ref, low_ref, *refs):
        parts, (out_ref, store, sems) = refs[:8], refs[8:]
        step = pl.program_id(0)

        @pl.when(step == 0)
        def _():
            fetch(me_ref[0], parts, store, sems, 3 * half, half)

        for y_at in range(2):

            @pl.when(step == y_at)
            def _():
                arrived(store, sems, y_at)

        out_ref[...] = mm(low_ref[...], store[step]).astype(LOW)

    return call(
        body,
        (2,),
        [whole(count, width)] + [ANY] * 8,
        pl.BlockSpec((count, half), lambda t, me: (0, t)),
        jax.ShapeDtypeStruct((count, width), LOW),
        [pltpu.VMEM((2, width, half), LOW), pltpu.SemaphoreType.DMA((2,))],
        2 * count * width * width,
        count * width * 4 + width * width * 2,
        "mixed_back",
    )(me, middle_low, *pieces)


def attend_back_call(me, qkv, grads, visible):
    images, _, seq = visible.shape
    count, full = qkv.shape
    half = full // 6
    scale = HEAD_DIM**-0.5

    def body(me_ref, qkv_ref, grad_ref, seen_ref, out_ref, sum_ref):
        seen = seen_ref[0] > 0

        @pl.loop(0, half // TILE)
        def _(pair):
            col = pl.multiple_of(pair * TILE, TILE)
            query = qkv_ref[:, pl.ds(col, TILE)]
            key = qkv_ref[:, pl.ds(half + col, TILE)]
            value = qkv_ref[:, pl.ds(2 * half + col, TILE)]
            grad = grad_ref[:, pl.ds(col, TILE)]
            lanes = head_halves(query.shape)
            parts = []
            for keep in lanes:
                probs = soft(jnp.where(keep, query, 0), key, seen)
                prob_grad = mm_nt(jnp.where(keep, grad, 0), value)
                row_dot = jnp.sum(probs * prob_grad, axis=-1, keepdims=True)
                score_grad = (probs * (prob_grad - row_dot)).astype(LOW)
                parts.append(
                    (
                        mm(score_grad, key) * scale,
                        mm_tn(score_grad, query) * scale,
                        mm_tn(probs.astype(LOW), grad),
                    )
                )
            for at in range(3):
                merged = jnp.where(lanes[0], parts[0][at], parts[1][at])
                out_ref[:, pl.ds(at * half + col, TILE)] = merged.astype(LOW)
                sum_ref[0, 0, :, pl.ds(at * half + col, TILE)] = jnp.sum(
                    merged, axis=0, keepdims=True
                )

    return call(
        body,
        (images, 2),
        [
            pl.BlockSpec((seq, 3 * half), lambda i, y, me: (i, y)),
            pl.BlockSpec((seq, half), lambda i, y, me: (i, y)),
            pl.BlockSpec((1, 1, seq), lambda i, y, me: (i, 0, 0)),
        ],
        [
            pl.BlockSpec((seq, 3 * half), lambda i, y, me: (i, y)),
            pl.BlockSpec((1, 1, 1, 3 * half), lambda i, y, me: (i, y, 0, 0)),
        ],
        [
            jax.ShapeDtypeStruct((count, full), LOW),
            jax.ShapeDtypeStruct((images, 2, 1, 3 * half), F32),
        ],
        [],
        10 * count * seq * 2 * half * 4,
        count * full * 5,
        "attend_back",
    )(me, qkv, grads, visible)


def weight_grad_call(me, turned, right, depth, core_flip, received, name):
    width, count = turned.shape
    span = right.shape[1] // 2
    chunk = next(c for c in (1024, 768, 512, 384, 256, 128) if span % c == 0)
    parts = span // chunk
    rows = width // (4 * depth)

    def spot(t):
        first = 1 - t // (2 * parts)
        return first, t // parts % 2, t % parts

    def right_at(t, me):
        first, second, part = spot(t)
        off_y, _ = places(me[0], core_flip, first, second)
        return 0, ((me[0] & 1) ^ off_y) * parts + part

    def body(me_ref, turn_ref, right_ref, *refs):
        step = pl.program_id(0)
        first, second, _ = spot(step)
        _, off_x = places(me_ref[0], core_flip, first, second)
        lefts = refs[-1]
        for off_z in range(depth):
            row = pl.multiple_of(dp_of(me_ref[0], core_flip, off_x, off_z) * rows, rows)
            lefts[off_z * rows : (off_z + 1) * rows, :] = turn_ref[pl.ds(row, rows), :]
        product = mm(lefts[...], right_ref[...])
        if core_flip:
            refs[0][0, 0] = product.astype(LOW).reshape(depth, rows, chunk)
            return
        total = product.reshape(depth, rows, chunk) + refs[0][0, 0].astype(F32)
        for at in range(2):

            @pl.when(first == at)
            def _():
                refs[1 + at][0] = total.astype(LOW)

    def both(t, me):
        first, second, part = spot(t)
        return first, second, 0, 0, part

    def only(at):
        def index(t, me):
            first, second, part = spot(t)
            idle_second, idle_part = (0, 0) if at == 0 else (1, parts - 1)
            return (
                jnp.where(first == at, second, idle_second),
                0,
                0,
                jnp.where(first == at, part, idle_part),
            )

        return index

    block5 = pl.BlockSpec((1, 1, depth, rows, chunk), both)
    ins = [whole(width, count), pl.BlockSpec((count, chunk), right_at)]
    if core_flip:
        outs = block5
        shapes = jax.ShapeDtypeStruct((2, 2, depth, rows, span), LOW)
        extra = ()
    else:
        ins = ins + [block5]
        outs = [pl.BlockSpec((1, depth, rows, chunk), only(at)) for at in range(2)]
        shapes = [jax.ShapeDtypeStruct((2, depth, rows, span), LOW)] * 2
        extra = (received,)
    return call(
        body,
        (4 * parts,),
        ins,
        outs,
        shapes,
        [pltpu.VMEM((width // 4, count), LOW)],
        2 * count * width * span,
        count * (width + span * 2) * 2 + width * span * 4,
        name,
    )(me, turned, right, *extra)


def swap(value, size, bits, other=None):
    other = bits if other is None else other
    return lax.ppermute(
        value, AXES, [(i, i ^ (other if i & CORE_BIT else bits)) for i in range(size)]
    )


def gather_pieces(piece, size, depth):
    own = jnp.stack([piece] + [swap(piece, size, k << Z_SHIFT) for k in range(1, depth)])
    first = swap(own, size, Y_BIT, X_BIT)
    second = swap(own, size, X_BIT, Y_BIT)
    both = swap(first, size, X_BIT, Y_BIT)
    held = [own, second, first, both]
    return held + [swap(value, size, CORE_BIT) for value in held]


def gather_vectors(vector, size, depth, dp_rank):
    dp_size = 4 * depth
    held = jnp.stack([vector] + [swap(vector, size, k << Z_SHIFT) for k in range(1, depth)])
    held = jnp.stack([held, swap(held, size, X_BIT)], axis=1)
    held = jnp.stack([held, swap(held, size, CORE_BIT)], axis=2)
    held = held.reshape(dp_size, -1)
    spot = jnp.arange(dp_size)
    pick = (spot[None, :] == (spot ^ dp_rank)[:, None]).astype(F32)
    return jnp.matmul(pick, held, precision=lax.Precision.HIGHEST)


def finish_scatter(kept, sent, size, depth):
    received = swap(sent, size, Y_BIT, X_BIT)
    total = (kept.astype(F32) + received.astype(F32)).astype(LOW)
    received = swap(total[1], size, X_BIT, Y_BIT)
    total = (total[0].astype(F32) + received.astype(F32)).astype(LOW)
    result = total[0].astype(F32)
    for k in range(1, depth):
        result = result + swap(total[k], size, k << Z_SHIFT).astype(F32)
    return result


def sum_all(value, size, depth):
    for bits in (CORE_BIT, X_BIT, Y_BIT):
        value = value + swap(value, size, bits)
    return sum((swap(value, size, k << Z_SHIFT) for k in range(1, depth)), value)


def shards(
    inputs,
    key_mask,
    ln1_gain,
    ln1_bias,
    w_qkv,
    qv_bias,
    w_proj,
    proj_bias,
    ln2_gain,
    ln2_bias,
    w_fc1,
    fc1_bias,
    w_fc2,
    fc2_bias,
    out_grad,
):
    tensor_rank = lax.axis_index("tensor")
    dp_rank = lax.axis_index("dp")
    dp_size = lax.axis_size("dp")
    size = 2 * dp_size
    depth = dp_size // 4
    own_images, seq, width = inputs.shape
    count = own_images * seq
    half = w_qkv.shape[2]
    rows = ln1_gain.shape[0]
    me = jnp.reshape(dp_rank * 2 + tensor_rank, (1,)).astype(jnp.int32)

    piece_one = jnp.concatenate([w_qkv[0], w_qkv[1], w_qkv[2], w_proj.T], axis=1).astype(LOW)
    piece_two = w_fc1.astype(LOW)
    piece_three = w_fc2.T.astype(LOW)
    vector = jnp.concatenate(
        [
            ln1_gain,
            ln1_bias,
            qv_bias[0],
            qv_bias[1],
            proj_bias,
            ln2_gain,
            ln2_bias,
            fc2_bias,
            fc1_bias,
        ]
    )
    vector = jnp.pad(vector.astype(LOW).astype(F32), (0, -vector.shape[0] % 1024))
    pieces_one = gather_pieces(piece_one, size, depth)
    gathered = gather_vectors(vector.reshape(-1, TILE), size, depth, dp_rank)
    pieces_two = gather_pieces(piece_two, size, depth)
    pieces_three = gather_pieces(piece_three, size, depth)
    table = gathered[:, : 8 * rows].reshape(dp_size, 8, rows).transpose(1, 0, 2).reshape(8, width)
    fc1_full = gathered[:, 8 * rows : 12 * rows].reshape(1, 4 * width)
    qkv_bias = jnp.stack(
        [table[2].reshape(2, half), jnp.zeros((2, half), F32), table[3].reshape(2, half)], axis=1
    ).reshape(1, 6 * half)

    rows_in = inputs.reshape(count, width)
    grad_in = out_grad.reshape(count, width)
    out_low = grad_in.astype(LOW)
    out_turned = out_low.T
    own_mask = lax.dynamic_slice_in_dim(key_mask, tensor_rank * own_images, own_images, 0)
    visible = jnp.concatenate(
        [jnp.ones((own_images, seq - key_mask.shape[1]), jnp.int32), own_mask], axis=1
    )[:, None, :]

    normed_one, turned_one, qkv = qkv_call(me, rows_in, table, qkv_bias, pieces_one)
    mixed = attend_call(me, qkv, visible)
    middle, normed_two, turned_two = project_call(me, mixed, rows_in, table, pieces_one)
    hidden, slope = expand_call(me, normed_two, fc1_full, pieces_two)

    def weight_grad(turned, right, name):
        sent = weight_grad_call(me, turned, right, depth, 1, None, name + "_far")
        received = swap(sent, size, CORE_BIT)
        kept, sent = weight_grad_call(me, turned, right, depth, 0, received, name + "_near")
        return finish_scatter(kept, sent, size, depth)

    fc2_grad = weight_grad(out_turned, hidden, "fc2_grad")
    outputs, pre_low, fc1_sum = contract_call(
        me, hidden, slope, out_low, middle, table, pieces_three
    )
    fc1_grad = weight_grad(turned_two, pre_low, "fc1_grad")
    middle_grad, vec_two, middle_low, turned_mid = norm_back_call(
        me, pre_low, 0, 5, middle, grad_in, table, pieces_two, True, "norm_two_back"
    )
    proj_grad = weight_grad(turned_mid, mixed, "proj_grad")
    mixed_grad = mixed_back_call(me, middle_low, pieces_one)
    qkv_low, qkv_sum = attend_back_call(me, qkv, mixed_grad, visible)
    qkv_grad = weight_grad(turned_one, qkv_low, "qkv_grad")
    input_grad, vec_one = norm_back_call(
        me, qkv_low, 0, 0, rows_in, middle_grad, table, pieces_one, False, "norm_one_back"
    )

    qkv_sum = jnp.sum(qkv_sum, axis=(0, 2)).reshape(2, 3, half)
    sums = jnp.concatenate(
        [
            vec_one[:2],
            qkv_sum[:, 0].reshape(1, width),
            qkv_sum[:, 2].reshape(1, width),
            vec_two[2:3],
            vec_two[:2],
            jnp.sum(grad_in, axis=0, keepdims=True),
            fc1_sum.reshape(4, width),
        ]
    )
    sums = sum_all(sums, size, depth)
    mine = lax.dynamic_slice_in_dim(sums[:8], dp_rank * rows, rows, 1)
    fc1_mine = lax.dynamic_slice_in_dim(sums[8:].reshape(-1), dp_rank * 4 * rows, 4 * rows, 0)
    return (
        outputs.reshape(inputs.shape),
        input_grad.reshape(inputs.shape),
        mine[0],
        mine[1],
        qkv_grad.reshape(rows, 3, half).transpose(1, 0, 2),
        mine[2:4],
        proj_grad.T,
        mine[4],
        mine[5],
        mine[6],
        fc1_grad,
        fc1_mine,
        fc2_grad.T,
        mine[7],
    )


def solution(mesh):
    placed = (
        P(("dp", "tensor"), None, None),
        P("dp", None),
        P("dp"),
        P("dp"),
        P(None, "dp", "tensor"),
        P(None, "dp"),
        P("tensor", "dp"),
        P("dp"),
        P("dp"),
        P("dp"),
        P("dp", "tensor"),
        P("dp"),
        P("tensor", "dp"),
        P("dp"),
        P(("dp", "tensor"), None, None),
    )
    return jax.shard_map(
        shards,
        mesh=mesh,
        in_specs=placed,
        out_specs=(
            P(("dp", "tensor"), None, None),
            P(("dp", "tensor"), None, None),
            P("dp"),
            P("dp"),
            P(None, "dp", "tensor"),
            P(None, "dp"),
            P("tensor", "dp"),
            P("dp"),
            P("dp"),
            P("dp"),
            P("dp", "tensor"),
            P("dp"),
            P("tensor", "dp"),
            P("dp"),
        ),
        check_vma=False,
    )
```

```python
import jax
import jax.numpy as jnp
from jax import lax
from jax.experimental import pallas as pl
from jax.experimental.pallas import tpu as pltpu
from jax.sharding import PartitionSpec as P

HEAD_DIM = 64
norm_eps = 1e-06
masked_score = -1e30
AXES = ("dp", "tensor")
LOW = jnp.bfloat16
F32 = jnp.float32
TILE = 128
Y_BIT, CORE_BIT, X_BIT, Z_SHIFT = 1, 2, 4, 3
ANY = pl.BlockSpec(memory_space=pl.ANY)


def mm(left, right):
    return lax.dot_general(left, right, (((1,), (0,)), ((), ())), preferred_element_type=F32)


def mm_nt(left, right):
    return lax.dot_general(left, right, (((1,), (1,)), ((), ())), preferred_element_type=F32)


def mm_tn(left, right):
    return lax.dot_general(left, right, (((0,), (0,)), ((), ())), preferred_element_type=F32)


def whole(*shape):
    return pl.BlockSpec(shape, lambda t, me: (0,) * len(shape))


def call(body, grid, ins, outs, shapes, scratch, flops, moved, name):
    return pl.pallas_call(
        body,
        grid_spec=pltpu.PrefetchScalarGridSpec(
            num_scalar_prefetch=1,
            grid=grid,
            in_specs=ins,
            out_specs=outs,
            scratch_shapes=scratch,
        ),
        out_shape=shapes,
        compiler_params=pltpu.CompilerParams(
            dimension_semantics=("arbitrary",) * len(grid), vmem_limit_bytes=32 << 20
        ),
        cost_estimate=pl.CostEstimate(flops=flops, bytes_accessed=moved, transcendentals=0),
        name=name,
    )


def places(me, core_flip, first, second):
    owner = ((me >> 1) & 1) ^ core_flip
    off_y = jnp.where(owner == 0, first, second)
    off_x = jnp.where(owner == 0, second, first)
    return off_y, off_x


def dp_of(me, core_flip, off_x, off_z):
    core = ((me >> 1) & 1) ^ core_flip
    return (((me >> Z_SHIFT) ^ off_z) << 2) | ((((me >> 2) & 1) ^ off_x) << 1) | core


def fetch(me, pieces, store, sems, start, width):
    for index, piece in enumerate(pieces):
        core_flip, first, second = index >> 2, (index >> 1) & 1, index & 1
        off_y, off_x = places(me, core_flip, first, second)
        y_at = (me & 1) ^ off_y
        depth, rows, _ = piece.shape
        for off_z in range(depth):
            row = pl.multiple_of(dp_of(me, core_flip, off_x, off_z) * rows, rows)
            pltpu.make_async_copy(
                piece.at[off_z, :, pl.ds(start, width)],
                store.at[y_at, pl.ds(row, rows), :],
                sems.at[y_at],
            ).start()


def arrived(store, sems, y_at):
    pltpu.make_async_copy(store.at[y_at], store.at[y_at], sems.at[y_at]).wait()


def normed(rows, gain, shift):
    center = rows - jnp.mean(rows, axis=-1, keepdims=True)
    spread = jnp.mean(center * center, axis=-1, keepdims=True)
    return center * lax.rsqrt(spread + norm_eps) * gain + shift


def qkv_call(me, rows_in, table, bias, pieces):
    count, width = rows_in.shape
    half = width // 2
    span = 3 * half

    def body(me_ref, x_ref, table_ref, bias_ref, *refs):
        parts, (norm_ref, turn_ref, out_ref, store, sems) = refs[:8], refs[8:]
        step = pl.program_id(0)

        @pl.when(step == 0)
        def _():
            fetch(me_ref[0], parts, store, sems, 0, span)

            @pl.loop(0, count // TILE)
            def _(i):
                at = pl.ds(pl.multiple_of(i * TILE, TILE), TILE)
                value = normed(x_ref[at, :], table_ref[0:1, :], table_ref[1:2, :])
                norm_ref[at, :] = value.astype(LOW)
                turn_ref[:, at] = value.T.astype(LOW)

        for y_at in range(2):

            @pl.when(step == 3 * y_at)
            def _():
                arrived(store, sems, y_at)

        y_at, col = step // 3, pl.multiple_of(step % 3 * half, half)
        product = mm(norm_ref[...], store[y_at, :, pl.ds(col, half)])
        out_ref[...] = (product + bias_ref[...]).astype(LOW)

    return call(
        body,
        (6,),
        [whole(count, width), whole(*table.shape), pl.BlockSpec((1, half), lambda t, me: (0, t))]
        + [ANY] * 8,
        [
            whole(count, width),
            whole(width, count),
            pl.BlockSpec((count, half), lambda t, me: (0, t)),
        ],
        [
            jax.ShapeDtypeStruct((count, width), LOW),
            jax.ShapeDtypeStruct((width, count), LOW),
            jax.ShapeDtypeStruct((count, 2 * span), LOW),
        ],
        [pltpu.VMEM((2, width, span), LOW), pltpu.SemaphoreType.DMA((2,))],
        2 * count * width * 2 * span,
        count * width * 16 + width * span * 4,
        "qkv",
    )(me, rows_in, table, bias, *pieces)


def head_halves(shape):
    lane = lax.broadcasted_iota(jnp.int32, shape, 1)
    return lane < HEAD_DIM, lane >= HEAD_DIM


def attend_call(me, qkv, visible):
    images, _, seq = visible.shape
    count, full = qkv.shape
    half = full // 6

    def body(me_ref, qkv_ref, seen_ref, out_ref):
        seen = seen_ref[0] > 0

        for col in range(0, half, TILE):
            query = qkv_ref[:, col : col + TILE] * jnp.asarray(HEAD_DIM**-0.5, LOW)
            key = qkv_ref[:, half + col : half + col + TILE]
            value = qkv_ref[:, 2 * half + col : 2 * half + col + TILE]
            lanes = head_halves(query.shape)
            mixed = []
            for keep in lanes:
                scores = jnp.where(seen, mm_nt(jnp.where(keep, query, 0), key), masked_score)
                exps = jnp.exp(scores - jnp.max(scores, axis=-1, keepdims=True))
                total = jnp.sum(exps, axis=-1, keepdims=True)
                mixed.append(mm(exps.astype(LOW), value) * (1.0 / total))
            out_ref[:, col : col + TILE] = jnp.where(lanes[0], mixed[0], mixed[1]).astype(LOW)

    return call(
        body,
        (images, 2),
        [
            pl.BlockSpec((seq, 3 * half), lambda i, y, me: (i, y)),
            pl.BlockSpec((1, 1, seq), lambda i, y, me: (i, 0, 0)),
        ],
        pl.BlockSpec((seq, half), lambda i, y, me: (i, y)),
        jax.ShapeDtypeStruct((count, 2 * half), LOW),
        [],
        4 * count * seq * 2 * half * 4,
        count * full * 3,
        "attend",
    )(me, qkv, visible)


def project_call(me, mixed, rows_in, table, pieces):
    count, width = rows_in.shape
    half = width // 2

    def body(me_ref, mixed_ref, x_ref, table_ref, *refs):
        parts, (mid_ref, norm_ref, turn_ref, store, sems) = refs[:8], refs[8:]
        fetch(me_ref[0], parts, store, sems, 3 * half, half)
        arrived(store, sems, 0)
        mid_ref[...] = mm_nt(mixed_ref[:, :half], store[0])
        arrived(store, sems, 1)
        mid_ref[...] += mm_nt(mixed_ref[:, half:], store[1])

        @pl.loop(0, count // TILE)
        def _(i):
            at = pl.ds(pl.multiple_of(i * TILE, TILE), TILE)
            middle = x_ref[at, :] + (mid_ref[at, :] + table_ref[4:5, :])
            mid_ref[at, :] = middle
            value = normed(middle, table_ref[5:6, :], table_ref[6:7, :])
            norm_ref[at, :] = value.astype(LOW)
            turn_ref[:, at] = value.T.astype(LOW)

    return call(
        body,
        (1,),
        [whole(count, width), whole(count, width), whole(*table.shape)] + [ANY] * 8,
        [whole(count, width), whole(count, width), whole(width, count)],
        [
            jax.ShapeDtypeStruct((count, width), F32),
            jax.ShapeDtypeStruct((count, width), LOW),
            jax.ShapeDtypeStruct((width, count), LOW),
        ],
        [pltpu.VMEM((2, width, half), LOW), pltpu.SemaphoreType.DMA((2,))],
        2 * count * width * width,
        count * width * 14 + width * width * 2,
        "project",
    )(me, mixed, rows_in, table, *pieces)


def expand_call(me, normed_two, bias, pieces):
    count, width = normed_two.shape
    span = bias.shape[1] // 2
    chunk = span // 4

    def body(me_ref, norm_ref, bias_ref, *refs):
        parts, (hid_ref, slope_ref, store, sems) = refs[:8], refs[8:]
        step = pl.program_id(0)

        @pl.when(step == 0)
        def _():
            fetch(me_ref[0], parts, store, sems, 0, span)

        for y_at in range(2):

            @pl.when(step == 4 * y_at)
            def _():
                arrived(store, sems, y_at)

        y_at, col = step // 4, pl.multiple_of(step % 4 * chunk, chunk)
        pre = mm(norm_ref[...], store[y_at, :, pl.ds(col, chunk)]) + bias_ref[...]
        below = 0.5 + 0.5 * lax.erf(pre * 0.5**0.5)
        hid_ref[...] = (pre * below).astype(LOW)
        slope_ref[...] = (below + pre * jnp.exp(pre * pre * -0.5) * 0.3989422804014327).astype(LOW)

    out = pl.BlockSpec((count, chunk), lambda t, me: (0, t))
    return call(
        body,
        (8,),
        [whole(count, width), pl.BlockSpec((1, chunk), lambda t, me: (0, t))] + [ANY] * 8,
        [out, out],
        [jax.ShapeDtypeStruct((count, 2 * span), LOW)] * 2,
        [pltpu.VMEM((2, width, span), LOW), pltpu.SemaphoreType.DMA((2,))],
        2 * count * width * 2 * span,
        count * span * 8 + width * span * 4,
        "expand",
    )(me, normed_two, bias, *pieces)


def contract_call(me, hidden, slope, out_low, middle, table, pieces):
    count, width = middle.shape
    span = hidden.shape[1] // 2
    chunk = span // 4

    def body(me_ref, hid_ref, slope_ref, low_ref, mid_ref, table_ref, *refs):
        parts, (act_ref, pre_ref, sum_ref, store, sems) = refs[:8], refs[8:]
        step = pl.program_id(0)

        @pl.when(step == 0)
        def _():
            fetch(me_ref[0], parts, store, sems, 0, span)
            act_ref[...] = mid_ref[...] + table_ref[7:8, :]

        for y_at in range(2):

            @pl.when(step == 4 * y_at)
            def _():
                arrived(store, sems, y_at)

        y_at, col = step // 4, pl.multiple_of(step % 4 * chunk, chunk)
        weight = store[y_at, :, pl.ds(col, chunk)]
        act_ref[...] += mm_nt(hid_ref[...], weight)
        pre = mm(low_ref[...], weight) * slope_ref[...].astype(F32)
        pre_ref[...] = pre.astype(LOW)
        sum_ref[...] = jnp.sum(pre, axis=0, keepdims=True)

    part = pl.BlockSpec((count, chunk), lambda t, me: (0, t))
    return call(
        body,
        (8,),
        [part, part, whole(count, width), whole(count, width), whole(*table.shape)] + [ANY] * 8,
        [whole(count, width), part, pl.BlockSpec((1, chunk), lambda t, me: (0, t))],
        [
            jax.ShapeDtypeStruct((count, width), F32),
            jax.ShapeDtypeStruct((count, 2 * span), LOW),
            jax.ShapeDtypeStruct((1, 2 * span), F32),
        ],
        [pltpu.VMEM((2, width, span), LOW), pltpu.SemaphoreType.DMA((2,))],
        4 * count * width * 2 * span,
        count * span * 12 + width * span * 4,
        "contract",
    )(me, hidden, slope, out_low, middle, table, *pieces)


def norm_back_call(me, low, start, gain_row, rows_in, base, table, pieces, keep_low, name):
    count, width = rows_in.shape
    span = low.shape[1] // 2
    chunk = span // 2

    def body(me_ref, low_ref, x_ref, base_ref, table_ref, *refs):
        parts, outs = refs[:8], refs[8:]
        if keep_low:
            grad_ref, vec_ref, out_low_ref, turn_ref, store, sems = outs
        else:
            grad_ref, vec_ref, store, sems = outs
        step = pl.program_id(0)

        @pl.when(step == 0)
        def _():
            fetch(me_ref[0], parts, store, sems, start, span)

        for y_at in range(2):

            @pl.when(step == 2 * y_at)
            def _():
                arrived(store, sems, y_at)

        y_at, col = step // 2, pl.multiple_of(step % 2 * chunk, chunk)
        product = mm_nt(low_ref[...], store[y_at, :, pl.ds(col, chunk)])

        @pl.when(step == 0)
        def _():
            grad_ref[...] = product

        @pl.when(step > 0)
        def _():
            grad_ref[...] += product

        @pl.when(step == 3)
        def _():
            vec_ref[...] = jnp.zeros_like(vec_ref)

            @pl.loop(0, count // TILE)
            def _(i):
                at = pl.ds(pl.multiple_of(i * TILE, TILE), TILE)
                back = grad_ref[at, :]
                rows = x_ref[at, :]
                center = rows - jnp.mean(rows, axis=-1, keepdims=True)
                spread = jnp.mean(center * center, axis=-1, keepdims=True)
                scale = lax.rsqrt(spread + norm_eps)
                unit = center * scale
                inner = back * table_ref[gain_row : gain_row + 1, :]
                along = jnp.mean(inner * unit, axis=-1, keepdims=True)
                level = jnp.mean(inner, axis=-1, keepdims=True)
                grad = base_ref[at, :] + scale * (inner - level - unit * along)
                grad_ref[at, :] = grad
                vec_ref[0:1, :] += jnp.sum(back * unit, axis=0, keepdims=True)
                vec_ref[1:2, :] += jnp.sum(back, axis=0, keepdims=True)
                vec_ref[2:3, :] += jnp.sum(grad, axis=0, keepdims=True)
                if keep_low:
                    out_low_ref[at, :] = grad.astype(LOW)
                    turn_ref[:, at] = grad.T.astype(LOW)

    outs = [whole(count, width), whole(8, width)]
    shapes = [jax.ShapeDtypeStruct((count, width), F32), jax.ShapeDtypeStruct((8, width), F32)]
    if keep_low:
        outs += [whole(count, width), whole(width, count)]
        shapes += [
            jax.ShapeDtypeStruct((count, width), LOW),
            jax.ShapeDtypeStruct((width, count), LOW),
        ]
    return call(
        body,
        (4,),
        [
            pl.BlockSpec((count, chunk), lambda t, me: (0, t)),
            whole(count, width),
            whole(count, width),
            whole(*table.shape),
        ]
        + [ANY] * 8,
        outs,
        shapes,
        [pltpu.VMEM((2, width, span), LOW), pltpu.SemaphoreType.DMA((2,))],
        2 * count * width * 2 * span,
        count * width * 16 + width * span * 4 + count * span * 4,
        name,
    )(me, low, rows_in, base, table, *pieces)


def mixed_back_call(me, middle_low, pieces):
    count, width = middle_low.shape
    half = width // 2

    def body(me_ref, low_ref, *refs):
        parts, (out_ref, store, sems) = refs[:8], refs[8:]
        step = pl.program_id(0)

        @pl.when(step == 0)
        def _():
            fetch(me_ref[0], parts, store, sems, 3 * half, half)

        for y_at in range(2):

            @pl.when(step == y_at)
            def _():
                arrived(store, sems, y_at)

        out_ref[...] = mm(low_ref[...], store[step]).astype(LOW)

    return call(
        body,
        (2,),
        [whole(count, width)] + [ANY] * 8,
        pl.BlockSpec((count, half), lambda t, me: (0, t)),
        jax.ShapeDtypeStruct((count, width), LOW),
        [pltpu.VMEM((2, width, half), LOW), pltpu.SemaphoreType.DMA((2,))],
        2 * count * width * width,
        count * width * 4 + width * width * 2,
        "mixed_back",
    )(me, middle_low, *pieces)


def attend_back_call(me, qkv, grads, visible):
    images, seq, _ = visible.shape
    count, full = qkv.shape
    half = full // 6
    scale = HEAD_DIM**-0.5

    def body(me_ref, qkv_ref, grad_ref, seen_ref, out_ref, sum_ref):
        seen = seen_ref[0] > 0
        for col in range(0, half, TILE):
            query = qkv_ref[:, col : col + TILE] * jnp.asarray(scale, LOW)
            key = qkv_ref[:, half + col : half + col + TILE]
            value = qkv_ref[:, 2 * half + col : 2 * half + col + TILE]
            grad = grad_ref[:, col : col + TILE]
            lanes = head_halves(query.shape)
            parts = []
            for keep in lanes:
                scores = jnp.where(seen, mm_nt(jnp.where(keep, key, 0), query), masked_score)
                exps = jnp.exp(scores - jnp.max(scores, axis=0, keepdims=True))
                probs = exps * (1.0 / jnp.sum(exps, axis=0, keepdims=True))
                prob_grad = mm_nt(jnp.where(keep, value, 0), grad)
                row_dot = jnp.sum(probs * prob_grad, axis=0, keepdims=True)
                score_grad = (probs * (prob_grad - row_dot)).astype(LOW)
                parts.append(
                    (
                        mm_tn(key, score_grad).T * scale,
                        mm(score_grad, query),
                        mm(probs.astype(LOW), grad),
                    )
                )
            for at in range(3):
                merged = jnp.where(lanes[0], parts[0][at], parts[1][at])
                put = at * half + col
                out_ref[:, put : put + TILE] = merged.astype(LOW)
                sum_ref[0, 0, :, put : put + TILE] = jnp.sum(merged, axis=0, keepdims=True)

    return call(
        body,
        (images, 2),
        [
            pl.BlockSpec((seq, 3 * half), lambda i, y, me: (i, y)),
            pl.BlockSpec((seq, half), lambda i, y, me: (i, y)),
            pl.BlockSpec((1, seq, 1), lambda i, y, me: (i, 0, 0)),
        ],
        [
            pl.BlockSpec((seq, 3 * half), lambda i, y, me: (i, y)),
            pl.BlockSpec((1, 1, 1, 3 * half), lambda i, y, me: (i, y, 0, 0)),
        ],
        [
            jax.ShapeDtypeStruct((count, full), LOW),
            jax.ShapeDtypeStruct((images, 2, 1, 3 * half), F32),
        ],
        [],
        10 * count * seq * 2 * half * 4,
        count * full * 5,
        "attend_back",
    )(me, qkv, grads, visible)


def weight_grad_call(me, turned, right, depth, core_flip, received, name):
    width, count = turned.shape
    span = right.shape[1] // 2
    chunk = next(c for c in (1024, 768, 512, 384, 256, 128) if span % c == 0)
    parts = span // chunk
    steps = 2 * parts
    rows = width // (4 * depth)
    quarter = width // 4

    def body(me_ref, turn_ref, right_ref, *refs):
        if core_flip:
            (far_ref, lefts, ready, sems) = refs
        else:
            (got_ref, kept_ref, sent_ref, lefts, ready, sems, got, got_sems) = refs
        step = pl.program_id(0)
        slot = step % 2
        owner = ((me_ref[0] >> 1) & 1) ^ core_flip

        def spot(off_y, off_x):
            return jnp.where(owner == 0, off_y, off_x), jnp.where(owner == 0, off_x, off_y)

        def fetched(at, off_x):
            first, second = spot(1 - at // parts, off_x)
            col = pl.multiple_of(at % parts * chunk, chunk)
            return pltpu.make_async_copy(
                got_ref.at[first, second, :, :, pl.ds(col, chunk)],
                got.at[at, off_x],
                got_sems.at[at, off_x],
            )

        def leaving(target, at, off_x):
            col = pl.multiple_of(at % parts * chunk, chunk)
            return pltpu.make_async_copy(
                ready.at[at % 2, off_x],
                target.at[:, :, pl.ds(col, chunk)],
                sems.at[at % 2, off_x],
            )

        @pl.when(step == 0)
        def _():
            if not core_flip:
                for at in range(steps):
                    for off_x in range(2):
                        fetched(at, off_x).start()
            for off_x in range(2):
                for off_z in range(depth):
                    row = pl.multiple_of(dp_of(me_ref[0], core_flip, off_x, off_z) * rows, rows)
                    put = off_x * quarter + off_z * rows
                    lefts[put : put + rows, :] = turn_ref[pl.ds(row, rows), :]

        product = mm(lefts[...], right_ref[...]).reshape(2, depth, rows, chunk)

        @pl.when(step >= 2)
        def _():
            for off_x in range(2):
                some = far_ref.at[0, 0] if core_flip else kept_ref.at[0]
                leaving(some, step, off_x).wait()

        for off_x in range(2):
            total = product[off_x]
            if not core_flip:
                fetched(step, off_x).wait()
                total = total + got[step, off_x].astype(F32)
            ready[slot, off_x] = total.astype(LOW)
            first, second = spot(1 - step // parts, off_x)
            if core_flip:
                leaving(far_ref.at[first, second], step, off_x).start()
            else:
                for at, target in enumerate((kept_ref, sent_ref)):

                    @pl.when(first == at)
                    def _():
                        leaving(target.at[second], step, off_x).start()

        @pl.when(step == steps - 1)
        def _():
            for back in range(min(2, steps)):
                for off_x in range(2):
                    some = far_ref.at[0, 0] if core_flip else kept_ref.at[0]
                    leaving(some, step - back, off_x).wait()

    def right_at(t, me):
        return 0, ((me[0] & 1) ^ (1 - t // parts)) * parts + t % parts

    ins = [whole(width, count), pl.BlockSpec((count, chunk), right_at)]
    scratch = [
        pltpu.VMEM((2 * quarter, count), LOW),
        pltpu.VMEM((2, 2, depth, rows, chunk), LOW),
        pltpu.SemaphoreType.DMA((2, 2)),
    ]
    if core_flip:
        outs = ANY
        shapes = jax.ShapeDtypeStruct((2, 2, depth, rows, span), LOW)
        extra = ()
    else:
        ins = ins + [ANY]
        outs = [ANY, ANY]
        shapes = [jax.ShapeDtypeStruct((2, depth, rows, span), LOW)] * 2
        extra = (received,)
        scratch += [
            pltpu.VMEM((steps, 2, depth, rows, chunk), LOW),
            pltpu.SemaphoreType.DMA((steps, 2)),
        ]
    return call(
        body,
        (steps,),
        ins,
        outs,
        shapes,
        scratch,
        2 * count * width * span,
        count * (width + span * 2) * 2 + width * span * 4,
        name,
    )(me, turned, right, *extra)


def swap(value, size, bits, other=None):
    other = bits if other is None else other
    return lax.ppermute(
        value, AXES, [(i, i ^ (other if i & CORE_BIT else bits)) for i in range(size)]
    )


def after(value, *others):
    return lax.optimization_barrier((value, *others))[0]


def gather_depth(piece, size, depth):
    return jnp.stack([piece] + [swap(piece, size, k << Z_SHIFT) for k in range(1, depth)])


def along_first(value, size):
    return swap(value, size, Y_BIT, X_BIT)


def along_second(value, size):
    return swap(value, size, X_BIT, Y_BIT)


def along_core(value, size):
    return swap(value, size, CORE_BIT)


class Scatter:
    def __init__(self, turned, right, size, depth, name):
        self.size, self.depth, self.name = size, depth, name
        self.turned, self.right = turned, right

    def far(self, me):
        self.me = me
        self.sent = weight_grad_call(
            me, self.turned, self.right, self.depth, 1, None, self.name + "_far"
        )
        self.received = swap(self.sent, self.size, CORE_BIT)
        return self.sent

    def near(self, *others):
        right = after(self.right, *others)
        self.kept, self.sent = weight_grad_call(
            self.me, self.turned, right, self.depth, 0, self.received, self.name + "_near"
        )
        self.received = swap(self.sent, self.size, Y_BIT, X_BIT)
        return self.kept

    def second(self, *others):
        kept = after(self.kept, *others)
        total = (kept.astype(F32) + self.received.astype(F32)).astype(LOW)
        self.kept = total[0]
        self.received = swap(total[1], self.size, X_BIT, Y_BIT)
        return self.kept

    def third(self, *others):
        kept = after(self.kept, *others)
        total = (kept.astype(F32) + self.received.astype(F32)).astype(LOW)
        self.kept = total[0]
        self.received = [
            swap(total[k], self.size, k << Z_SHIFT) for k in range(1, self.depth)
        ]
        return self.kept

    def last(self, *others):
        result = after(self.kept, *others).astype(F32)
        for value in self.received:
            result = result + value.astype(F32)
        return result


def sum_all(value, size, depth):
    for bits in (CORE_BIT, X_BIT, Y_BIT):
        value = value + swap(value, size, bits)
    return sum((swap(value, size, k << Z_SHIFT) for k in range(1, depth)), value)


def shards(
    inputs,
    key_mask,
    ln1_gain,
    ln1_bias,
    w_qkv,
    qv_bias,
    w_proj,
    proj_bias,
    ln2_gain,
    ln2_bias,
    w_fc1,
    fc1_bias,
    w_fc2,
    fc2_bias,
    out_grad,
):
    tensor_rank = lax.axis_index("tensor")
    dp_rank = lax.axis_index("dp")
    dp_size = lax.axis_size("dp")
    size = 2 * dp_size
    depth = dp_size // 4
    own_images, seq, width = inputs.shape
    count = own_images * seq
    half = w_qkv.shape[2]
    rows = ln1_gain.shape[0]
    me = jnp.reshape(dp_rank * 2 + tensor_rank, (1,)).astype(jnp.int32)

    piece_one = jnp.concatenate([w_qkv[0], w_qkv[1], w_qkv[2], w_proj.T], axis=1).astype(LOW)
    piece_two = w_fc1.astype(LOW)
    piece_three = w_fc2.T.astype(LOW)
    vector = jnp.concatenate(
        [
            ln1_gain,
            ln1_bias,
            qv_bias[0],
            qv_bias[1],
            proj_bias,
            ln2_gain,
            ln2_bias,
            fc2_bias,
            fc1_bias,
        ]
    )
    vector = lax.optimization_barrier(vector).astype(LOW).astype(F32)

    held_one = gather_depth(piece_one, size, depth)
    gathered = lax.all_gather(vector, "dp", axis=0, tiled=False)
    held_one, gathered = lax.optimization_barrier((held_one, gathered))
    first_one = along_first(held_one, size)
    second_one = along_second(held_one, size)
    held_two = gather_depth(after(piece_two, held_one), size, depth)
    first_one, second_one, held_two = lax.optimization_barrier((first_one, second_one, held_two))
    both_one = along_second(first_one, size)
    plane_one = [held_one, second_one, first_one]
    pieces_one = [along_core(value, size) for value in plane_one]
    both_one, *pieces_one = lax.optimization_barrier((both_one, *pieces_one))
    pieces_one = plane_one + [both_one] + pieces_one + [along_core(both_one, size)]
    *pieces_one, held_two = lax.optimization_barrier((*pieces_one, held_two))
    first_two = along_first(held_two, size)
    second_two = along_second(held_two, size)
    held_three = gather_depth(after(piece_three, held_two), size, depth)
    table = gathered[:, : 8 * rows].reshape(dp_size, 8, rows).transpose(1, 0, 2).reshape(8, width)
    fc1_full = gathered[:, 8 * rows : 12 * rows].reshape(1, 4 * width)
    qkv_bias = jnp.stack(
        [table[2].reshape(2, half), jnp.zeros((2, half), F32), table[3].reshape(2, half)], axis=1
    ).reshape(1, 6 * half)

    rows_in = inputs.reshape(count, width)
    grad_in = out_grad.reshape(count, width)
    out_low = grad_in.astype(LOW)
    out_turned = out_low.T
    own_mask = lax.dynamic_slice_in_dim(key_mask, tensor_rank * own_images, own_images, 0)
    visible = jnp.concatenate(
        [jnp.ones((own_images, seq - key_mask.shape[1]), jnp.int32), own_mask], axis=1
    )
    visible_rows = after(visible, held_one)[:, :, None]
    visible = visible[:, None, :]

    normed_one, turned_one, qkv = qkv_call(me, rows_in, table, qkv_bias, pieces_one)
    mixed = attend_call(me, qkv, visible)
    mixed, first_two, second_two, held_three = lax.optimization_barrier(
        (mixed, first_two, second_two, held_three)
    )
    both_two = along_second(first_two, size)
    plane_two = [held_two, second_two, first_two]
    pieces_two = [along_core(value, size) for value in plane_two]
    middle, normed_two, turned_two = project_call(me, mixed, rows_in, table, pieces_one)
    both_two, normed_two, *pieces_two = lax.optimization_barrier((both_two, normed_two, *pieces_two))
    pieces_two = plane_two + [both_two] + pieces_two + [along_core(both_two, size)]
    *pieces_two, held_three = lax.optimization_barrier((*pieces_two, held_three))
    first_three = along_first(held_three, size)
    second_three = along_second(held_three, size)
    hidden, slope = expand_call(me, normed_two, fc1_full, pieces_two)
    hidden, first_three, second_three = lax.optimization_barrier(
        (hidden, first_three, second_three)
    )
    both_three = along_second(first_three, size)
    plane_three = [held_three, second_three, first_three]
    pieces_three = [along_core(value, size) for value in plane_three]
    fc2 = Scatter(out_turned, hidden, size, depth, "fc2_grad")
    done = fc2.far(me)
    done, both_three, *pieces_three = lax.optimization_barrier((done, both_three, *pieces_three))
    pieces_three = plane_three + [both_three] + pieces_three + [along_core(both_three, size)]
    outputs, pre_low, fc1_sum = contract_call(
        me, after(hidden, done), slope, out_low, middle, table, pieces_three
    )
    done = fc2.near(pre_low)
    fc1 = Scatter(turned_two, after(pre_low, done), size, depth, "fc1_grad")
    done = fc1.far(me)
    middle_grad, vec_two, middle_low, turned_mid = norm_back_call(
        me, after(pre_low, done), 0, 5, middle, grad_in, table, pieces_two, True, "norm_two_back"
    )
    done = fc2.second(middle_low)
    done = fc1.near(done)
    done = fc2.third(done)
    mixed_grad = mixed_back_call(me, after(middle_low, done), pieces_one)
    proj = Scatter(turned_mid, after(mixed, mixed_grad), size, depth, "proj_grad")
    done = proj.far(me)
    qkv_low, qkv_sum = attend_back_call(me, qkv, after(mixed_grad, done), visible_rows)
    done = proj.near(qkv_low)
    done = fc1.second(done)
    qkv_out = Scatter(turned_one, after(qkv_low, done), size, depth, "qkv_grad")
    done = qkv_out.far(me)
    done = fc1.third(proj.second(done))
    fc2_grad = fc2.last(done)
    done = qkv_out.near(fc2_grad)
    input_grad, vec_one = norm_back_call(
        me,
        after(qkv_low, done),
        0,
        0,
        rows_in,
        middle_grad,
        table,
        pieces_one,
        False,
        "norm_one_back",
    )
    proj.third(input_grad)
    qkv_out.second(input_grad)
    qkv_out.third()
    fc1_grad = fc1.last()
    proj_grad = proj.last()
    qkv_grad = qkv_out.last()

    qkv_sum = jnp.sum(qkv_sum, axis=(0, 2)).reshape(2, 3, half)
    sums = jnp.concatenate(
        [
            vec_one[:2],
            qkv_sum[:, 0].reshape(1, width),
            qkv_sum[:, 2].reshape(1, width),
            vec_two[2:3],
            vec_two[:2],
            jnp.sum(grad_in, axis=0, keepdims=True),
            fc1_sum.reshape(4, width),
        ]
    )
    sums = sum_all(sums, size, depth)
    mine = lax.dynamic_slice_in_dim(sums[:8], dp_rank * rows, rows, 1)
    fc1_mine = lax.dynamic_slice_in_dim(sums[8:].reshape(-1), dp_rank * 4 * rows, 4 * rows, 0)
    return (
        outputs.reshape(inputs.shape),
        input_grad.reshape(inputs.shape),
        mine[0],
        mine[1],
        qkv_grad.reshape(rows, 3, half).transpose(1, 0, 2),
        mine[2:4],
        proj_grad.T,
        mine[4],
        mine[5],
        mine[6],
        fc1_grad,
        fc1_mine,
        fc2_grad.T,
        mine[7],
    )


def solution(mesh):
    placed = (
        P(("dp", "tensor"), None, None),
        P("dp", None),
        P("dp"),
        P("dp"),
        P(None, "dp", "tensor"),
        P(None, "dp"),
        P("tensor", "dp"),
        P("dp"),
        P("dp"),
        P("dp"),
        P("dp", "tensor"),
        P("dp"),
        P("tensor", "dp"),
        P("dp"),
        P(("dp", "tensor"), None, None),
    )
    return jax.shard_map(
        shards,
        mesh=mesh,
        in_specs=placed,
        out_specs=(
            P(("dp", "tensor"), None, None),
            P(("dp", "tensor"), None, None),
            P("dp"),
            P("dp"),
            P(None, "dp", "tensor"),
            P(None, "dp"),
            P("tensor", "dp"),
            P("dp"),
            P("dp"),
            P("dp"),
            P("dp", "tensor"),
            P("dp"),
            P("tensor", "dp"),
            P("dp"),
        ),
        check_vma=False,
    )
```

```python
import jax
import jax.numpy as jnp
from jax import lax
from jax.experimental import pallas as pl
from jax.experimental.pallas import tpu as pltpu
from jax.sharding import PartitionSpec as P

HEAD_DIM = 64
norm_eps = 1e-06
masked_score = -1e30
AXES = ("dp", "tensor")
LOW = jnp.bfloat16
F32 = jnp.float32
TILE = 128
Y_BIT, CORE_BIT, X_BIT, Z_SHIFT = 1, 2, 4, 3
ANY = pl.BlockSpec(memory_space=pltpu.HBM)


def mm(left, right):
    return lax.dot_general(left, right, (((1,), (0,)), ((), ())), preferred_element_type=F32)


def mm_nt(left, right):
    return lax.dot_general(left, right, (((1,), (1,)), ((), ())), preferred_element_type=F32)


def mm_tn(left, right):
    return lax.dot_general(left, right, (((0,), (0,)), ((), ())), preferred_element_type=F32)


def whole(*shape):
    return pl.BlockSpec(shape, lambda t, me: (0,) * len(shape))


def call(body, grid, ins, outs, shapes, scratch, flops, moved, name):
    return pl.pallas_call(
        body,
        grid_spec=pltpu.PrefetchScalarGridSpec(
            num_scalar_prefetch=1,
            grid=grid,
            in_specs=ins,
            out_specs=outs,
            scratch_shapes=scratch,
        ),
        out_shape=shapes,
        compiler_params=pltpu.CompilerParams(
            dimension_semantics=("arbitrary",) * len(grid), vmem_limit_bytes=32 << 20
        ),
        cost_estimate=pl.CostEstimate(flops=1, bytes_accessed=1, transcendentals=0),
        name=name,
    )


def places(me, core_flip, first, second):
    owner = ((me >> 1) & 1) ^ core_flip
    off_y = jnp.where(owner == 0, first, second)
    off_x = jnp.where(owner == 0, second, first)
    return off_y, off_x


def dp_of(me, core_flip, off_x, off_z):
    core = ((me >> 1) & 1) ^ core_flip
    return (((me >> Z_SHIFT) ^ off_z) << 2) | ((((me >> 2) & 1) ^ off_x) << 1) | core


def fetch(me, pieces, store, sems, start, width):
    for index, piece in enumerate(pieces):
        core_flip, first, second = index >> 2, (index >> 1) & 1, index & 1
        off_y, off_x = places(me, core_flip, first, second)
        y_at = (me & 1) ^ off_y
        depth, rows, _ = piece.shape
        for off_z in range(depth):
            row = pl.multiple_of(dp_of(me, core_flip, off_x, off_z) * rows, rows)
            pltpu.make_async_copy(
                piece.at[off_z, :, pl.ds(start, width)],
                store.at[y_at, pl.ds(row, rows), :],
                sems.at[y_at],
            ).start()


def arrived(store, sems, y_at):
    pltpu.make_async_copy(store.at[y_at], store.at[y_at], sems.at[y_at]).wait()


def normed(rows, gain, shift):
    center = rows - jnp.mean(rows, axis=-1, keepdims=True)
    spread = jnp.mean(center * center, axis=-1, keepdims=True)
    return center * lax.rsqrt(spread + norm_eps) * gain + shift


def qkv_call(me, rows_in, pieces):
    count, width = rows_in.shape
    half = width // 2
    span = 3 * half

    def body(me_ref, x_ref, *refs):
        parts, refs = refs[:8], refs[8:]
        norm_ref, turn_ref, out_ref, table_ref, store, sems, vectors, vector_sems = refs
        step = pl.program_id(0)

        @pl.when(step == 0)
        def _():
            fetch(me_ref[0], parts, vectors, vector_sems, span, TILE)
            fetch(me_ref[0], parts, store, sems, 0, span)
            for y_at in range(2):
                arrived(vectors, vector_sems, y_at)
            table_ref[...] = vectors[0].astype(F32).T[: table_ref.shape[0]]

            @pl.loop(0, count // TILE)
            def _(i):
                at = pl.ds(pl.multiple_of(i * TILE, TILE), TILE)
                value = normed(x_ref[at, :], table_ref[0:1, :], table_ref[1:2, :])
                norm_ref[at, :] = value.astype(LOW)
                turn_ref[:, at] = value.T.astype(LOW)

        for y_at in range(2):

            @pl.when(step == 3 * y_at)
            def _():
                arrived(store, sems, y_at)

        y_at, kind = step // 3, step % 3
        col = pl.multiple_of(kind * half, half)
        own = pl.ds(pl.multiple_of(y_at * half, half), half)
        product = mm(norm_ref[...], store[y_at, :, pl.ds(col, half)])
        bias = jnp.where(kind == 0, table_ref[2:3, own], table_ref[3:4, own])
        bias = jnp.where(kind == 1, 0.0, bias)
        out_ref[...] = (product + bias).astype(LOW)

    return call(
        body,
        (6,),
        [whole(count, width)] + [ANY] * 8,
        [
            whole(count, width),
            whole(width, count),
            pl.BlockSpec((count, half), lambda t, me: (0, t)),
            whole(16, width),
        ],
        [
            jax.ShapeDtypeStruct((count, width), LOW),
            jax.ShapeDtypeStruct((width, count), LOW),
            jax.ShapeDtypeStruct((count, 2 * span), LOW),
            jax.ShapeDtypeStruct((16, width), F32),
        ],
        [
            pltpu.VMEM((2, width, span), LOW),
            pltpu.SemaphoreType.DMA((2,)),
            pltpu.VMEM((2, width, TILE), LOW),
            pltpu.SemaphoreType.DMA((2,)),
        ],
        2 * count * width * 2 * span,
        count * width * 16 + width * span * 4,
        "qkv",
    )(me, rows_in, *pieces)


def head_halves(shape):
    lane = lax.broadcasted_iota(jnp.int32, shape, 1)
    return lane < HEAD_DIM, lane >= HEAD_DIM


def attend_call(me, qkv, visible):
    images, _, seq = visible.shape
    count, full = qkv.shape
    half = full // 6

    def body(me_ref, qkv_ref, seen_ref, out_ref):
        seen = seen_ref[0] > 0

        for col in range(0, half, TILE):
            query = qkv_ref[:, col : col + TILE] * jnp.asarray(HEAD_DIM**-0.5, LOW)
            key = qkv_ref[:, half + col : half + col + TILE]
            value = qkv_ref[:, 2 * half + col : 2 * half + col + TILE]
            lanes = head_halves(query.shape)
            mixed = []
            for keep in lanes:
                scores = jnp.where(seen, mm_nt(jnp.where(keep, query, 0), key), masked_score)
                exps = jnp.exp(scores - jnp.max(scores, axis=-1, keepdims=True))
                total = jnp.sum(exps, axis=-1, keepdims=True)
                mixed.append(mm(exps.astype(LOW), value) * (1.0 / total))
            out_ref[:, col : col + TILE] = jnp.where(lanes[0], mixed[0], mixed[1]).astype(LOW)

    return call(
        body,
        (images, 2),
        [
            pl.BlockSpec((seq, 3 * half), lambda i, y, me: (i, y)),
            pl.BlockSpec((1, 1, seq), lambda i, y, me: (i, 0, 0)),
        ],
        pl.BlockSpec((seq, half), lambda i, y, me: (i, y)),
        jax.ShapeDtypeStruct((count, 2 * half), LOW),
        [],
        4 * count * seq * 2 * half * 4,
        count * full * 3,
        "attend",
    )(me, qkv, visible)


def project_call(me, mixed, rows_in, table, pieces):
    count, width = rows_in.shape
    half = width // 2

    def body(me_ref, mixed_ref, x_ref, table_ref, *refs):
        parts, (mid_ref, norm_ref, turn_ref, store, sems) = refs[:8], refs[8:]
        fetch(me_ref[0], parts, store, sems, 2 * width, half)
        arrived(store, sems, 0)
        mid_ref[...] = mm_nt(mixed_ref[:, :half], store[0])
        arrived(store, sems, 1)
        mid_ref[...] += mm_nt(mixed_ref[:, half:], store[1])

        @pl.loop(0, count // TILE)
        def _(i):
            at = pl.ds(pl.multiple_of(i * TILE, TILE), TILE)
            middle = x_ref[at, :] + (mid_ref[at, :] + table_ref[4:5, :])
            mid_ref[at, :] = middle
            value = normed(middle, table_ref[5:6, :], table_ref[6:7, :])
            norm_ref[at, :] = value.astype(LOW)
            turn_ref[:, at] = value.T.astype(LOW)

    return call(
        body,
        (1,),
        [whole(count, width), whole(count, width), whole(*table.shape)] + [ANY] * 8,
        [whole(count, width), whole(count, width), whole(width, count)],
        [
            jax.ShapeDtypeStruct((count, width), F32),
            jax.ShapeDtypeStruct((count, width), LOW),
            jax.ShapeDtypeStruct((width, count), LOW),
        ],
        [pltpu.VMEM((2, width, half), LOW), pltpu.SemaphoreType.DMA((2,))],
        2 * count * width * width,
        count * width * 14 + width * width * 2,
        "project",
    )(me, mixed, rows_in, table, *pieces)


def expand_call(me, normed_two, bias, pieces):
    count, width = normed_two.shape
    span = bias.shape[1] // 2
    chunk = span // 4

    def body(me_ref, norm_ref, bias_ref, *refs):
        parts, (hid_ref, slope_ref, store, sems) = refs[:8], refs[8:]
        step = pl.program_id(0)

        @pl.when(step == 0)
        def _():
            fetch(me_ref[0], parts, store, sems, 0, span)

        for y_at in range(2):

            @pl.when(step == 4 * y_at)
            def _():
                arrived(store, sems, y_at)

        y_at, col = step // 4, pl.multiple_of(step % 4 * chunk, chunk)
        pre = mm(norm_ref[...], store[y_at, :, pl.ds(col, chunk)]) + bias_ref[...]
        below = 0.5 + 0.5 * lax.erf(pre * 0.5**0.5)
        hid_ref[...] = (pre * below).astype(LOW)
        slope_ref[...] = (below + pre * jnp.exp(pre * pre * -0.5) * 0.3989422804014327).astype(LOW)

    out = pl.BlockSpec((count, chunk), lambda t, me: (0, t))
    return call(
        body,
        (8,),
        [whole(count, width), pl.BlockSpec((1, chunk), lambda t, me: (0, t))] + [ANY] * 8,
        [out, out],
        [jax.ShapeDtypeStruct((count, 2 * span), LOW)] * 2,
        [pltpu.VMEM((2, width, span), LOW), pltpu.SemaphoreType.DMA((2,))],
        2 * count * width * 2 * span,
        count * span * 8 + width * span * 4,
        "expand",
    )(me, normed_two, bias, *pieces)


def contract_call(me, hidden, slope, out_low, middle, table, pieces):
    count, width = middle.shape
    span = hidden.shape[1] // 2
    chunk = span // 4

    def body(me_ref, hid_ref, slope_ref, low_ref, mid_ref, table_ref, *refs):
        parts, (act_ref, pre_ref, sum_ref, store, sems) = refs[:8], refs[8:]
        step = pl.program_id(0)

        @pl.when(step == 0)
        def _():
            fetch(me_ref[0], parts, store, sems, 0, span)
            act_ref[...] = mid_ref[...] + table_ref[7:8, :]

        for y_at in range(2):

            @pl.when(step == 4 * y_at)
            def _():
                arrived(store, sems, y_at)

        y_at, col = step // 4, pl.multiple_of(step % 4 * chunk, chunk)
        weight = store[y_at, :, pl.ds(col, chunk)]
        act_ref[...] += mm_nt(hid_ref[...], weight)
        pre = mm(low_ref[...], weight) * slope_ref[...].astype(F32)
        pre_ref[...] = pre.astype(LOW)
        sum_ref[...] = jnp.sum(pre, axis=0, keepdims=True)

    part = pl.BlockSpec((count, chunk), lambda t, me: (0, t))
    return call(
        body,
        (8,),
        [part, part, whole(count, width), whole(count, width), whole(*table.shape)] + [ANY] * 8,
        [whole(count, width), part, pl.BlockSpec((1, chunk), lambda t, me: (0, t))],
        [
            jax.ShapeDtypeStruct((count, width), F32),
            jax.ShapeDtypeStruct((count, 2 * span), LOW),
            jax.ShapeDtypeStruct((1, 2 * span), F32),
        ],
        [pltpu.VMEM((2, width, span), LOW), pltpu.SemaphoreType.DMA((2,))],
        4 * count * width * 2 * span,
        count * span * 12 + width * span * 4,
        "contract",
    )(me, hidden, slope, out_low, middle, table, *pieces)


def norm_back_call(me, low, start, gain_row, rows_in, base, table, pieces, keep_low, name):
    count, width = rows_in.shape
    span = low.shape[1] // 2
    chunk = span // 2

    def body(me_ref, low_ref, x_ref, base_ref, table_ref, *refs):
        parts, outs = refs[:8], refs[8:]
        if keep_low:
            grad_ref, vec_ref, out_low_ref, turn_ref, store, sems = outs
        else:
            grad_ref, vec_ref, store, sems = outs
        step = pl.program_id(0)

        @pl.when(step == 0)
        def _():
            fetch(me_ref[0], parts, store, sems, start, span)

        for y_at in range(2):

            @pl.when(step == 2 * y_at)
            def _():
                arrived(store, sems, y_at)

        y_at, col = step // 2, pl.multiple_of(step % 2 * chunk, chunk)
        product = mm_nt(low_ref[...], store[y_at, :, pl.ds(col, chunk)])

        @pl.when(step == 0)
        def _():
            grad_ref[...] = product

        @pl.when(step > 0)
        def _():
            grad_ref[...] += product

        @pl.when(step == 3)
        def _():
            vec_ref[...] = jnp.zeros_like(vec_ref)

            @pl.loop(0, count // TILE)
            def _(i):
                at = pl.ds(pl.multiple_of(i * TILE, TILE), TILE)
                back = grad_ref[at, :]
                rows = x_ref[at, :]
                center = rows - jnp.mean(rows, axis=-1, keepdims=True)
                spread = jnp.mean(center * center, axis=-1, keepdims=True)
                scale = lax.rsqrt(spread + norm_eps)
                unit = center * scale
                inner = back * table_ref[gain_row : gain_row + 1, :]
                along = jnp.mean(inner * unit, axis=-1, keepdims=True)
                level = jnp.mean(inner, axis=-1, keepdims=True)
                grad = base_ref[at, :] + scale * (inner - level - unit * along)
                grad_ref[at, :] = grad
                vec_ref[0:1, :] += jnp.sum(back * unit, axis=0, keepdims=True)
                vec_ref[1:2, :] += jnp.sum(back, axis=0, keepdims=True)
                vec_ref[2:3, :] += jnp.sum(grad, axis=0, keepdims=True)
                if keep_low:
                    out_low_ref[at, :] = grad.astype(LOW)
                    turn_ref[:, at] = grad.T.astype(LOW)

    outs = [whole(count, width), whole(8, width)]
    shapes = [jax.ShapeDtypeStruct((count, width), F32), jax.ShapeDtypeStruct((8, width), F32)]
    if keep_low:
        outs += [whole(count, width), whole(width, count)]
        shapes += [
            jax.ShapeDtypeStruct((count, width), LOW),
            jax.ShapeDtypeStruct((width, count), LOW),
        ]
    return call(
        body,
        (4,),
        [
            pl.BlockSpec((count, chunk), lambda t, me: (0, t)),
            whole(count, width),
            whole(count, width),
            whole(*table.shape),
        ]
        + [ANY] * 8,
        outs,
        shapes,
        [pltpu.VMEM((2, width, span), LOW), pltpu.SemaphoreType.DMA((2,))],
        2 * count * width * 2 * span,
        count * width * 16 + width * span * 4 + count * span * 4,
        name,
    )(me, low, rows_in, base, table, *pieces)


def mixed_back_call(me, middle_low, pieces):
    count, width = middle_low.shape
    half = width // 2

    def body(me_ref, low_ref, *refs):
        parts, (out_ref, store, sems) = refs[:8], refs[8:]
        step = pl.program_id(0)

        @pl.when(step == 0)
        def _():
            fetch(me_ref[0], parts, store, sems, 2 * width, half)

        for y_at in range(2):

            @pl.when(step == y_at)
            def _():
                arrived(store, sems, y_at)

        out_ref[...] = mm(low_ref[...], store[step]).astype(LOW)

    return call(
        body,
        (2,),
        [whole(count, width)] + [ANY] * 8,
        pl.BlockSpec((count, half), lambda t, me: (0, t)),
        jax.ShapeDtypeStruct((count, width), LOW),
        [pltpu.VMEM((2, width, half), LOW), pltpu.SemaphoreType.DMA((2,))],
        2 * count * width * width,
        count * width * 4 + width * width * 2,
        "mixed_back",
    )(me, middle_low, *pieces)


def attend_back_call(me, qkv, grads, visible):
    images, seq, _ = visible.shape
    count, full = qkv.shape
    half = full // 6
    scale = HEAD_DIM**-0.5

    def body(me_ref, qkv_ref, grad_ref, seen_ref, out_ref, sum_ref):
        seen = seen_ref[0] > 0
        for col in range(0, half, TILE):
            query = qkv_ref[:, col : col + TILE] * jnp.asarray(scale, LOW)
            key = qkv_ref[:, half + col : half + col + TILE]
            value = qkv_ref[:, 2 * half + col : 2 * half + col + TILE]
            grad = grad_ref[:, col : col + TILE]
            lanes = head_halves(query.shape)
            parts = []
            for keep in lanes:
                scores = jnp.where(seen, mm_nt(jnp.where(keep, key, 0), query), masked_score)
                exps = jnp.exp(scores - jnp.max(scores, axis=0, keepdims=True))
                probs = exps * (1.0 / jnp.sum(exps, axis=0, keepdims=True))
                prob_grad = mm_nt(jnp.where(keep, value, 0), grad)
                row_dot = jnp.sum(probs * prob_grad, axis=0, keepdims=True)
                score_grad = (probs * (prob_grad - row_dot)).astype(LOW)
                parts.append(
                    (
                        mm_tn(key, score_grad).T * scale,
                        mm(score_grad, query),
                        mm(probs.astype(LOW), grad),
                    )
                )
            for at in range(3):
                merged = jnp.where(lanes[0], parts[0][at], parts[1][at])
                put = at * half + col
                out_ref[:, put : put + TILE] = merged.astype(LOW)
                sum_ref[0, 0, :, put : put + TILE] = jnp.sum(merged, axis=0, keepdims=True)

    return call(
        body,
        (images, 2),
        [
            pl.BlockSpec((seq, 3 * half), lambda i, y, me: (i, y)),
            pl.BlockSpec((seq, half), lambda i, y, me: (i, y)),
            pl.BlockSpec((1, seq, 1), lambda i, y, me: (i, 0, 0)),
        ],
        [
            pl.BlockSpec((seq, 3 * half), lambda i, y, me: (i, y)),
            pl.BlockSpec((1, 1, 1, 3 * half), lambda i, y, me: (i, y, 0, 0)),
        ],
        [
            jax.ShapeDtypeStruct((count, full), LOW),
            jax.ShapeDtypeStruct((images, 2, 1, 3 * half), F32),
        ],
        [],
        10 * count * seq * 2 * half * 4,
        count * full * 5,
        "attend_back",
    )(me, qkv, grads, visible)


def weight_grad_call(me, turned, right, depth, core_flip, received, name):
    width, count = turned.shape
    span = right.shape[1] // 2
    chunk = next(c for c in (1024, 768, 512, 384, 256, 128) if span % c == 0)
    parts = span // chunk
    steps = 2 * parts
    rows = width // (4 * depth)
    quarter = width // 4

    def body(me_ref, turn_ref, right_ref, *refs):
        if core_flip:
            (far_ref, lefts, ready, sems) = refs
        else:
            (got_ref, kept_ref, sent_ref, lefts, ready, sems, got, got_sems) = refs
        step = pl.program_id(0)
        slot = step % 2
        owner = ((me_ref[0] >> 1) & 1) ^ core_flip

        def spot(off_y, off_x):
            return jnp.where(owner == 0, off_y, off_x), jnp.where(owner == 0, off_x, off_y)

        def fetched(at, off_x):
            first, second = spot(1 - at // parts, off_x)
            col = pl.multiple_of(at % parts * chunk, chunk)
            return pltpu.make_async_copy(
                got_ref.at[first, second, :, :, pl.ds(col, chunk)],
                got.at[at, off_x],
                got_sems.at[at, off_x],
            )

        def leaving(target, at, off_x):
            col = pl.multiple_of(at % parts * chunk, chunk)
            return pltpu.make_async_copy(
                ready.at[at % 2, off_x],
                target.at[:, :, pl.ds(col, chunk)],
                sems.at[at % 2, off_x],
            )

        @pl.when(step == 0)
        def _():
            if not core_flip:
                for at in range(steps):
                    for off_x in range(2):
                        fetched(at, off_x).start()
            for off_x in range(2):
                for off_z in range(depth):
                    row = pl.multiple_of(dp_of(me_ref[0], core_flip, off_x, off_z) * rows, rows)
                    put = off_x * quarter + off_z * rows
                    lefts[put : put + rows, :] = turn_ref[pl.ds(row, rows), :]

        product = mm(lefts[...], right_ref[...]).reshape(2, depth, rows, chunk)

        @pl.when(step >= 2)
        def _():
            for off_x in range(2):
                some = far_ref.at[0, 0] if core_flip else kept_ref.at[0]
                leaving(some, step, off_x).wait()

        for off_x in range(2):
            total = product[off_x]
            if not core_flip:
                fetched(step, off_x).wait()
                total = total + got[step, off_x].astype(F32)
            ready[slot, off_x] = total.astype(LOW)
            first, second = spot(1 - step // parts, off_x)
            if core_flip:
                leaving(far_ref.at[first, second], step, off_x).start()
            else:
                for at, target in enumerate((kept_ref, sent_ref)):

                    @pl.when(first == at)
                    def _():
                        leaving(target.at[second], step, off_x).start()

        @pl.when(step == steps - 1)
        def _():
            for back in range(min(2, steps)):
                for off_x in range(2):
                    some = far_ref.at[0, 0] if core_flip else kept_ref.at[0]
                    leaving(some, step - back, off_x).wait()

    def right_at(t, me):
        return 0, ((me[0] & 1) ^ (1 - t // parts)) * parts + t % parts

    ins = [whole(width, count), pl.BlockSpec((count, chunk), right_at)]
    scratch = [
        pltpu.VMEM((2 * quarter, count), LOW),
        pltpu.VMEM((2, 2, depth, rows, chunk), LOW),
        pltpu.SemaphoreType.DMA((2, 2)),
    ]
    if core_flip:
        outs = ANY
        shapes = jax.ShapeDtypeStruct((2, 2, depth, rows, span), LOW)
        extra = ()
    else:
        ins = ins + [ANY]
        outs = [ANY, ANY]
        shapes = [jax.ShapeDtypeStruct((2, depth, rows, span), LOW)] * 2
        extra = (received,)
        scratch += [
            pltpu.VMEM((steps, 2, depth, rows, chunk), LOW),
            pltpu.SemaphoreType.DMA((steps, 2)),
        ]
    return call(
        body,
        (steps,),
        ins,
        outs,
        shapes,
        scratch,
        2 * count * width * span,
        count * (width + span * 2) * 2 + width * span * 4,
        name,
    )(me, turned, right, *extra)


def swap(value, size, bits, other=None):
    other = bits if other is None else other
    return lax.ppermute(
        value, AXES, [(i, i ^ (other if i & CORE_BIT else bits)) for i in range(size)]
    )


def after(value, *others):
    return lax.optimization_barrier((value, *others))[0]


def along_depth(piece, size, steps):
    return [piece] + [swap(piece, size, k << Z_SHIFT) for k in steps]


def along_first(value, size):
    return swap(value, size, Y_BIT, X_BIT)


def along_second(value, size):
    return swap(value, size, X_BIT, Y_BIT)


def along_core(value, size):
    return swap(value, size, CORE_BIT)


class Scatter:
    def __init__(self, turned, right, size, depth, name):
        self.size, self.depth, self.name = size, depth, name
        self.turned, self.right = turned, right

    def far(self, me):
        self.me = me
        self.sent = weight_grad_call(
            me, self.turned, self.right, self.depth, 1, None, self.name + "_far"
        )
        self.received = swap(self.sent, self.size, CORE_BIT)
        return self.sent

    def near(self, *others):
        right = after(self.right, *others)
        self.kept, self.sent = weight_grad_call(
            self.me, self.turned, right, self.depth, 0, self.received, self.name + "_near"
        )
        self.received = swap(self.sent, self.size, Y_BIT, X_BIT)
        return self.kept

    def second(self, *others):
        kept = after(self.kept, *others)
        total = (kept.astype(F32) + self.received.astype(F32)).astype(LOW)
        self.kept = total[0]
        self.received = swap(total[1], self.size, X_BIT, Y_BIT)
        return self.kept

    def third(self, *others):
        kept = after(self.kept, *others)
        total = (kept.astype(F32) + self.received.astype(F32)).astype(LOW)
        self.kept = total[0]
        self.received = [
            swap(total[k], self.size, k << Z_SHIFT) for k in range(1, self.depth)
        ]
        return self.kept

    def last(self, *others):
        result = after(self.kept, *others).astype(F32)
        for value in self.received:
            result = result + value.astype(F32)
        return result


def shards(
    inputs,
    key_mask,
    ln1_gain,
    ln1_bias,
    w_qkv,
    qv_bias,
    w_proj,
    proj_bias,
    ln2_gain,
    ln2_bias,
    w_fc1,
    fc1_bias,
    w_fc2,
    fc2_bias,
    out_grad,
):
    tensor_rank = lax.axis_index("tensor")
    dp_rank = lax.axis_index("dp")
    dp_size = lax.axis_size("dp")
    size = 2 * dp_size
    depth = dp_size // 4
    own_images, seq, width = inputs.shape
    count = own_images * seq
    half = w_qkv.shape[2]
    rows = ln1_gain.shape[0]
    me = jnp.reshape(dp_rank * 2 + tensor_rank, (1,)).astype(jnp.int32)

    vectors = jnp.concatenate(
        [
            jnp.stack([ln1_gain, ln1_bias, qv_bias[0], qv_bias[1]]),
            jnp.stack([proj_bias, ln2_gain, ln2_bias, fc2_bias]),
            fc1_bias.reshape(4, rows),
        ]
    )
    vectors = jnp.pad(vectors, ((0, TILE - vectors.shape[0]), (0, 0))).T
    piece_one = jnp.concatenate([w_qkv[0], w_qkv[1], w_qkv[2], vectors], axis=1).astype(LOW)
    piece_two = jnp.concatenate([w_fc1, w_proj.T], axis=1).astype(LOW)
    piece_three = w_fc2.T.astype(LOW)

    held_one = jnp.stack(along_depth(piece_one, size, range(1, depth)))
    held_one, piece_two = lax.optimization_barrier((held_one, piece_two))
    first_one = along_first(held_one, size)
    second_one = along_second(held_one, size)
    far_one = [along_core(held_one, size)]
    deep_two = along_depth(piece_two, size, range(1, depth - 1))
    first_one, second_one, far_own, *deep_two = lax.optimization_barrier(
        (first_one, second_one, *far_one, *deep_two)
    )
    both_one = along_second(first_one, size)
    far_one = [far_own, along_core(second_one, size), along_core(first_one, size)]
    plane_one = [held_one, second_one, first_one]
    deep_two += along_depth(deep_two[0], size, [depth - 1])[1:]
    far_one += [along_core(both_one, size)]
    both_one, piece_three, *deep_two = lax.optimization_barrier((both_one, piece_three, *deep_two))
    pieces_one = plane_one + [both_one] + far_one
    held_two = jnp.stack(deep_two)
    first_two = along_first(held_two, size)
    second_two = along_second(held_two, size)
    far_two = [along_core(held_two, size)]
    deep_three = along_depth(piece_three, size, range(1, depth - 1))

    rows_in = inputs.reshape(count, width)
    grad_in = out_grad.reshape(count, width)
    out_low = grad_in.astype(LOW)
    out_turned = out_low.T
    own_mask = lax.dynamic_slice_in_dim(key_mask, tensor_rank * own_images, own_images, 0)
    visible = jnp.concatenate(
        [jnp.ones((own_images, seq - key_mask.shape[1]), jnp.int32), own_mask], axis=1
    )
    visible_rows = after(visible, held_one)[:, :, None]
    visible = visible[:, None, :]

    normed_one, turned_one, qkv, table = qkv_call(me, rows_in, pieces_one)
    fc1_full = table[8:12].reshape(4, dp_size, rows).transpose(1, 0, 2).reshape(1, 4 * width)
    mixed = attend_call(me, qkv, visible)
    mixed, first_two, second_two, *deep_three, far_own = lax.optimization_barrier(
        (mixed, first_two, second_two, *deep_three, *far_two)
    )
    both_two = along_second(first_two, size)
    far_two = [far_own, along_core(second_two, size), along_core(first_two, size)]
    plane_two = [held_two, second_two, first_two]
    deep_three += along_depth(deep_three[0], size, [depth - 1])[1:]
    far_two += [along_core(both_two, size)]
    both_two, *deep_three = lax.optimization_barrier((both_two, *deep_three))
    pieces_two = plane_two + [both_two] + far_two
    held_three = jnp.stack(deep_three)
    first_three = along_first(held_three, size)
    second_three = along_second(held_three, size)
    far_three = [along_core(held_three, size)]
    middle, normed_two, turned_two = project_call(me, mixed, rows_in, table, pieces_two)
    hidden, slope = expand_call(me, normed_two, fc1_full, pieces_two)
    hidden, first_three, second_three, far_own = lax.optimization_barrier(
        (hidden, first_three, second_three, *far_three)
    )
    both_three = along_second(first_three, size)
    far_three = [far_own, along_core(second_three, size), along_core(first_three, size)]
    plane_three = [held_three, second_three, first_three]
    fc2 = Scatter(out_turned, hidden, size, depth, "fc2_grad")
    done = fc2.far(me)
    fc2.near(done, both_three)
    pieces_three = plane_three + [both_three] + far_three + [along_core(both_three, size)]
    outputs, pre_low, fc1_sum = contract_call(
        me, after(hidden, fc2.kept), slope, out_low, middle, table, pieces_three
    )
    middle_grad, vec_two, middle_low, turned_mid = norm_back_call(
        me, pre_low, 0, 5, middle, grad_in, table, pieces_two, True, "norm_two_back"
    )
    fc1 = Scatter(turned_two, after(pre_low, middle_low), size, depth, "fc1_grad")
    done = fc1.far(me)
    done = fc2.second(done)
    mixed_grad = mixed_back_call(me, after(middle_low, done), pieces_two)
    proj = Scatter(turned_mid, after(mixed, mixed_grad), size, depth, "proj_grad")
    done = proj.far(me)
    done = fc2.third(done)
    done = fc1.near(done)
    qkv_low, qkv_sum = attend_back_call(me, qkv, after(mixed_grad, done), visible_rows)
    fc2_grad = fc2.last(qkv_low)
    done = fc1.second(fc2_grad)
    done = proj.near(done)
    qkv_out = Scatter(turned_one, after(qkv_low, done), size, depth, "qkv_grad")
    done = qkv_out.far(me)
    done = proj.second(done)
    done = qkv_out.near(done)
    done = fc1.third(done)
    input_grad, vec_one = norm_back_call(
        me,
        after(qkv_low, done),
        0,
        0,
        rows_in,
        middle_grad,
        table,
        pieces_one,
        False,
        "norm_one_back",
    )

    qkv_sum = jnp.sum(qkv_sum, axis=(0, 2)).reshape(2, 3, half)
    sums = jnp.concatenate(
        [
            vec_one[:2],
            qkv_sum[:, 0].reshape(1, width),
            qkv_sum[:, 2].reshape(1, width),
            vec_two[2:3],
            vec_two[:2],
            jnp.sum(grad_in, axis=0, keepdims=True),
            fc1_sum.reshape(4, width),
        ]
    )
    fc1_grad = fc1.last(input_grad)
    done = qkv_out.second(fc1_grad)
    done = proj.third(done)
    sums = after(sums, done)
    for bits in (CORE_BIT, X_BIT, Y_BIT):
        sums = sums + swap(sums, size, bits)
    done = qkv_out.third(sums)
    proj_grad = proj.last(done)
    sums = sum(along_depth(after(sums, done), size, range(1, depth)))
    qkv_grad = qkv_out.last()
    mine = lax.dynamic_slice_in_dim(sums[:8], dp_rank * rows, rows, 1)
    fc1_mine = lax.dynamic_slice_in_dim(sums[8:].reshape(-1), dp_rank * 4 * rows, 4 * rows, 0)
    return (
        outputs.reshape(inputs.shape),
        input_grad.reshape(inputs.shape),
        mine[0],
        mine[1],
        qkv_grad.reshape(rows, 3, half).transpose(1, 0, 2),
        mine[2:4],
        proj_grad.T,
        mine[4],
        mine[5],
        mine[6],
        fc1_grad,
        fc1_mine,
        fc2_grad.T,
        mine[7],
    )


def solution(mesh):
    placed = (
        P(("dp", "tensor"), None, None),
        P("dp", None),
        P("dp"),
        P("dp"),
        P(None, "dp", "tensor"),
        P(None, "dp"),
        P("tensor", "dp"),
        P("dp"),
        P("dp"),
        P("dp"),
        P("dp", "tensor"),
        P("dp"),
        P("tensor", "dp"),
        P("dp"),
        P(("dp", "tensor"), None, None),
    )
    return jax.shard_map(
        shards,
        mesh=mesh,
        in_specs=placed,
        out_specs=(
            P(("dp", "tensor"), None, None),
            P(("dp", "tensor"), None, None),
            P("dp"),
            P("dp"),
            P(None, "dp", "tensor"),
            P(None, "dp"),
            P("tensor", "dp"),
            P("dp"),
            P("dp"),
            P("dp"),
            P("dp", "tensor"),
            P("dp"),
            P("tensor", "dp"),
            P("dp"),
        ),
        check_vma=False,
    )
```

```python
import jax
import jax.numpy as jnp
from jax import lax
from jax.experimental import pallas as pl
from jax.experimental.pallas import tpu as pltpu
from jax.sharding import PartitionSpec as P

HEAD_DIM = 64
norm_eps = 1e-06
masked_score = -1e30
AXES = ("dp", "tensor")
LOW = jnp.bfloat16
F32 = jnp.float32
TILE = 128
Y_BIT, CORE_BIT, X_BIT, Z_SHIFT = 1, 2, 4, 3
ANY = pl.BlockSpec(memory_space=pltpu.HBM)


def mm(left, right):
    return lax.dot_general(left, right, (((1,), (0,)), ((), ())), preferred_element_type=F32)


def mm_nt(left, right):
    return lax.dot_general(left, right, (((1,), (1,)), ((), ())), preferred_element_type=F32)


def mm_tn(left, right):
    return lax.dot_general(left, right, (((0,), (0,)), ((), ())), preferred_element_type=F32)


def whole(*shape):
    return pl.BlockSpec(shape, lambda t, me: (0,) * len(shape))


def call(body, grid, ins, outs, shapes, scratch, flops, moved, name, room=32):
    return pl.pallas_call(
        body,
        grid_spec=pltpu.PrefetchScalarGridSpec(
            num_scalar_prefetch=1,
            grid=grid,
            in_specs=ins,
            out_specs=outs,
            scratch_shapes=scratch,
        ),
        out_shape=shapes,
        compiler_params=pltpu.CompilerParams(
            dimension_semantics=("arbitrary",) * len(grid), vmem_limit_bytes=room << 20
        ),
        cost_estimate=pl.CostEstimate(flops=1, bytes_accessed=1, transcendentals=0),
        name=name,
    )


def places(me, core_flip, first, second):
    owner = ((me >> 1) & 1) ^ core_flip
    off_y = jnp.where(owner == 0, first, second)
    off_x = jnp.where(owner == 0, second, first)
    return off_y, off_x


def dp_of(me, core_flip, off_x, off_z):
    core = ((me >> 1) & 1) ^ core_flip
    return (((me >> Z_SHIFT) ^ off_z) << 2) | ((((me >> 2) & 1) ^ off_x) << 1) | core


def fetch(me, pieces, store, sems, start, width):
    for index, piece in enumerate(pieces):
        core_flip, first, second = index >> 2, (index >> 1) & 1, index & 1
        off_y, off_x = places(me, core_flip, first, second)
        y_at = (me & 1) ^ off_y
        depth, rows, _ = piece.shape
        for off_z in range(depth):
            row = pl.multiple_of(dp_of(me, core_flip, off_x, off_z) * rows, rows)
            pltpu.make_async_copy(
                piece.at[off_z, :, pl.ds(start, width)],
                store.at[y_at, pl.ds(row, rows), :],
                sems.at[y_at],
            ).start()


def arrived(store, sems, y_at):
    pltpu.make_async_copy(store.at[y_at], store.at[y_at], sems.at[y_at]).wait()


def normed(rows, gain, shift):
    center = rows - jnp.mean(rows, axis=-1, keepdims=True)
    spread = jnp.mean(center * center, axis=-1, keepdims=True)
    return center * lax.rsqrt(spread + norm_eps) * gain + shift


def qkv_call(me, rows_in, pieces):
    count, width = rows_in.shape
    half = width // 2
    span = 3 * half

    def body(me_ref, x_ref, *refs):
        parts, refs = refs[:8], refs[8:]
        norm_ref, turn_ref, out_ref, table_ref, store, sems, vectors, vector_sems = refs
        step = pl.program_id(0)

        @pl.when(step == 0)
        def _():
            fetch(me_ref[0], parts, vectors, vector_sems, span, TILE)
            fetch(me_ref[0], parts, store, sems, 0, span)
            for y_at in range(2):
                arrived(vectors, vector_sems, y_at)
            table_ref[...] = vectors[0].astype(F32).T[: table_ref.shape[0]]

            @pl.loop(0, count // TILE)
            def _(i):
                at = pl.ds(pl.multiple_of(i * TILE, TILE), TILE)
                value = normed(x_ref[at, :], table_ref[0:1, :], table_ref[1:2, :])
                norm_ref[at, :] = value.astype(LOW)
                turn_ref[:, at] = value.T.astype(LOW)

        for y_at in range(2):

            @pl.when(step == 3 * y_at)
            def _():
                arrived(store, sems, y_at)

        y_at, kind = step // 3, step % 3
        col = pl.multiple_of(kind * half, half)
        own = pl.ds(pl.multiple_of(y_at * half, half), half)
        product = mm(norm_ref[...], store[y_at, :, pl.ds(col, half)])
        bias = jnp.where(kind == 0, table_ref[2:3, own], table_ref[3:4, own])
        bias = jnp.where(kind == 1, 0.0, bias)
        out_ref[...] = (product + bias).astype(LOW)

    return call(
        body,
        (6,),
        [whole(count, width)] + [ANY] * 8,
        [
            whole(count, width),
            whole(width, count),
            pl.BlockSpec((count, half), lambda t, me: (0, t)),
            whole(16, width),
        ],
        [
            jax.ShapeDtypeStruct((count, width), LOW),
            jax.ShapeDtypeStruct((width, count), LOW),
            jax.ShapeDtypeStruct((count, 2 * span), LOW),
            jax.ShapeDtypeStruct((16, width), F32),
        ],
        [
            pltpu.VMEM((2, width, span), LOW),
            pltpu.SemaphoreType.DMA((2,)),
            pltpu.VMEM((2, width, TILE), LOW),
            pltpu.SemaphoreType.DMA((2,)),
        ],
        2 * count * width * 2 * span,
        count * width * 16 + width * span * 4,
        "qkv",
        60,
    )(me, rows_in, *pieces)


def head_halves(shape):
    lane = lax.broadcasted_iota(jnp.int32, shape, 1)
    return lane < HEAD_DIM, lane >= HEAD_DIM


def attend_call(me, qkv, visible):
    images, _, seq = visible.shape
    count, full = qkv.shape
    half = full // 6

    def body(me_ref, qkv_ref, seen_ref, out_ref):
        seen = seen_ref[0] > 0

        @pl.loop(0, half // (2 * TILE))
        def _(pair):
            for part in range(2):
                col = pl.multiple_of((2 * pair + part) * TILE, TILE)
                query = qkv_ref[:, pl.ds(col, TILE)] * jnp.asarray(HEAD_DIM**-0.5, LOW)
                key = qkv_ref[:, pl.ds(half + col, TILE)]
                value = qkv_ref[:, pl.ds(2 * half + col, TILE)]
                lanes = head_halves(query.shape)
                mixed = []
                for keep in lanes:
                    scores = jnp.where(seen, mm_nt(jnp.where(keep, query, 0), key), masked_score)
                    exps = jnp.exp(scores - jnp.max(scores, axis=-1, keepdims=True))
                    total = jnp.sum(exps, axis=-1, keepdims=True)
                    mixed.append(mm(exps.astype(LOW), value) * (1.0 / total))
                out_ref[:, pl.ds(col, TILE)] = jnp.where(lanes[0], mixed[0], mixed[1]).astype(LOW)

    return call(
        body,
        (images, 2),
        [
            pl.BlockSpec((seq, 3 * half), lambda i, y, me: (i, y)),
            pl.BlockSpec((1, 1, seq), lambda i, y, me: (i, 0, 0)),
        ],
        pl.BlockSpec((seq, half), lambda i, y, me: (i, y)),
        jax.ShapeDtypeStruct((count, 2 * half), LOW),
        [],
        4 * count * seq * 2 * half * 4,
        count * full * 3,
        "attend",
    )(me, qkv, visible)


def project_call(me, mixed, rows_in, table, pieces):
    count, width = rows_in.shape
    half = width // 2

    def body(me_ref, mixed_ref, x_ref, table_ref, *refs):
        parts, (mid_ref, norm_ref, turn_ref, store, sems) = refs[:8], refs[8:]
        fetch(me_ref[0], parts, store, sems, 2 * width, half)
        arrived(store, sems, 0)
        mid_ref[...] = mm_nt(mixed_ref[:, :half], store[0])
        arrived(store, sems, 1)
        mid_ref[...] += mm_nt(mixed_ref[:, half:], store[1])

        @pl.loop(0, count // TILE)
        def _(i):
            at = pl.ds(pl.multiple_of(i * TILE, TILE), TILE)
            middle = x_ref[at, :] + (mid_ref[at, :] + table_ref[4:5, :])
            mid_ref[at, :] = middle
            value = normed(middle, table_ref[5:6, :], table_ref[6:7, :])
            norm_ref[at, :] = value.astype(LOW)
            turn_ref[:, at] = value.T.astype(LOW)

    return call(
        body,
        (1,),
        [whole(count, width), whole(count, width), whole(*table.shape)] + [ANY] * 8,
        [whole(count, width), whole(count, width), whole(width, count)],
        [
            jax.ShapeDtypeStruct((count, width), F32),
            jax.ShapeDtypeStruct((count, width), LOW),
            jax.ShapeDtypeStruct((width, count), LOW),
        ],
        [pltpu.VMEM((2, width, half), LOW), pltpu.SemaphoreType.DMA((2,))],
        2 * count * width * width,
        count * width * 14 + width * width * 2,
        "project",
    )(me, mixed, rows_in, table, *pieces)


def expand_call(me, normed_two, bias, pieces):
    count, width = normed_two.shape
    span = bias.shape[1] // 2
    chunk = span // 4

    def body(me_ref, norm_ref, bias_ref, *refs):
        parts, (hid_ref, slope_ref, store, sems) = refs[:8], refs[8:]
        step = pl.program_id(0)

        @pl.when(step == 0)
        def _():
            fetch(me_ref[0], parts, store, sems, 0, span)

        for y_at in range(2):

            @pl.when(step == 4 * y_at)
            def _():
                arrived(store, sems, y_at)

        y_at, col = step // 4, pl.multiple_of(step % 4 * chunk, chunk)
        pre = mm(norm_ref[...], store[y_at, :, pl.ds(col, chunk)]) + bias_ref[...]
        below = 0.5 + 0.5 * lax.erf(pre * 0.5**0.5)
        hid_ref[...] = (pre * below).astype(LOW)
        slope_ref[...] = (below + pre * jnp.exp(pre * pre * -0.5) * 0.3989422804014327).astype(LOW)

    out = pl.BlockSpec((count, chunk), lambda t, me: (0, t))
    return call(
        body,
        (8,),
        [whole(count, width), pl.BlockSpec((1, chunk), lambda t, me: (0, t))] + [ANY] * 8,
        [out, out],
        [jax.ShapeDtypeStruct((count, 2 * span), LOW)] * 2,
        [pltpu.VMEM((2, width, span), LOW), pltpu.SemaphoreType.DMA((2,))],
        2 * count * width * 2 * span,
        count * span * 8 + width * span * 4,
        "expand",
    )(me, normed_two, bias, *pieces)


def contract_call(me, hidden, slope, out_low, middle, table, pieces):
    count, width = middle.shape
    span = hidden.shape[1] // 2
    chunk = span // 4

    def body(me_ref, hid_ref, slope_ref, low_ref, mid_ref, table_ref, *refs):
        parts, (act_ref, pre_ref, sum_ref, store, sems) = refs[:8], refs[8:]
        step = pl.program_id(0)

        @pl.when(step == 0)
        def _():
            fetch(me_ref[0], parts, store, sems, 0, span)
            act_ref[...] = mid_ref[...] + table_ref[7:8, :]

        for y_at in range(2):

            @pl.when(step == 4 * y_at)
            def _():
                arrived(store, sems, y_at)

        y_at, col = step // 4, pl.multiple_of(step % 4 * chunk, chunk)
        weight = store[y_at, :, pl.ds(col, chunk)]
        act_ref[...] += mm_nt(hid_ref[...], weight)
        pre = mm(low_ref[...], weight) * slope_ref[...].astype(F32)
        pre_ref[...] = pre.astype(LOW)
        sum_ref[...] = jnp.sum(pre, axis=0, keepdims=True)

    part = pl.BlockSpec((count, chunk), lambda t, me: (0, t))
    return call(
        body,
        (8,),
        [part, part, whole(count, width), whole(count, width), whole(*table.shape)] + [ANY] * 8,
        [whole(count, width), part, pl.BlockSpec((1, chunk), lambda t, me: (0, t))],
        [
            jax.ShapeDtypeStruct((count, width), F32),
            jax.ShapeDtypeStruct((count, 2 * span), LOW),
            jax.ShapeDtypeStruct((1, 2 * span), F32),
        ],
        [pltpu.VMEM((2, width, span), LOW), pltpu.SemaphoreType.DMA((2,))],
        4 * count * width * 2 * span,
        count * span * 12 + width * span * 4,
        "contract",
    )(me, hidden, slope, out_low, middle, table, *pieces)


def norm_back_call(me, low, start, gain_row, rows_in, base, table, pieces, keep_low, name):
    count, width = rows_in.shape
    span = low.shape[1] // 2
    chunk = span // 2

    def body(me_ref, low_ref, x_ref, base_ref, table_ref, *refs):
        parts, outs = refs[:8], refs[8:]
        if keep_low:
            grad_ref, vec_ref, out_low_ref, turn_ref, store, sems = outs
        else:
            grad_ref, vec_ref, store, sems = outs
        step = pl.program_id(0)

        @pl.when(step == 0)
        def _():
            fetch(me_ref[0], parts, store, sems, start, span)

        for y_at in range(2):

            @pl.when(step == 2 * y_at)
            def _():
                arrived(store, sems, y_at)

        y_at, col = step // 2, pl.multiple_of(step % 2 * chunk, chunk)
        product = mm_nt(low_ref[...], store[y_at, :, pl.ds(col, chunk)])

        @pl.when(step == 0)
        def _():
            grad_ref[...] = product

        @pl.when(step > 0)
        def _():
            grad_ref[...] += product

        @pl.when(step == 3)
        def _():
            vec_ref[...] = jnp.zeros_like(vec_ref)

            @pl.loop(0, count // TILE)
            def _(i):
                at = pl.ds(pl.multiple_of(i * TILE, TILE), TILE)
                back = grad_ref[at, :]
                rows = x_ref[at, :]
                center = rows - jnp.mean(rows, axis=-1, keepdims=True)
                spread = jnp.mean(center * center, axis=-1, keepdims=True)
                scale = lax.rsqrt(spread + norm_eps)
                unit = center * scale
                inner = back * table_ref[gain_row : gain_row + 1, :]
                along = jnp.mean(inner * unit, axis=-1, keepdims=True)
                level = jnp.mean(inner, axis=-1, keepdims=True)
                grad = base_ref[at, :] + scale * (inner - level - unit * along)
                grad_ref[at, :] = grad
                vec_ref[0:1, :] += jnp.sum(back * unit, axis=0, keepdims=True)
                vec_ref[1:2, :] += jnp.sum(back, axis=0, keepdims=True)
                vec_ref[2:3, :] += jnp.sum(grad, axis=0, keepdims=True)
                if keep_low:
                    out_low_ref[at, :] = grad.astype(LOW)
                    turn_ref[:, at] = grad.T.astype(LOW)

    outs = [whole(count, width), whole(8, width)]
    shapes = [jax.ShapeDtypeStruct((count, width), F32), jax.ShapeDtypeStruct((8, width), F32)]
    if keep_low:
        outs += [whole(count, width), whole(width, count)]
        shapes += [
            jax.ShapeDtypeStruct((count, width), LOW),
            jax.ShapeDtypeStruct((width, count), LOW),
        ]
    return call(
        body,
        (4,),
        [
            pl.BlockSpec((count, chunk), lambda t, me: (0, t)),
            whole(count, width),
            whole(count, width),
            whole(*table.shape),
        ]
        + [ANY] * 8,
        outs,
        shapes,
        [pltpu.VMEM((2, width, span), LOW), pltpu.SemaphoreType.DMA((2,))],
        2 * count * width * 2 * span,
        count * width * 16 + width * span * 4 + count * span * 4,
        name,
        32 if keep_low else 60,
    )(me, low, rows_in, base, table, *pieces)


def mixed_back_call(me, middle_low, pieces):
    count, width = middle_low.shape
    half = width // 2

    def body(me_ref, low_ref, *refs):
        parts, (out_ref, store, sems) = refs[:8], refs[8:]
        step = pl.program_id(0)

        @pl.when(step == 0)
        def _():
            fetch(me_ref[0], parts, store, sems, 2 * width, half)

        for y_at in range(2):

            @pl.when(step == y_at)
            def _():
                arrived(store, sems, y_at)

        out_ref[...] = mm(low_ref[...], store[step]).astype(LOW)

    return call(
        body,
        (2,),
        [whole(count, width)] + [ANY] * 8,
        pl.BlockSpec((count, half), lambda t, me: (0, t)),
        jax.ShapeDtypeStruct((count, width), LOW),
        [pltpu.VMEM((2, width, half), LOW), pltpu.SemaphoreType.DMA((2,))],
        2 * count * width * width,
        count * width * 4 + width * width * 2,
        "mixed_back",
    )(me, middle_low, *pieces)


def attend_back_call(me, qkv, grads, visible):
    images, seq, _ = visible.shape
    count, full = qkv.shape
    half = full // 6
    scale = HEAD_DIM**-0.5

    def body(me_ref, qkv_ref, grad_ref, seen_ref, out_ref, sum_ref):
        seen = seen_ref[0] > 0
        @pl.loop(0, half // (2 * TILE))
        def _(pair):
            for part in range(2):
                col = pl.multiple_of((2 * pair + part) * TILE, TILE)
                query = qkv_ref[:, pl.ds(col, TILE)] * jnp.asarray(scale, LOW)
                key = qkv_ref[:, pl.ds(half + col, TILE)]
                value = qkv_ref[:, pl.ds(2 * half + col, TILE)]
                grad = grad_ref[:, pl.ds(col, TILE)]
                lanes = head_halves(query.shape)
                parts = []
                for keep in lanes:
                    scores = jnp.where(seen, mm_nt(jnp.where(keep, key, 0), query), masked_score)
                    exps = jnp.exp(scores - jnp.max(scores, axis=0, keepdims=True))
                    probs = exps * (1.0 / jnp.sum(exps, axis=0, keepdims=True))
                    prob_grad = mm_nt(jnp.where(keep, value, 0), grad)
                    row_dot = jnp.sum(probs * prob_grad, axis=0, keepdims=True)
                    score_grad = (probs * (prob_grad - row_dot)).astype(LOW)
                    parts.append(
                        (
                            mm_tn(key, score_grad).T * scale,
                            mm(score_grad, query),
                            mm(probs.astype(LOW), grad),
                        )
                    )
                for at in range(3):
                    merged = jnp.where(lanes[0], parts[0][at], parts[1][at])
                    put = at * half + col
                    out_ref[:, pl.ds(put, TILE)] = merged.astype(LOW)
                    sum_ref[0, 0, :, pl.ds(put, TILE)] = jnp.sum(merged, axis=0, keepdims=True)

    return call(
        body,
        (images, 2),
        [
            pl.BlockSpec((seq, 3 * half), lambda i, y, me: (i, y)),
            pl.BlockSpec((seq, half), lambda i, y, me: (i, y)),
            pl.BlockSpec((1, seq, 1), lambda i, y, me: (i, 0, 0)),
        ],
        [
            pl.BlockSpec((seq, 3 * half), lambda i, y, me: (i, y)),
            pl.BlockSpec((1, 1, 1, 3 * half), lambda i, y, me: (i, y, 0, 0)),
        ],
        [
            jax.ShapeDtypeStruct((count, full), LOW),
            jax.ShapeDtypeStruct((images, 2, 1, 3 * half), F32),
        ],
        [],
        10 * count * seq * 2 * half * 4,
        count * full * 5,
        "attend_back",
    )(me, qkv, grads, visible)


def weight_grad_call(me, turned, right, depth, core_flip, received, name):
    width, count = turned.shape
    span = right.shape[1] // 2
    chunk = next(c for c in (1024, 768, 512, 384, 256, 128) if span % c == 0)
    parts = span // chunk
    steps = 2 * parts
    rows = width // (4 * depth)
    quarter = width // 4

    def body(me_ref, turn_ref, right_ref, *refs):
        if core_flip:
            (far_ref, lefts, ready, sems) = refs
        else:
            (got_ref, kept_ref, sent_ref, lefts, ready, sems, got, got_sems) = refs
        step = pl.program_id(0)
        slot = step % 2
        owner = ((me_ref[0] >> 1) & 1) ^ core_flip

        def spot(off_y, off_x):
            return jnp.where(owner == 0, off_y, off_x), jnp.where(owner == 0, off_x, off_y)

        def fetched(at, off_x):
            first, second = spot(1 - at // parts, off_x)
            col = pl.multiple_of(at % parts * chunk, chunk)
            return pltpu.make_async_copy(
                got_ref.at[first, second, :, :, pl.ds(col, chunk)],
                got.at[at, off_x],
                got_sems.at[at, off_x],
            )

        def leaving(target, at, off_x):
            col = pl.multiple_of(at % parts * chunk, chunk)
            return pltpu.make_async_copy(
                ready.at[at % 2, off_x],
                target.at[:, :, pl.ds(col, chunk)],
                sems.at[at % 2, off_x],
            )

        @pl.when(step == 0)
        def _():
            if not core_flip:
                for at in range(steps):
                    for off_x in range(2):
                        fetched(at, off_x).start()
            for off_x in range(2):
                for off_z in range(depth):
                    row = pl.multiple_of(dp_of(me_ref[0], core_flip, off_x, off_z) * rows, rows)
                    put = off_x * quarter + off_z * rows
                    lefts[put : put + rows, :] = turn_ref[pl.ds(row, rows), :]

        product = mm(lefts[...], right_ref[...]).reshape(2, depth, rows, chunk)

        @pl.when(step >= 2)
        def _():
            for off_x in range(2):
                some = far_ref.at[0, 0] if core_flip else kept_ref.at[0]
                leaving(some, step, off_x).wait()

        for off_x in range(2):
            total = product[off_x]
            if not core_flip:
                fetched(step, off_x).wait()
                total = total + got[step, off_x].astype(F32)
            ready[slot, off_x] = total.astype(LOW)
            first, second = spot(1 - step // parts, off_x)
            if core_flip:
                leaving(far_ref.at[first, second], step, off_x).start()
            else:
                for at, target in enumerate((kept_ref, sent_ref)):

                    @pl.when(first == at)
                    def _():
                        leaving(target.at[second], step, off_x).start()

        @pl.when(step == steps - 1)
        def _():
            for back in range(min(2, steps)):
                for off_x in range(2):
                    some = far_ref.at[0, 0] if core_flip else kept_ref.at[0]
                    leaving(some, step - back, off_x).wait()

    def right_at(t, me):
        return 0, ((me[0] & 1) ^ (1 - t // parts)) * parts + t % parts

    ins = [whole(width, count), pl.BlockSpec((count, chunk), right_at)]
    scratch = [
        pltpu.VMEM((2 * quarter, count), LOW),
        pltpu.VMEM((2, 2, depth, rows, chunk), LOW),
        pltpu.SemaphoreType.DMA((2, 2)),
    ]
    if core_flip:
        outs = ANY
        shapes = jax.ShapeDtypeStruct((2, 2, depth, rows, span), LOW)
        extra = ()
    else:
        ins = ins + [ANY]
        outs = [ANY, ANY]
        shapes = [jax.ShapeDtypeStruct((2, depth, rows, span), LOW)] * 2
        extra = (received,)
        scratch += [
            pltpu.VMEM((steps, 2, depth, rows, chunk), LOW),
            pltpu.SemaphoreType.DMA((steps, 2)),
        ]
    return call(
        body,
        (steps,),
        ins,
        outs,
        shapes,
        scratch,
        2 * count * width * span,
        count * (width + span * 2) * 2 + width * span * 4,
        name,
    )(me, turned, right, *extra)


def swap(value, size, bits, other=None):
    other = bits if other is None else other
    return lax.ppermute(
        value, AXES, [(i, i ^ (other if i & CORE_BIT else bits)) for i in range(size)]
    )


def after(value, *others):
    return lax.optimization_barrier((value, *others))[0]


def along_depth(piece, size, steps):
    return [piece] + [swap(piece, size, k << Z_SHIFT) for k in steps]


def along_first(value, size):
    return swap(value, size, Y_BIT, X_BIT)


def along_second(value, size):
    return swap(value, size, X_BIT, Y_BIT)


def along_core(value, size):
    return swap(value, size, CORE_BIT)


class Scatter:
    def __init__(self, turned, right, size, depth, name):
        self.size, self.depth, self.name = size, depth, name
        self.turned, self.right = turned, right

    def far(self, me):
        self.me = me
        self.sent = weight_grad_call(
            me, self.turned, self.right, self.depth, 1, None, self.name + "_far"
        )
        self.received = swap(self.sent, self.size, CORE_BIT)
        return self.sent

    def near(self, *others):
        right = after(self.right, *others)
        self.kept, self.sent = weight_grad_call(
            self.me, self.turned, right, self.depth, 0, self.received, self.name + "_near"
        )
        self.received = swap(self.sent, self.size, Y_BIT, X_BIT)
        return self.kept

    def second(self, *others):
        kept = after(self.kept, *others)
        total = (kept.astype(F32) + self.received.astype(F32)).astype(LOW)
        self.kept = total[0]
        self.received = swap(total[1], self.size, X_BIT, Y_BIT)
        return self.kept

    def third(self, *others):
        kept = after(self.kept, *others)
        total = (kept.astype(F32) + self.received.astype(F32)).astype(LOW)
        self.kept = total[0]
        self.received = [
            swap(total[k], self.size, k << Z_SHIFT) for k in range(1, self.depth)
        ]
        return self.kept

    def last(self, *others):
        result = after(self.kept, *others).astype(F32)
        for value in self.received:
            result = result + value.astype(F32)
        return result


def shards(
    inputs,
    key_mask,
    ln1_gain,
    ln1_bias,
    w_qkv,
    qv_bias,
    w_proj,
    proj_bias,
    ln2_gain,
    ln2_bias,
    w_fc1,
    fc1_bias,
    w_fc2,
    fc2_bias,
    out_grad,
):
    tensor_rank = lax.axis_index("tensor")
    dp_rank = lax.axis_index("dp")
    dp_size = lax.axis_size("dp")
    size = 2 * dp_size
    depth = dp_size // 4
    own_images, seq, width = inputs.shape
    count = own_images * seq
    half = w_qkv.shape[2]
    rows = ln1_gain.shape[0]
    me = jnp.reshape(dp_rank * 2 + tensor_rank, (1,)).astype(jnp.int32)

    vectors = jnp.concatenate(
        [
            jnp.stack([ln1_gain, ln1_bias, qv_bias[0], qv_bias[1]]),
            jnp.stack([proj_bias, ln2_gain, ln2_bias, fc2_bias]),
            fc1_bias.reshape(4, rows),
        ]
    )
    vectors = jnp.pad(vectors, ((0, TILE - vectors.shape[0]), (0, 0))).T
    piece_one = jnp.concatenate([w_qkv[0], w_qkv[1], w_qkv[2], vectors], axis=1).astype(LOW)
    piece_two = jnp.concatenate([w_fc1, w_proj.T], axis=1).astype(LOW)
    piece_three = w_fc2.T.astype(LOW)

    held_one = jnp.stack(along_depth(piece_one, size, range(1, depth)))
    grad_in = out_grad.reshape(count, width)
    out_low = grad_in.astype(LOW)
    out_turned = out_low.T
    held_one, piece_two, out_low, out_turned = lax.optimization_barrier(
        (held_one, piece_two, out_low, out_turned)
    )
    first_one = along_first(held_one, size)
    second_one = along_second(held_one, size)
    far_one = [along_core(held_one, size)]
    deep_two = along_depth(piece_two, size, range(1, depth - 1))
    first_one, second_one, far_own, *deep_two = lax.optimization_barrier(
        (first_one, second_one, *far_one, *deep_two)
    )
    both_one = along_second(first_one, size)
    far_one = [far_own, along_core(second_one, size), along_core(first_one, size)]
    plane_one = [held_one, second_one, first_one]
    deep_two += along_depth(deep_two[0], size, [depth - 1])[1:]
    far_one += [along_core(both_one, size)]
    both_one, piece_three, *deep_two = lax.optimization_barrier((both_one, piece_three, *deep_two))
    pieces_one = plane_one + [both_one] + far_one
    held_two = jnp.stack(deep_two)
    first_two = along_first(held_two, size)
    second_two = along_second(held_two, size)
    far_two = [along_core(held_two, size)]
    deep_three = along_depth(piece_three, size, range(1, depth - 1))

    rows_in = inputs.reshape(count, width)
    own_mask = lax.dynamic_slice_in_dim(key_mask, tensor_rank * own_images, own_images, 0)
    visible = jnp.concatenate(
        [jnp.ones((own_images, seq - key_mask.shape[1]), jnp.int32), own_mask], axis=1
    )
    visible_rows = after(visible, held_one)[:, :, None]
    visible = visible[:, None, :]

    normed_one, turned_one, qkv, table = qkv_call(me, rows_in, pieces_one)
    fc1_full = table[8:12].reshape(4, dp_size, rows).transpose(1, 0, 2).reshape(1, 4 * width)
    mixed = attend_call(me, qkv, visible)
    mixed, fc1_full, first_two, second_two, *deep_three, far_own = lax.optimization_barrier(
        (mixed, fc1_full, first_two, second_two, *deep_three, *far_two)
    )
    both_two = along_second(first_two, size)
    far_two = [far_own, along_core(second_two, size), along_core(first_two, size)]
    plane_two = [held_two, second_two, first_two]
    deep_three += along_depth(deep_three[0], size, [depth - 1])[1:]
    far_two += [along_core(both_two, size)]
    both_two, *deep_three = lax.optimization_barrier((both_two, *deep_three))
    pieces_two = plane_two + [both_two] + far_two
    held_three = jnp.stack(deep_three)
    first_three = along_first(held_three, size)
    second_three = along_second(held_three, size)
    far_three = [along_core(held_three, size)]
    middle, normed_two, turned_two = project_call(me, mixed, rows_in, table, pieces_two)
    normed_two, first_three, second_three, far_own = lax.optimization_barrier(
        (normed_two, first_three, second_three, *far_three)
    )
    both_three = along_second(first_three, size)
    far_three = [far_own, along_core(second_three, size), along_core(first_three, size)]
    plane_three = [held_three, second_three, first_three]
    hidden, slope = expand_call(me, normed_two, fc1_full, pieces_two)
    hidden, both_three = lax.optimization_barrier((hidden, both_three))
    pieces_three = plane_three + [both_three] + far_three + [along_core(both_three, size)]
    fc2 = Scatter(out_turned, hidden, size, depth, "fc2_grad")
    done = fc2.far(me)
    outputs, pre_low, fc1_sum = contract_call(
        me, after(hidden, done), slope, out_low, middle, table, pieces_three
    )
    done = fc2.near(pre_low)
    middle_grad, vec_two, middle_low, turned_mid = norm_back_call(
        me, after(pre_low, done), 0, 5, middle, grad_in, table, pieces_two, True, "norm_two_back"
    )
    fc1 = Scatter(turned_two, after(pre_low, middle_low), size, depth, "fc1_grad")
    done = fc1.far(me)
    done = fc2.second(done)
    mixed_grad = mixed_back_call(me, after(middle_low, done), pieces_two)
    proj = Scatter(turned_mid, after(mixed, mixed_grad), size, depth, "proj_grad")
    done = proj.far(me)
    done = fc2.third(done)
    done = fc1.near(done)
    qkv_low, qkv_sum = attend_back_call(me, qkv, after(mixed_grad, done), visible_rows)
    fc2_grad = fc2.last(qkv_low)
    done = fc1.second(fc2_grad)
    done = proj.near(done)
    qkv_out = Scatter(turned_one, after(qkv_low, done), size, depth, "qkv_grad")
    done = qkv_out.far(me)
    done = qkv_out.near(done)
    done = fc1.third(proj.second(done))
    input_grad, vec_one = norm_back_call(
        me,
        after(qkv_low, done),
        0,
        0,
        rows_in,
        middle_grad,
        table,
        pieces_one,
        False,
        "norm_one_back",
    )

    qkv_sum = jnp.sum(qkv_sum, axis=(0, 2)).reshape(2, 3, half)
    sums = jnp.concatenate(
        [
            vec_one[:2],
            qkv_sum[:, 0].reshape(1, width),
            qkv_sum[:, 2].reshape(1, width),
            vec_two[2:3],
            vec_two[:2],
            jnp.sum(grad_in, axis=0, keepdims=True),
            fc1_sum.reshape(4, width),
        ]
    )
    fc1_grad = fc1.last(input_grad)
    done = qkv_out.second(fc1_grad)
    done = proj.third(done)
    sums = after(sums, done)
    for bits in (CORE_BIT, X_BIT, Y_BIT):
        sums = sums + swap(sums, size, bits)
    done = qkv_out.third(sums)
    proj_grad = proj.last(done)
    sums = sum(along_depth(after(sums, qkv_out.received[0]), size, range(1, depth)))
    qkv_grad = qkv_out.last()
    mine = lax.dynamic_slice_in_dim(sums[:8], dp_rank * rows, rows, 1)
    fc1_mine = lax.dynamic_slice_in_dim(sums[8:].reshape(-1), dp_rank * 4 * rows, 4 * rows, 0)
    return (
        outputs.reshape(inputs.shape),
        input_grad.reshape(inputs.shape),
        mine[0],
        mine[1],
        qkv_grad.reshape(rows, 3, half).transpose(1, 0, 2),
        mine[2:4],
        proj_grad.T,
        mine[4],
        mine[5],
        mine[6],
        fc1_grad,
        fc1_mine,
        fc2_grad.T,
        mine[7],
    )


def solution(mesh):
    placed = (
        P(("dp", "tensor"), None, None),
        P("dp", None),
        P("dp"),
        P("dp"),
        P(None, "dp", "tensor"),
        P(None, "dp"),
        P("tensor", "dp"),
        P("dp"),
        P("dp"),
        P("dp"),
        P("dp", "tensor"),
        P("dp"),
        P("tensor", "dp"),
        P("dp"),
        P(("dp", "tensor"), None, None),
    )
    return jax.shard_map(
        shards,
        mesh=mesh,
        in_specs=placed,
        out_specs=(
            P(("dp", "tensor"), None, None),
            P(("dp", "tensor"), None, None),
            P("dp"),
            P("dp"),
            P(None, "dp", "tensor"),
            P(None, "dp"),
            P("tensor", "dp"),
            P("dp"),
            P("dp"),
            P("dp"),
            P("dp", "tensor"),
            P("dp"),
            P("tensor", "dp"),
            P("dp"),
        ),
        check_vma=False,
    )
```

```python
import jax
import jax.numpy as jnp
from jax import lax
from jax.experimental import pallas as pl
from jax.experimental.pallas import tpu as pltpu
from jax.sharding import PartitionSpec as P

HEAD_DIM = 64
norm_eps = 1e-06
masked_score = -1e30
AXES = ("dp", "tensor")
LOW = jnp.bfloat16
F32 = jnp.float32
TILE = 128
Y_BIT, CORE_BIT, X_BIT, Z_SHIFT = 1, 2, 4, 3
ANY = pl.BlockSpec(memory_space=pltpu.HBM)


def mm(left, right):
    return lax.dot_general(left, right, (((1,), (0,)), ((), ())), preferred_element_type=F32)


def mm_nt(left, right):
    return lax.dot_general(left, right, (((1,), (1,)), ((), ())), preferred_element_type=F32)


def mm_tn(left, right):
    return lax.dot_general(left, right, (((0,), (0,)), ((), ())), preferred_element_type=F32)


def whole(*shape):
    return pl.BlockSpec(shape, lambda t, me: (0,) * len(shape))


def call(body, grid, ins, outs, shapes, scratch, flops, moved, name, room=32):
    return pl.pallas_call(
        body,
        grid_spec=pltpu.PrefetchScalarGridSpec(
            num_scalar_prefetch=1,
            grid=grid,
            in_specs=ins,
            out_specs=outs,
            scratch_shapes=scratch,
        ),
        out_shape=shapes,
        compiler_params=pltpu.CompilerParams(
            dimension_semantics=("arbitrary",) * len(grid), vmem_limit_bytes=room << 20
        ),
        cost_estimate=pl.CostEstimate(flops=1, bytes_accessed=1, transcendentals=0),
        name=name,
    )


def places(me, core_flip, first, second):
    owner = ((me >> 1) & 1) ^ core_flip
    off_y = jnp.where(owner == 0, first, second)
    off_x = jnp.where(owner == 0, second, first)
    return off_y, off_x


def dp_of(me, core_flip, off_x, off_z):
    core = ((me >> 1) & 1) ^ core_flip
    return (((me >> Z_SHIFT) ^ off_z) << 2) | ((((me >> 2) & 1) ^ off_x) << 1) | core


def fetch(me, pieces, store, sems, start, width):
    for index, piece in enumerate(pieces):
        core_flip, first, second = index >> 2, (index >> 1) & 1, index & 1
        off_y, off_x = places(me, core_flip, first, second)
        y_at = (me & 1) ^ off_y
        depth, rows, _ = piece.shape
        for off_z in range(depth):
            row = pl.multiple_of(dp_of(me, core_flip, off_x, off_z) * rows, rows)
            pltpu.make_async_copy(
                piece.at[off_z, :, pl.ds(start, width)],
                store.at[y_at, pl.ds(row, rows), :],
                sems.at[y_at],
            ).start()


def arrived(store, sems, y_at):
    pltpu.make_async_copy(store.at[y_at], store.at[y_at], sems.at[y_at]).wait()


def normed(rows, gain, shift):
    center = rows - jnp.mean(rows, axis=-1, keepdims=True)
    spread = jnp.mean(center * center, axis=-1, keepdims=True)
    return center * lax.rsqrt(spread + norm_eps) * gain + shift


def qkv_call(me, rows_in, pieces):
    count, width = rows_in.shape
    half = width // 2
    span = 3 * half

    def body(me_ref, x_ref, *refs):
        parts, refs = refs[:8], refs[8:]
        norm_ref, turn_ref, out_ref, table_ref, store, sems, vectors, vector_sems = refs
        step = pl.program_id(0)

        @pl.when(step == 0)
        def _():
            fetch(me_ref[0], parts, vectors, vector_sems, span, TILE)
            fetch(me_ref[0], parts, store, sems, 0, span)
            for y_at in range(2):
                arrived(vectors, vector_sems, y_at)
            table_ref[...] = vectors[0].astype(F32).T[: table_ref.shape[0]]

            @pl.loop(0, count // TILE)
            def _(i):
                at = pl.ds(pl.multiple_of(i * TILE, TILE), TILE)
                value = normed(x_ref[at, :], table_ref[0:1, :], table_ref[1:2, :])
                norm_ref[at, :] = value.astype(LOW)
                turn_ref[:, at] = value.T.astype(LOW)

        for y_at in range(2):

            @pl.when(step == 3 * y_at)
            def _():
                arrived(store, sems, y_at)

        y_at, kind = step // 3, step % 3
        col = pl.multiple_of(kind * half, half)
        own = pl.ds(pl.multiple_of(y_at * half, half), half)
        product = mm(norm_ref[...], store[y_at, :, pl.ds(col, half)])
        bias = jnp.where(kind == 0, table_ref[2:3, own], table_ref[3:4, own])
        bias = jnp.where(kind == 1, 0.0, bias)
        out_ref[...] = (product + bias).astype(LOW)

    return call(
        body,
        (6,),
        [whole(count, width)] + [ANY] * 8,
        [
            whole(count, width),
            whole(width, count),
            pl.BlockSpec((count, half), lambda t, me: (0, t)),
            whole(16, width),
        ],
        [
            jax.ShapeDtypeStruct((count, width), LOW),
            jax.ShapeDtypeStruct((width, count), LOW),
            jax.ShapeDtypeStruct((count, 2 * span), LOW),
            jax.ShapeDtypeStruct((16, width), F32),
        ],
        [
            pltpu.VMEM((2, width, span), LOW),
            pltpu.SemaphoreType.DMA((2,)),
            pltpu.VMEM((2, width, TILE), LOW),
            pltpu.SemaphoreType.DMA((2,)),
        ],
        2 * count * width * 2 * span,
        count * width * 16 + width * span * 4,
        "qkv",
        60,
    )(me, rows_in, *pieces)


def head_halves(shape):
    lane = lax.broadcasted_iota(jnp.int32, shape, 1)
    return lane < HEAD_DIM, lane >= HEAD_DIM


def attend_call(me, qkv, visible):
    images, _, seq = visible.shape
    count, full = qkv.shape
    half = full // 6

    def body(me_ref, qkv_ref, seen_ref, out_ref):
        seen = seen_ref[0] > 0

        @pl.loop(0, half // (2 * TILE))
        def _(pair):
            for part in range(2):
                col = pl.multiple_of((2 * pair + part) * TILE, TILE)
                query = qkv_ref[:, pl.ds(col, TILE)] * jnp.asarray(HEAD_DIM**-0.5, LOW)
                key = qkv_ref[:, pl.ds(half + col, TILE)]
                value = qkv_ref[:, pl.ds(2 * half + col, TILE)]
                lanes = head_halves(query.shape)
                mixed = []
                for keep in lanes:
                    scores = jnp.where(seen, mm_nt(jnp.where(keep, query, 0), key), masked_score)
                    exps = jnp.exp(scores - jnp.max(scores, axis=-1, keepdims=True))
                    total = jnp.sum(exps, axis=-1, keepdims=True)
                    mixed.append(mm(exps.astype(LOW), value) * (1.0 / total))
                out_ref[:, pl.ds(col, TILE)] = jnp.where(lanes[0], mixed[0], mixed[1]).astype(LOW)

    return call(
        body,
        (images, 2),
        [
            pl.BlockSpec((seq, 3 * half), lambda i, y, me: (i, y)),
            pl.BlockSpec((1, 1, seq), lambda i, y, me: (i, 0, 0)),
        ],
        pl.BlockSpec((seq, half), lambda i, y, me: (i, y)),
        jax.ShapeDtypeStruct((count, 2 * half), LOW),
        [],
        4 * count * seq * 2 * half * 4,
        count * full * 3,
        "attend",
    )(me, qkv, visible)


def project_call(me, mixed, rows_in, table, pieces):
    count, width = rows_in.shape
    half = width // 2

    def body(me_ref, mixed_ref, x_ref, table_ref, *refs):
        parts, (mid_ref, norm_ref, turn_ref, store, sems) = refs[:8], refs[8:]
        fetch(me_ref[0], parts, store, sems, 2 * width, half)
        arrived(store, sems, 0)
        mid_ref[...] = mm_nt(mixed_ref[:, :half], store[0])
        arrived(store, sems, 1)
        mid_ref[...] += mm_nt(mixed_ref[:, half:], store[1])

        @pl.loop(0, count // TILE)
        def _(i):
            at = pl.ds(pl.multiple_of(i * TILE, TILE), TILE)
            middle = x_ref[at, :] + (mid_ref[at, :] + table_ref[4:5, :])
            mid_ref[at, :] = middle
            value = normed(middle, table_ref[5:6, :], table_ref[6:7, :])
            norm_ref[at, :] = value.astype(LOW)
            turn_ref[:, at] = value.T.astype(LOW)

    return call(
        body,
        (1,),
        [whole(count, width), whole(count, width), whole(*table.shape)] + [ANY] * 8,
        [whole(count, width), whole(count, width), whole(width, count)],
        [
            jax.ShapeDtypeStruct((count, width), F32),
            jax.ShapeDtypeStruct((count, width), LOW),
            jax.ShapeDtypeStruct((width, count), LOW),
        ],
        [pltpu.VMEM((2, width, half), LOW), pltpu.SemaphoreType.DMA((2,))],
        2 * count * width * width,
        count * width * 14 + width * width * 2,
        "project",
    )(me, mixed, rows_in, table, *pieces)


def expand_call(me, normed_two, bias, pieces):
    count, width = normed_two.shape
    span = bias.shape[1] // 2
    chunk = span // 4

    def body(me_ref, norm_ref, bias_ref, *refs):
        parts, (hid_ref, slope_ref, store, sems) = refs[:8], refs[8:]
        step = pl.program_id(0)

        @pl.when(step == 0)
        def _():
            fetch(me_ref[0], parts, store, sems, 0, span)

        for y_at in range(2):

            @pl.when(step == 4 * y_at)
            def _():
                arrived(store, sems, y_at)

        y_at, col = step // 4, pl.multiple_of(step % 4 * chunk, chunk)
        pre = mm(norm_ref[...], store[y_at, :, pl.ds(col, chunk)]) + bias_ref[...]
        below = 0.5 + 0.5 * lax.erf(pre * 0.5**0.5)
        hid_ref[...] = (pre * below).astype(LOW)
        slope_ref[...] = (below + pre * jnp.exp(pre * pre * -0.5) * 0.3989422804014327).astype(LOW)

    out = pl.BlockSpec((count, chunk), lambda t, me: (0, t))
    return call(
        body,
        (8,),
        [whole(count, width), pl.BlockSpec((1, chunk), lambda t, me: (0, t))] + [ANY] * 8,
        [out, out],
        [jax.ShapeDtypeStruct((count, 2 * span), LOW)] * 2,
        [pltpu.VMEM((2, width, span), LOW), pltpu.SemaphoreType.DMA((2,))],
        2 * count * width * 2 * span,
        count * span * 8 + width * span * 4,
        "expand",
        60,
    )(me, normed_two, bias, *pieces)


def contract_call(me, hidden, slope, out_low, middle, table, pieces):
    count, width = middle.shape
    span = hidden.shape[1] // 2
    chunk = span // 4

    def body(me_ref, hid_ref, slope_ref, low_ref, mid_ref, table_ref, *refs):
        parts, (act_ref, pre_ref, sum_ref, store, sems) = refs[:8], refs[8:]
        step = pl.program_id(0)

        @pl.when(step == 0)
        def _():
            fetch(me_ref[0], parts, store, sems, 0, span)
            act_ref[...] = mid_ref[...] + table_ref[7:8, :]

        for y_at in range(2):

            @pl.when(step == 4 * y_at)
            def _():
                arrived(store, sems, y_at)

        y_at, col = step // 4, pl.multiple_of(step % 4 * chunk, chunk)
        weight = store[y_at, :, pl.ds(col, chunk)]
        act_ref[...] += mm_nt(hid_ref[...], weight)
        pre = mm(low_ref[...], weight) * slope_ref[...].astype(F32)
        pre_ref[...] = pre.astype(LOW)
        sum_ref[...] = jnp.sum(pre, axis=0, keepdims=True)

    part = pl.BlockSpec((count, chunk), lambda t, me: (0, t))
    return call(
        body,
        (8,),
        [part, part, whole(count, width), whole(count, width), whole(*table.shape)] + [ANY] * 8,
        [whole(count, width), part, pl.BlockSpec((1, chunk), lambda t, me: (0, t))],
        [
            jax.ShapeDtypeStruct((count, width), F32),
            jax.ShapeDtypeStruct((count, 2 * span), LOW),
            jax.ShapeDtypeStruct((1, 2 * span), F32),
        ],
        [pltpu.VMEM((2, width, span), LOW), pltpu.SemaphoreType.DMA((2,))],
        4 * count * width * 2 * span,
        count * span * 12 + width * span * 4,
        "contract",
    )(me, hidden, slope, out_low, middle, table, *pieces)


def norm_back_call(me, low, start, gain_row, rows_in, base, table, pieces, keep_low, name):
    count, width = rows_in.shape
    span = low.shape[1] // 2
    chunk = span // 2

    def body(me_ref, low_ref, x_ref, base_ref, table_ref, *refs):
        parts, outs = refs[:8], refs[8:]
        if keep_low:
            grad_ref, vec_ref, out_low_ref, turn_ref, store, sems = outs
        else:
            grad_ref, vec_ref, store, sems = outs
        step = pl.program_id(0)

        @pl.when(step == 0)
        def _():
            fetch(me_ref[0], parts, store, sems, start, span)

        for y_at in range(2):

            @pl.when(step == 2 * y_at)
            def _():
                arrived(store, sems, y_at)

        y_at, col = step // 2, pl.multiple_of(step % 2 * chunk, chunk)
        product = mm_nt(low_ref[...], store[y_at, :, pl.ds(col, chunk)])

        @pl.when(step == 0)
        def _():
            grad_ref[...] = product

        @pl.when(step > 0)
        def _():
            grad_ref[...] += product

        @pl.when(step == 3)
        def _():
            vec_ref[...] = jnp.zeros_like(vec_ref)

            @pl.loop(0, count // TILE)
            def _(i):
                at = pl.ds(pl.multiple_of(i * TILE, TILE), TILE)
                back = grad_ref[at, :]
                rows = x_ref[at, :]
                center = rows - jnp.mean(rows, axis=-1, keepdims=True)
                spread = jnp.mean(center * center, axis=-1, keepdims=True)
                scale = lax.rsqrt(spread + norm_eps)
                unit = center * scale
                inner = back * table_ref[gain_row : gain_row + 1, :]
                along = jnp.mean(inner * unit, axis=-1, keepdims=True)
                level = jnp.mean(inner, axis=-1, keepdims=True)
                grad = base_ref[at, :] + scale * (inner - level - unit * along)
                grad_ref[at, :] = grad
                vec_ref[0:1, :] += jnp.sum(back * unit, axis=0, keepdims=True)
                vec_ref[1:2, :] += jnp.sum(back, axis=0, keepdims=True)
                vec_ref[2:3, :] += jnp.sum(grad, axis=0, keepdims=True)
                if keep_low:
                    out_low_ref[at, :] = grad.astype(LOW)
                    turn_ref[:, at] = grad.T.astype(LOW)

    outs = [whole(count, width), whole(8, width)]
    shapes = [jax.ShapeDtypeStruct((count, width), F32), jax.ShapeDtypeStruct((8, width), F32)]
    if keep_low:
        outs += [whole(count, width), whole(width, count)]
        shapes += [
            jax.ShapeDtypeStruct((count, width), LOW),
            jax.ShapeDtypeStruct((width, count), LOW),
        ]
    return call(
        body,
        (4,),
        [
            pl.BlockSpec((count, chunk), lambda t, me: (0, t)),
            whole(count, width),
            whole(count, width),
            whole(*table.shape),
        ]
        + [ANY] * 8,
        outs,
        shapes,
        [pltpu.VMEM((2, width, span), LOW), pltpu.SemaphoreType.DMA((2,))],
        2 * count * width * 2 * span,
        count * width * 16 + width * span * 4 + count * span * 4,
        name,
        32 if keep_low else 60,
    )(me, low, rows_in, base, table, *pieces)


def mixed_back_call(me, middle_low, pieces):
    count, width = middle_low.shape
    half = width // 2

    def body(me_ref, low_ref, *refs):
        parts, (out_ref, store, sems) = refs[:8], refs[8:]
        step = pl.program_id(0)

        @pl.when(step == 0)
        def _():
            fetch(me_ref[0], parts, store, sems, 2 * width, half)

        for y_at in range(2):

            @pl.when(step == y_at)
            def _():
                arrived(store, sems, y_at)

        out_ref[...] = mm(low_ref[...], store[step]).astype(LOW)

    return call(
        body,
        (2,),
        [whole(count, width)] + [ANY] * 8,
        pl.BlockSpec((count, half), lambda t, me: (0, t)),
        jax.ShapeDtypeStruct((count, width), LOW),
        [pltpu.VMEM((2, width, half), LOW), pltpu.SemaphoreType.DMA((2,))],
        2 * count * width * width,
        count * width * 4 + width * width * 2,
        "mixed_back",
    )(me, middle_low, *pieces)


def attend_back_call(me, qkv, grads, visible):
    images, seq, _ = visible.shape
    count, full = qkv.shape
    half = full // 6
    scale = HEAD_DIM**-0.5

    def body(me_ref, qkv_ref, grad_ref, seen_ref, out_ref, sum_ref):
        seen = seen_ref[0] > 0
        @pl.loop(0, half // (2 * TILE))
        def _(pair):
            for part in range(2):
                col = pl.multiple_of((2 * pair + part) * TILE, TILE)
                query = qkv_ref[:, pl.ds(col, TILE)] * jnp.asarray(scale, LOW)
                key = qkv_ref[:, pl.ds(half + col, TILE)]
                value = qkv_ref[:, pl.ds(2 * half + col, TILE)]
                grad = grad_ref[:, pl.ds(col, TILE)]
                lanes = head_halves(query.shape)
                parts = []
                for keep in lanes:
                    scores = jnp.where(seen, mm_nt(jnp.where(keep, key, 0), query), masked_score)
                    exps = jnp.exp(scores - jnp.max(scores, axis=0, keepdims=True))
                    probs = exps * (1.0 / jnp.sum(exps, axis=0, keepdims=True))
                    prob_grad = mm_nt(jnp.where(keep, value, 0), grad)
                    row_dot = jnp.sum(probs * prob_grad, axis=0, keepdims=True)
                    score_grad = (probs * (prob_grad - row_dot)).astype(LOW)
                    parts.append(
                        (
                            mm_tn(key, score_grad).T * scale,
                            mm(score_grad, query),
                            mm(probs.astype(LOW), grad),
                        )
                    )
                for at in range(3):
                    merged = jnp.where(lanes[0], parts[0][at], parts[1][at])
                    put = at * half + col
                    out_ref[:, pl.ds(put, TILE)] = merged.astype(LOW)
                    sum_ref[0, 0, :, pl.ds(put, TILE)] = jnp.sum(merged, axis=0, keepdims=True)

    return call(
        body,
        (images, 2),
        [
            pl.BlockSpec((seq, 3 * half), lambda i, y, me: (i, y)),
            pl.BlockSpec((seq, half), lambda i, y, me: (i, y)),
            pl.BlockSpec((1, seq, 1), lambda i, y, me: (i, 0, 0)),
        ],
        [
            pl.BlockSpec((seq, 3 * half), lambda i, y, me: (i, y)),
            pl.BlockSpec((1, 1, 1, 3 * half), lambda i, y, me: (i, y, 0, 0)),
        ],
        [
            jax.ShapeDtypeStruct((count, full), LOW),
            jax.ShapeDtypeStruct((images, 2, 1, 3 * half), F32),
        ],
        [],
        10 * count * seq * 2 * half * 4,
        count * full * 5,
        "attend_back",
    )(me, qkv, grads, visible)


def weight_grad_call(me, turned, right, depth, core_flip, received, name):
    width, count = turned.shape
    span = right.shape[1] // 2
    chunk = next(c for c in (1024, 768, 512, 384, 256, 128) if span % c == 0)
    parts = span // chunk
    steps = 2 * parts
    rows = width // (4 * depth)
    quarter = width // 4

    def body(me_ref, turn_ref, right_ref, *refs):
        if core_flip:
            (far_ref, lefts, ready, sems) = refs
        else:
            (got_ref, kept_ref, sent_ref, lefts, ready, sems, got, got_sems) = refs
        step = pl.program_id(0)
        slot = step % 2
        owner = ((me_ref[0] >> 1) & 1) ^ core_flip

        def spot(off_y, off_x):
            return jnp.where(owner == 0, off_y, off_x), jnp.where(owner == 0, off_x, off_y)

        def fetched(at, off_x):
            first, second = spot(1 - at // parts, off_x)
            col = pl.multiple_of(at % parts * chunk, chunk)
            return pltpu.make_async_copy(
                got_ref.at[first, second, :, :, pl.ds(col, chunk)],
                got.at[at, off_x],
                got_sems.at[at, off_x],
            )

        def leaving(target, at, off_x):
            col = pl.multiple_of(at % parts * chunk, chunk)
            return pltpu.make_async_copy(
                ready.at[at % 2, off_x],
                target.at[:, :, pl.ds(col, chunk)],
                sems.at[at % 2, off_x],
            )

        @pl.when(step == 0)
        def _():
            if not core_flip:
                for at in range(steps):
                    for off_x in range(2):
                        fetched(at, off_x).start()
            for off_x in range(2):
                for off_z in range(depth):
                    row = pl.multiple_of(dp_of(me_ref[0], core_flip, off_x, off_z) * rows, rows)
                    put = off_x * quarter + off_z * rows
                    lefts[put : put + rows, :] = turn_ref[pl.ds(row, rows), :]

        product = mm(lefts[...], right_ref[...]).reshape(2, depth, rows, chunk)

        @pl.when(step >= 2)
        def _():
            for off_x in range(2):
                some = far_ref.at[0, 0] if core_flip else kept_ref.at[0]
                leaving(some, step, off_x).wait()

        for off_x in range(2):
            total = product[off_x]
            if not core_flip:
                fetched(step, off_x).wait()
                total = total + got[step, off_x].astype(F32)
            ready[slot, off_x] = total.astype(LOW)
            first, second = spot(1 - step // parts, off_x)
            if core_flip:
                leaving(far_ref.at[first, second], step, off_x).start()
            else:
                for at, target in enumerate((kept_ref, sent_ref)):

                    @pl.when(first == at)
                    def _():
                        leaving(target.at[second], step, off_x).start()

        @pl.when(step == steps - 1)
        def _():
            for back in range(min(2, steps)):
                for off_x in range(2):
                    some = far_ref.at[0, 0] if core_flip else kept_ref.at[0]
                    leaving(some, step - back, off_x).wait()

    def right_at(t, me):
        return 0, ((me[0] & 1) ^ (1 - t // parts)) * parts + t % parts

    ins = [whole(width, count), pl.BlockSpec((count, chunk), right_at)]
    scratch = [
        pltpu.VMEM((2 * quarter, count), LOW),
        pltpu.VMEM((2, 2, depth, rows, chunk), LOW),
        pltpu.SemaphoreType.DMA((2, 2)),
    ]
    if core_flip:
        outs = ANY
        shapes = jax.ShapeDtypeStruct((2, 2, depth, rows, span), LOW)
        extra = ()
    else:
        ins = ins + [ANY]
        outs = [ANY, ANY]
        shapes = [jax.ShapeDtypeStruct((2, depth, rows, span), LOW)] * 2
        extra = (received,)
        scratch += [
            pltpu.VMEM((steps, 2, depth, rows, chunk), LOW),
            pltpu.SemaphoreType.DMA((steps, 2)),
        ]
    return call(
        body,
        (steps,),
        ins,
        outs,
        shapes,
        scratch,
        2 * count * width * span,
        count * (width + span * 2) * 2 + width * span * 4,
        name,
    )(me, turned, right, *extra)


def swap(value, size, bits, other=None):
    other = bits if other is None else other
    return lax.ppermute(
        value, AXES, [(i, i ^ (other if i & CORE_BIT else bits)) for i in range(size)]
    )


def after(value, *others):
    return lax.optimization_barrier((value, *others))[0]


def along_depth(piece, size, steps):
    return [piece] + [swap(piece, size, k << Z_SHIFT) for k in steps]


def along_first(value, size):
    return swap(value, size, Y_BIT, X_BIT)


def along_second(value, size):
    return swap(value, size, X_BIT, Y_BIT)


def along_core(value, size):
    return swap(value, size, CORE_BIT)


class Scatter:
    def __init__(self, turned, right, size, depth, name):
        self.size, self.depth, self.name = size, depth, name
        self.turned, self.right = turned, right

    def far(self, me):
        self.me = me
        self.sent = weight_grad_call(
            me, self.turned, self.right, self.depth, 1, None, self.name + "_far"
        )
        self.received = swap(self.sent, self.size, CORE_BIT)
        return self.sent

    def near(self, *others):
        right = after(self.right, *others)
        self.kept, self.sent = weight_grad_call(
            self.me, self.turned, right, self.depth, 0, self.received, self.name + "_near"
        )
        self.received = swap(self.sent, self.size, Y_BIT, X_BIT)
        return self.kept

    def second(self, *others):
        kept = after(self.kept, *others)
        total = (kept.astype(F32) + self.received.astype(F32)).astype(LOW)
        self.kept = total[0]
        self.received = swap(total[1], self.size, X_BIT, Y_BIT)
        return self.kept

    def third(self, *others):
        kept = after(self.kept, *others)
        total = (kept.astype(F32) + self.received.astype(F32)).astype(LOW)
        self.kept = total[0]
        self.received = [
            swap(total[k], self.size, k << Z_SHIFT) for k in range(1, self.depth)
        ]
        return self.kept

    def last(self, *others):
        result = after(self.kept, *others).astype(F32)
        for value in self.received:
            result = result + value.astype(F32)
        return result


def shards(
    inputs,
    key_mask,
    ln1_gain,
    ln1_bias,
    w_qkv,
    qv_bias,
    w_proj,
    proj_bias,
    ln2_gain,
    ln2_bias,
    w_fc1,
    fc1_bias,
    w_fc2,
    fc2_bias,
    out_grad,
):
    tensor_rank = lax.axis_index("tensor")
    dp_rank = lax.axis_index("dp")
    dp_size = lax.axis_size("dp")
    size = 2 * dp_size
    depth = dp_size // 4
    own_images, seq, width = inputs.shape
    count = own_images * seq
    half = w_qkv.shape[2]
    rows = ln1_gain.shape[0]
    me = jnp.reshape(dp_rank * 2 + tensor_rank, (1,)).astype(jnp.int32)

    vectors = jnp.concatenate(
        [
            jnp.stack([ln1_gain, ln1_bias, qv_bias[0], qv_bias[1]]),
            jnp.stack([proj_bias, ln2_gain, ln2_bias, fc2_bias]),
            fc1_bias.reshape(4, rows),
        ]
    )
    vectors = jnp.pad(vectors, ((0, TILE - vectors.shape[0]), (0, 0))).T
    piece_one = jnp.concatenate([w_qkv[0], w_qkv[1], w_qkv[2], vectors], axis=1).astype(LOW)
    piece_two = jnp.concatenate([w_fc1, w_proj.T], axis=1).astype(LOW)
    piece_three = w_fc2.T.astype(LOW)

    held_one = jnp.stack(along_depth(piece_one, size, range(1, depth)))
    grad_in = out_grad.reshape(count, width)
    out_low = grad_in.astype(LOW)
    out_turned = out_low.T
    held_one, piece_two, out_low, out_turned = lax.optimization_barrier(
        (held_one, piece_two, out_low, out_turned)
    )
    first_one = along_first(held_one, size)
    second_one = along_second(held_one, size)
    far_one = [along_core(held_one, size)]
    deep_two = along_depth(piece_two, size, range(1, depth - 1))
    first_one, second_one, far_own, *deep_two = lax.optimization_barrier(
        (first_one, second_one, *far_one, *deep_two)
    )
    both_one = along_second(first_one, size)
    far_one = [far_own, along_core(second_one, size), along_core(first_one, size)]
    plane_one = [held_one, second_one, first_one]
    deep_two += along_depth(deep_two[0], size, [depth - 1])[1:]
    far_one += [along_core(both_one, size)]
    both_one, piece_three, *deep_two = lax.optimization_barrier((both_one, piece_three, *deep_two))
    pieces_one = plane_one + [both_one] + far_one
    held_two = jnp.stack(deep_two)
    first_two = along_first(held_two, size)
    second_two = along_second(held_two, size)
    far_two = [along_core(held_two, size)]
    deep_three = along_depth(piece_three, size, range(1, depth - 1))

    rows_in = inputs.reshape(count, width)
    own_mask = lax.dynamic_slice_in_dim(key_mask, tensor_rank * own_images, own_images, 0)
    visible = jnp.concatenate(
        [jnp.ones((own_images, seq - key_mask.shape[1]), jnp.int32), own_mask], axis=1
    )
    visible_rows = after(visible, held_one)[:, :, None]
    visible = visible[:, None, :]

    normed_one, turned_one, qkv, table = qkv_call(me, rows_in, pieces_one)
    fc1_full = table[8:12].reshape(4, dp_size, rows).transpose(1, 0, 2).reshape(1, 4 * width)
    qkv, first_two, second_two, *deep_three, far_own = lax.optimization_barrier(
        (qkv, first_two, second_two, *deep_three, *far_two)
    )
    both_two = along_second(first_two, size)
    far_two = [far_own, along_core(second_two, size), along_core(first_two, size)]
    plane_two = [held_two, second_two, first_two]
    deep_three += along_depth(deep_three[0], size, [depth - 1])[1:]
    mixed = attend_call(me, qkv, visible)
    mixed, fc1_full, both_two, *far_two = lax.optimization_barrier(
        (mixed, fc1_full, both_two, *far_two)
    )
    far_two += [along_core(both_two, size)]
    both_two, *deep_three = lax.optimization_barrier((both_two, *deep_three))
    pieces_two = plane_two + [both_two] + far_two
    held_three = jnp.stack(deep_three)
    first_three = along_first(held_three, size)
    second_three = along_second(held_three, size)
    far_three = [along_core(held_three, size)]
    middle, normed_two, turned_two = project_call(me, mixed, rows_in, table, pieces_two)
    normed_two, first_three, second_three, far_own = lax.optimization_barrier(
        (normed_two, first_three, second_three, *far_three)
    )
    both_three = along_second(first_three, size)
    far_three = [far_own, along_core(second_three, size), along_core(first_three, size)]
    plane_three = [held_three, second_three, first_three]
    hidden, slope = expand_call(me, normed_two, fc1_full, pieces_two)
    hidden, both_three, *far_three = lax.optimization_barrier((hidden, both_three, *far_three))
    far_three += [along_core(both_three, size)]
    pieces_three = plane_three + [both_three] + far_three
    fc2 = Scatter(out_turned, after(hidden, far_three[3]), size, depth, "fc2_grad")
    done = fc2.far(me)
    outputs, pre_low, fc1_sum = contract_call(
        me, after(hidden, done), slope, out_low, middle, table, pieces_three
    )
    fc1 = Scatter(turned_two, pre_low, size, depth, "fc1_grad")
    done = fc1.far(me)
    done = fc2.near(done)
    middle_grad, vec_two, middle_low, turned_mid = norm_back_call(
        me, after(pre_low, done), 0, 5, middle, grad_in, table, pieces_two, True, "norm_two_back"
    )
    mixed_grad = mixed_back_call(me, middle_low, pieces_two)
    proj = Scatter(turned_mid, after(mixed, mixed_grad), size, depth, "proj_grad")
    done = proj.far(me)
    done = fc2.second(done)
    done = proj.near(done)
    done = fc1.near(done)
    done = fc2.third(done)
    qkv_low, qkv_sum = attend_back_call(me, qkv, after(mixed_grad, done), visible_rows)
    landed = after(qkv_low, proj.received, *fc2.received)
    qkv_out = Scatter(turned_one, landed, size, depth, "qkv_grad")
    done = qkv_out.far(me)
    done = proj.second(done)
    done = fc1.second(done)
    done = qkv_out.near(done)
    done = fc1.third(done)
    input_grad, vec_one = norm_back_call(
        me,
        after(qkv_low, done),
        0,
        0,
        rows_in,
        middle_grad,
        table,
        pieces_one,
        False,
        "norm_one_back",
    )

    qkv_sum = jnp.sum(qkv_sum, axis=(0, 2)).reshape(2, 3, half)
    sums = jnp.concatenate(
        [
            vec_one[:2],
            qkv_sum[:, 0].reshape(1, width),
            qkv_sum[:, 2].reshape(1, width),
            vec_two[2:3],
            vec_two[:2],
            jnp.sum(grad_in, axis=0, keepdims=True),
            fc1_sum.reshape(4, width),
        ]
    )
    done = qkv_out.second(input_grad, *fc1.received)
    done = proj.third(done)
    sums = after(sums, done)
    sums = sums + along_core(sums, size)
    done = qkv_out.third(sums)
    fc1_grad = fc1.last(done)
    fc2_grad = fc2.last(done)
    proj_grad = proj.last(done)
    sums = after(sums, done)
    for bits in (X_BIT, Y_BIT):
        sums = sums + swap(sums, size, bits)
    sums = after(sums, *qkv_out.received)
    sums = sum(along_depth(sums, size, range(1, depth)))
    qkv_grad = qkv_out.last()
    mine = lax.dynamic_slice_in_dim(sums[:8], dp_rank * rows, rows, 1)
    fc1_mine = lax.dynamic_slice_in_dim(sums[8:].reshape(-1), dp_rank * 4 * rows, 4 * rows, 0)
    return (
        outputs.reshape(inputs.shape),
        input_grad.reshape(inputs.shape),
        mine[0],
        mine[1],
        qkv_grad.reshape(rows, 3, half).transpose(1, 0, 2),
        mine[2:4],
        proj_grad.T,
        mine[4],
        mine[5],
        mine[6],
        fc1_grad,
        fc1_mine,
        fc2_grad.T,
        mine[7],
    )


def solution(mesh):
    placed = (
        P(("dp", "tensor"), None, None),
        P("dp", None),
        P("dp"),
        P("dp"),
        P(None, "dp", "tensor"),
        P(None, "dp"),
        P("tensor", "dp"),
        P("dp"),
        P("dp"),
        P("dp"),
        P("dp", "tensor"),
        P("dp"),
        P("tensor", "dp"),
        P("dp"),
        P(("dp", "tensor"), None, None),
    )
    return jax.shard_map(
        shards,
        mesh=mesh,
        in_specs=placed,
        out_specs=(
            P(("dp", "tensor"), None, None),
            P(("dp", "tensor"), None, None),
            P("dp"),
            P("dp"),
            P(None, "dp", "tensor"),
            P(None, "dp"),
            P("tensor", "dp"),
            P("dp"),
            P("dp"),
            P("dp"),
            P("dp", "tensor"),
            P("dp"),
            P("tensor", "dp"),
            P("dp"),
        ),
        check_vma=False,
    )
```

```python
import jax
import jax.numpy as jnp
from jax import lax
from jax.experimental import pallas as pl
from jax.experimental.pallas import tpu as pltpu
from jax.sharding import PartitionSpec as P

HEAD_DIM = 64
norm_eps = 1e-06
masked_score = -1e30
AXES = ("dp", "tensor")
LOW = jnp.bfloat16
F32 = jnp.float32
TILE = 128
Y_BIT, CORE_BIT, X_BIT, Z_SHIFT = 1, 2, 4, 3
ANY = pl.BlockSpec(memory_space=pltpu.HBM)


def mm(left, right):
    return lax.dot_general(left, right, (((1,), (0,)), ((), ())), preferred_element_type=F32)


def mm_nt(left, right):
    return lax.dot_general(left, right, (((1,), (1,)), ((), ())), preferred_element_type=F32)


def mm_tn(left, right):
    return lax.dot_general(left, right, (((0,), (0,)), ((), ())), preferred_element_type=F32)


def whole(*shape):
    return pl.BlockSpec(shape, lambda t, me: (0,) * len(shape))


def call(body, grid, ins, outs, shapes, scratch, flops, moved, name, room=32, heavy=False):
    return pl.pallas_call(
        body,
        grid_spec=pltpu.PrefetchScalarGridSpec(
            num_scalar_prefetch=1,
            grid=grid,
            in_specs=ins,
            out_specs=outs,
            scratch_shapes=scratch,
        ),
        out_shape=shapes,
        compiler_params=pltpu.CompilerParams(
            dimension_semantics=("arbitrary",) * len(grid), vmem_limit_bytes=room << 20
        ),
        cost_estimate=pl.CostEstimate(
            flops=flops if heavy else 1, bytes_accessed=moved if heavy else 1, transcendentals=0
        ),
        name=name,
    )


def places(me, core_flip, first, second):
    owner = ((me >> 1) & 1) ^ core_flip
    off_y = jnp.where(owner == 0, first, second)
    off_x = jnp.where(owner == 0, second, first)
    return off_y, off_x


def dp_of(me, core_flip, off_x, off_z):
    core = ((me >> 1) & 1) ^ core_flip
    return (((me >> Z_SHIFT) ^ off_z) << 2) | ((((me >> 2) & 1) ^ off_x) << 1) | core


def fetch(me, pieces, store, sems, start, width):
    for index, piece in enumerate(pieces):
        core_flip, first, second = index >> 2, (index >> 1) & 1, index & 1
        off_y, off_x = places(me, core_flip, first, second)
        y_at = (me & 1) ^ off_y
        depth, rows, _ = piece.shape
        for off_z in range(depth):
            row = pl.multiple_of(dp_of(me, core_flip, off_x, off_z) * rows, rows)
            pltpu.make_async_copy(
                piece.at[off_z, :, pl.ds(start, width)],
                store.at[y_at, pl.ds(row, rows), :],
                sems.at[y_at],
            ).start()


def arrived(store, sems, y_at):
    pltpu.make_async_copy(store.at[y_at], store.at[y_at], sems.at[y_at]).wait()


def normed(rows, gain, shift):
    center = rows - jnp.mean(rows, axis=-1, keepdims=True)
    spread = jnp.mean(center * center, axis=-1, keepdims=True)
    return center * lax.rsqrt(spread + norm_eps) * gain + shift


def qkv_call(me, rows_in, pieces):
    count, width = rows_in.shape
    half = width // 2
    span = 3 * half

    def body(me_ref, x_ref, *refs):
        parts, refs = refs[:8], refs[8:]
        norm_ref, turn_ref, out_ref, table_ref, store, sems, vectors, vector_sems = refs
        step = pl.program_id(0)

        @pl.when(step == 0)
        def _():
            fetch(me_ref[0], parts, vectors, vector_sems, span, TILE)
            fetch(me_ref[0], parts, store, sems, 0, span)
            for y_at in range(2):
                arrived(vectors, vector_sems, y_at)
            table_ref[...] = vectors[0].astype(F32).T[: table_ref.shape[0]]

            @pl.loop(0, count // TILE)
            def _(i):
                at = pl.ds(pl.multiple_of(i * TILE, TILE), TILE)
                value = normed(x_ref[at, :], table_ref[0:1, :], table_ref[1:2, :])
                norm_ref[at, :] = value.astype(LOW)
                turn_ref[:, at] = value.T.astype(LOW)

        for y_at in range(2):

            @pl.when(step == 3 * y_at)
            def _():
                arrived(store, sems, y_at)

        y_at, kind = step // 3, step % 3
        col = pl.multiple_of(kind * half, half)
        own = pl.ds(pl.multiple_of(y_at * half, half), half)
        product = mm(norm_ref[...], store[y_at, :, pl.ds(col, half)])
        bias = jnp.where(kind == 0, table_ref[2:3, own], table_ref[3:4, own])
        bias = jnp.where(kind == 1, 0.0, bias)
        out_ref[...] = (product + bias).astype(LOW)

    return call(
        body,
        (6,),
        [whole(count, width)] + [ANY] * 8,
        [
            whole(count, width),
            whole(width, count),
            pl.BlockSpec((count, half), lambda t, me: (0, t)),
            whole(16, width),
        ],
        [
            jax.ShapeDtypeStruct((count, width), LOW),
            jax.ShapeDtypeStruct((width, count), LOW),
            jax.ShapeDtypeStruct((count, 2 * span), LOW),
            jax.ShapeDtypeStruct((16, width), F32),
        ],
        [
            pltpu.VMEM((2, width, span), LOW),
            pltpu.SemaphoreType.DMA((2,)),
            pltpu.VMEM((2, width, TILE), LOW),
            pltpu.SemaphoreType.DMA((2,)),
        ],
        2 * count * width * 2 * span,
        count * width * 16 + width * span * 4,
        "qkv",
        60,
    )(me, rows_in, *pieces)


def head_halves(shape):
    lane = lax.broadcasted_iota(jnp.int32, shape, 1)
    return lane < HEAD_DIM, lane >= HEAD_DIM


def attend_call(me, qkv, visible):
    images, _, seq = visible.shape
    count, full = qkv.shape
    half = full // 6

    def body(me_ref, qkv_ref, seen_ref, out_ref):
        seen = seen_ref[0] > 0

        @pl.loop(0, half // (2 * TILE))
        def _(pair):
            for part in range(2):
                col = pl.multiple_of((2 * pair + part) * TILE, TILE)
                query = qkv_ref[:, pl.ds(col, TILE)] * jnp.asarray(HEAD_DIM**-0.5, LOW)
                key = qkv_ref[:, pl.ds(half + col, TILE)]
                value = qkv_ref[:, pl.ds(2 * half + col, TILE)]
                lanes = head_halves(query.shape)
                mixed = []
                for keep in lanes:
                    scores = jnp.where(seen, mm_nt(jnp.where(keep, query, 0), key), masked_score)
                    exps = jnp.exp(scores - jnp.max(scores, axis=-1, keepdims=True))
                    total = jnp.sum(exps, axis=-1, keepdims=True)
                    mixed.append(mm(exps.astype(LOW), value) * (1.0 / total))
                out_ref[:, pl.ds(col, TILE)] = jnp.where(lanes[0], mixed[0], mixed[1]).astype(LOW)

    return call(
        body,
        (images, 2),
        [
            pl.BlockSpec((seq, 3 * half), lambda i, y, me: (i, y)),
            pl.BlockSpec((1, 1, seq), lambda i, y, me: (i, 0, 0)),
        ],
        pl.BlockSpec((seq, half), lambda i, y, me: (i, y)),
        jax.ShapeDtypeStruct((count, 2 * half), LOW),
        [],
        4 * count * seq * 2 * half * 4,
        count * full * 3,
        "attend",
    )(me, qkv, visible)


def project_call(me, mixed, rows_in, table, pieces):
    count, width = rows_in.shape
    half = width // 2

    def body(me_ref, mixed_ref, x_ref, table_ref, *refs):
        parts, (mid_ref, norm_ref, turn_ref, store, sems) = refs[:8], refs[8:]
        fetch(me_ref[0], parts, store, sems, 2 * width, half)
        arrived(store, sems, 0)
        mid_ref[...] = mm_nt(mixed_ref[:, :half], store[0])
        arrived(store, sems, 1)
        mid_ref[...] += mm_nt(mixed_ref[:, half:], store[1])

        @pl.loop(0, count // TILE)
        def _(i):
            at = pl.ds(pl.multiple_of(i * TILE, TILE), TILE)
            middle = x_ref[at, :] + (mid_ref[at, :] + table_ref[4:5, :])
            mid_ref[at, :] = middle
            value = normed(middle, table_ref[5:6, :], table_ref[6:7, :])
            norm_ref[at, :] = value.astype(LOW)
            turn_ref[:, at] = value.T.astype(LOW)

    return call(
        body,
        (1,),
        [whole(count, width), whole(count, width), whole(*table.shape)] + [ANY] * 8,
        [whole(count, width), whole(count, width), whole(width, count)],
        [
            jax.ShapeDtypeStruct((count, width), F32),
            jax.ShapeDtypeStruct((count, width), LOW),
            jax.ShapeDtypeStruct((width, count), LOW),
        ],
        [pltpu.VMEM((2, width, half), LOW), pltpu.SemaphoreType.DMA((2,))],
        2 * count * width * width,
        count * width * 14 + width * width * 2,
        "project",
    )(me, mixed, rows_in, table, *pieces)


def expand_call(me, normed_two, bias, pieces):
    count, width = normed_two.shape
    span = bias.shape[1] // 2
    chunk = span // 4

    def body(me_ref, norm_ref, bias_ref, *refs):
        parts, (hid_ref, slope_ref, store, sems) = refs[:8], refs[8:]
        step = pl.program_id(0)

        @pl.when(step == 0)
        def _():
            fetch(me_ref[0], parts, store, sems, 0, span)

        for y_at in range(2):

            @pl.when(step == 4 * y_at)
            def _():
                arrived(store, sems, y_at)

        y_at, col = step // 4, pl.multiple_of(step % 4 * chunk, chunk)
        pre = mm(norm_ref[...], store[y_at, :, pl.ds(col, chunk)]) + bias_ref[...]
        below = 0.5 + 0.5 * lax.erf(pre * 0.5**0.5)
        hid_ref[...] = (pre * below).astype(LOW)
        slope_ref[...] = (below + pre * jnp.exp(pre * pre * -0.5) * 0.3989422804014327).astype(LOW)

    out = pl.BlockSpec((count, chunk), lambda t, me: (0, t))
    return call(
        body,
        (8,),
        [whole(count, width), pl.BlockSpec((1, chunk), lambda t, me: (0, t))] + [ANY] * 8,
        [out, out],
        [jax.ShapeDtypeStruct((count, 2 * span), LOW)] * 2,
        [pltpu.VMEM((2, width, span), LOW), pltpu.SemaphoreType.DMA((2,))],
        2 * count * width * 2 * span,
        count * span * 8 + width * span * 4,
        "expand",
        60,
    )(me, normed_two, bias, *pieces)


def contract_call(me, hidden, slope, out_low, middle, table, pieces):
    count, width = middle.shape
    span = hidden.shape[1] // 2
    chunk = span // 4

    def body(me_ref, hid_ref, slope_ref, low_ref, mid_ref, table_ref, *refs):
        parts, (act_ref, pre_ref, sum_ref, store, sems) = refs[:8], refs[8:]
        step = pl.program_id(0)

        @pl.when(step == 0)
        def _():
            fetch(me_ref[0], parts, store, sems, 0, span)
            act_ref[...] = mid_ref[...] + table_ref[7:8, :]

        for y_at in range(2):

            @pl.when(step == 4 * y_at)
            def _():
                arrived(store, sems, y_at)

        y_at, col = step // 4, pl.multiple_of(step % 4 * chunk, chunk)
        weight = store[y_at, :, pl.ds(col, chunk)]
        act_ref[...] += mm_nt(hid_ref[...], weight)
        pre = mm(low_ref[...], weight) * slope_ref[...].astype(F32)
        pre_ref[...] = pre.astype(LOW)
        sum_ref[...] = jnp.sum(pre, axis=0, keepdims=True)

    part = pl.BlockSpec((count, chunk), lambda t, me: (0, t))
    return call(
        body,
        (8,),
        [part, part, whole(count, width), whole(count, width), whole(*table.shape)] + [ANY] * 8,
        [whole(count, width), part, pl.BlockSpec((1, chunk), lambda t, me: (0, t))],
        [
            jax.ShapeDtypeStruct((count, width), F32),
            jax.ShapeDtypeStruct((count, 2 * span), LOW),
            jax.ShapeDtypeStruct((1, 2 * span), F32),
        ],
        [pltpu.VMEM((2, width, span), LOW), pltpu.SemaphoreType.DMA((2,))],
        4 * count * width * 2 * span,
        count * span * 12 + width * span * 4,
        "contract",
        heavy=True,
    )(me, hidden, slope, out_low, middle, table, *pieces)


def norm_back_call(me, low, start, gain_row, rows_in, base, table, pieces, keep_low, name):
    count, width = rows_in.shape
    span = low.shape[1] // 2
    chunk = span // 2

    def body(me_ref, low_ref, x_ref, base_ref, table_ref, *refs):
        parts, outs = refs[:8], refs[8:]
        if keep_low:
            grad_ref, vec_ref, out_low_ref, turn_ref, store, sems = outs
        else:
            grad_ref, vec_ref, store, sems = outs
        step = pl.program_id(0)

        @pl.when(step == 0)
        def _():
            fetch(me_ref[0], parts, store, sems, start, span)

        for y_at in range(2):

            @pl.when(step == 2 * y_at)
            def _():
                arrived(store, sems, y_at)

        y_at, col = step // 2, pl.multiple_of(step % 2 * chunk, chunk)
        product = mm_nt(low_ref[...], store[y_at, :, pl.ds(col, chunk)])

        @pl.when(step == 0)
        def _():
            grad_ref[...] = product

        @pl.when(step > 0)
        def _():
            grad_ref[...] += product

        @pl.when(step == 3)
        def _():
            vec_ref[...] = jnp.zeros_like(vec_ref)

            @pl.loop(0, count // TILE)
            def _(i):
                at = pl.ds(pl.multiple_of(i * TILE, TILE), TILE)
                back = grad_ref[at, :]
                rows = x_ref[at, :]
                center = rows - jnp.mean(rows, axis=-1, keepdims=True)
                spread = jnp.mean(center * center, axis=-1, keepdims=True)
                scale = lax.rsqrt(spread + norm_eps)
                unit = center * scale
                inner = back * table_ref[gain_row : gain_row + 1, :]
                along = jnp.mean(inner * unit, axis=-1, keepdims=True)
                level = jnp.mean(inner, axis=-1, keepdims=True)
                grad = base_ref[at, :] + scale * (inner - level - unit * along)
                grad_ref[at, :] = grad
                vec_ref[0:1, :] += jnp.sum(back * unit, axis=0, keepdims=True)
                vec_ref[1:2, :] += jnp.sum(back, axis=0, keepdims=True)
                vec_ref[2:3, :] += jnp.sum(grad, axis=0, keepdims=True)
                if keep_low:
                    out_low_ref[at, :] = grad.astype(LOW)
                    turn_ref[:, at] = grad.T.astype(LOW)

    outs = [whole(count, width), whole(8, width)]
    shapes = [jax.ShapeDtypeStruct((count, width), F32), jax.ShapeDtypeStruct((8, width), F32)]
    if keep_low:
        outs += [whole(count, width), whole(width, count)]
        shapes += [
            jax.ShapeDtypeStruct((count, width), LOW),
            jax.ShapeDtypeStruct((width, count), LOW),
        ]
    return call(
        body,
        (4,),
        [
            pl.BlockSpec((count, chunk), lambda t, me: (0, t)),
            whole(count, width),
            whole(count, width),
            whole(*table.shape),
        ]
        + [ANY] * 8,
        outs,
        shapes,
        [pltpu.VMEM((2, width, span), LOW), pltpu.SemaphoreType.DMA((2,))],
        2 * count * width * 2 * span,
        count * width * 16 + width * span * 4 + count * span * 4,
        name,
        32 if keep_low else 60,
    )(me, low, rows_in, base, table, *pieces)


def mixed_back_call(me, middle_low, pieces):
    count, width = middle_low.shape
    half = width // 2

    def body(me_ref, low_ref, *refs):
        parts, (out_ref, store, sems) = refs[:8], refs[8:]
        step = pl.program_id(0)

        @pl.when(step == 0)
        def _():
            fetch(me_ref[0], parts, store, sems, 2 * width, half)

        for y_at in range(2):

            @pl.when(step == y_at)
            def _():
                arrived(store, sems, y_at)

        out_ref[...] = mm(low_ref[...], store[step]).astype(LOW)

    return call(
        body,
        (2,),
        [whole(count, width)] + [ANY] * 8,
        pl.BlockSpec((count, half), lambda t, me: (0, t)),
        jax.ShapeDtypeStruct((count, width), LOW),
        [pltpu.VMEM((2, width, half), LOW), pltpu.SemaphoreType.DMA((2,))],
        2 * count * width * width,
        count * width * 4 + width * width * 2,
        "mixed_back",
    )(me, middle_low, *pieces)


def attend_back_call(me, qkv, grads, visible):
    images, seq, _ = visible.shape
    count, full = qkv.shape
    half = full // 6
    scale = HEAD_DIM**-0.5

    def body(me_ref, qkv_ref, grad_ref, seen_ref, out_ref, sum_ref):
        seen = seen_ref[0] > 0
        @pl.loop(0, half // (2 * TILE))
        def _(pair):
            for part in range(2):
                col = pl.multiple_of((2 * pair + part) * TILE, TILE)
                query = qkv_ref[:, pl.ds(col, TILE)] * jnp.asarray(scale, LOW)
                key = qkv_ref[:, pl.ds(half + col, TILE)]
                value = qkv_ref[:, pl.ds(2 * half + col, TILE)]
                grad = grad_ref[:, pl.ds(col, TILE)]
                lanes = head_halves(query.shape)
                parts = []
                for keep in lanes:
                    scores = jnp.where(seen, mm_nt(jnp.where(keep, key, 0), query), masked_score)
                    exps = jnp.exp(scores - jnp.max(scores, axis=0, keepdims=True))
                    probs = exps * (1.0 / jnp.sum(exps, axis=0, keepdims=True))
                    prob_grad = mm_nt(jnp.where(keep, value, 0), grad)
                    row_dot = jnp.sum(probs * prob_grad, axis=0, keepdims=True)
                    score_grad = (probs * (prob_grad - row_dot)).astype(LOW)
                    parts.append(
                        (
                            mm_tn(key, score_grad).T * scale,
                            mm(score_grad, query),
                            mm(probs.astype(LOW), grad),
                        )
                    )
                for at in range(3):
                    merged = jnp.where(lanes[0], parts[0][at], parts[1][at])
                    put = at * half + col
                    out_ref[:, pl.ds(put, TILE)] = merged.astype(LOW)
                    sum_ref[0, 0, :, pl.ds(put, TILE)] = jnp.sum(merged, axis=0, keepdims=True)

    return call(
        body,
        (images, 2),
        [
            pl.BlockSpec((seq, 3 * half), lambda i, y, me: (i, y)),
            pl.BlockSpec((seq, half), lambda i, y, me: (i, y)),
            pl.BlockSpec((1, seq, 1), lambda i, y, me: (i, 0, 0)),
        ],
        [
            pl.BlockSpec((seq, 3 * half), lambda i, y, me: (i, y)),
            pl.BlockSpec((1, 1, 1, 3 * half), lambda i, y, me: (i, y, 0, 0)),
        ],
        [
            jax.ShapeDtypeStruct((count, full), LOW),
            jax.ShapeDtypeStruct((images, 2, 1, 3 * half), F32),
        ],
        [],
        10 * count * seq * 2 * half * 4,
        count * full * 5,
        "attend_back",
    )(me, qkv, grads, visible)


def weight_grad_call(me, turned, right, depth, core_flip, received, name):
    width, count = turned.shape
    span = right.shape[1] // 2
    chunk = next(c for c in (1024, 768, 512, 384, 256, 128) if span % c == 0)
    parts = span // chunk
    steps = 2 * parts
    rows = width // (4 * depth)
    quarter = width // 4

    def body(me_ref, turn_ref, right_ref, *refs):
        if core_flip:
            (far_ref, lefts, ready, sems) = refs
        else:
            (got_ref, kept_ref, sent_ref, lefts, ready, sems, got, got_sems) = refs
        step = pl.program_id(0)
        slot = step % 2
        owner = ((me_ref[0] >> 1) & 1) ^ core_flip

        def spot(off_y, off_x):
            return jnp.where(owner == 0, off_y, off_x), jnp.where(owner == 0, off_x, off_y)

        def fetched(at, off_x):
            first, second = spot(1 - at // parts, off_x)
            col = pl.multiple_of(at % parts * chunk, chunk)
            return pltpu.make_async_copy(
                got_ref.at[first, second, :, :, pl.ds(col, chunk)],
                got.at[at, off_x],
                got_sems.at[at, off_x],
            )

        def leaving(target, at, off_x):
            col = pl.multiple_of(at % parts * chunk, chunk)
            return pltpu.make_async_copy(
                ready.at[at % 2, off_x],
                target.at[:, :, pl.ds(col, chunk)],
                sems.at[at % 2, off_x],
            )

        @pl.when(step == 0)
        def _():
            if not core_flip:
                for at in range(steps):
                    for off_x in range(2):
                        fetched(at, off_x).start()
            for off_x in range(2):
                for off_z in range(depth):
                    row = pl.multiple_of(dp_of(me_ref[0], core_flip, off_x, off_z) * rows, rows)
                    put = off_x * quarter + off_z * rows
                    lefts[put : put + rows, :] = turn_ref[pl.ds(row, rows), :]

        product = mm(lefts[...], right_ref[...]).reshape(2, depth, rows, chunk)

        @pl.when(step >= 2)
        def _():
            for off_x in range(2):
                some = far_ref.at[0, 0] if core_flip else kept_ref.at[0]
                leaving(some, step, off_x).wait()

        for off_x in range(2):
            total = product[off_x]
            if not core_flip:
                fetched(step, off_x).wait()
                total = total + got[step, off_x].astype(F32)
            ready[slot, off_x] = total.astype(LOW)
            first, second = spot(1 - step // parts, off_x)
            if core_flip:
                leaving(far_ref.at[first, second], step, off_x).start()
            else:
                for at, target in enumerate((kept_ref, sent_ref)):

                    @pl.when(first == at)
                    def _():
                        leaving(target.at[second], step, off_x).start()

        @pl.when(step == steps - 1)
        def _():
            for back in range(min(2, steps)):
                for off_x in range(2):
                    some = far_ref.at[0, 0] if core_flip else kept_ref.at[0]
                    leaving(some, step - back, off_x).wait()

    def right_at(t, me):
        return 0, ((me[0] & 1) ^ (1 - t // parts)) * parts + t % parts

    ins = [whole(width, count), pl.BlockSpec((count, chunk), right_at)]
    scratch = [
        pltpu.VMEM((2 * quarter, count), LOW),
        pltpu.VMEM((2, 2, depth, rows, chunk), LOW),
        pltpu.SemaphoreType.DMA((2, 2)),
    ]
    if core_flip:
        outs = ANY
        shapes = jax.ShapeDtypeStruct((2, 2, depth, rows, span), LOW)
        extra = ()
    else:
        ins = ins + [ANY]
        outs = [ANY, ANY]
        shapes = [jax.ShapeDtypeStruct((2, depth, rows, span), LOW)] * 2
        extra = (received,)
        scratch += [
            pltpu.VMEM((steps, 2, depth, rows, chunk), LOW),
            pltpu.SemaphoreType.DMA((steps, 2)),
        ]
    return call(
        body,
        (steps,),
        ins,
        outs,
        shapes,
        scratch,
        2 * count * width * span,
        count * (width + span * 2) * 2 + width * span * 4,
        name,
    )(me, turned, right, *extra)


def swap(value, size, bits, other=None):
    other = bits if other is None else other
    return lax.ppermute(
        value, AXES, [(i, i ^ (other if i & CORE_BIT else bits)) for i in range(size)]
    )


def after(value, *others):
    return lax.optimization_barrier((value, *others))[0]


def along_depth(piece, size, steps):
    return [piece] + [swap(piece, size, k << Z_SHIFT) for k in steps]


def along_first(value, size):
    return swap(value, size, Y_BIT, X_BIT)


def along_second(value, size):
    return swap(value, size, X_BIT, Y_BIT)


def along_core(value, size):
    return swap(value, size, CORE_BIT)


class Scatter:
    def __init__(self, turned, right, size, depth, name):
        self.size, self.depth, self.name = size, depth, name
        self.turned, self.right = turned, right

    def far(self, me):
        self.me = me
        self.sent = weight_grad_call(
            me, self.turned, self.right, self.depth, 1, None, self.name + "_far"
        )
        self.received = swap(self.sent, self.size, CORE_BIT)
        return self.sent

    def near(self, *others):
        right = after(self.right, *others)
        self.kept, self.sent = weight_grad_call(
            self.me, self.turned, right, self.depth, 0, self.received, self.name + "_near"
        )
        self.received = swap(self.sent, self.size, Y_BIT, X_BIT)
        return self.kept

    def second(self, *others, joined=()):
        kept = after(self.kept, *others)
        total = (kept.astype(F32) + self.received.astype(F32)).astype(LOW)
        for other in joined:
            kept = after(other.kept, *others)
            more = (kept.astype(F32) + other.received.astype(F32)).astype(LOW)
            total = jnp.concatenate([total, more], axis=-1)
        self.kept = total[0]
        self.received = swap(total[1], self.size, X_BIT, Y_BIT)
        return self.kept

    def third(self, *others):
        kept = after(self.kept, *others)
        total = (kept.astype(F32) + self.received.astype(F32)).astype(LOW)
        self.kept = total[0]
        self.received = [
            swap(total[k], self.size, k << Z_SHIFT) for k in range(1, self.depth)
        ]
        return self.kept

    def last(self, *others):
        result = after(self.kept, *others).astype(F32)
        for value in self.received:
            result = result + value.astype(F32)
        return result


def shards(
    inputs,
    key_mask,
    ln1_gain,
    ln1_bias,
    w_qkv,
    qv_bias,
    w_proj,
    proj_bias,
    ln2_gain,
    ln2_bias,
    w_fc1,
    fc1_bias,
    w_fc2,
    fc2_bias,
    out_grad,
):
    tensor_rank = lax.axis_index("tensor")
    dp_rank = lax.axis_index("dp")
    dp_size = lax.axis_size("dp")
    size = 2 * dp_size
    depth = dp_size // 4
    own_images, seq, width = inputs.shape
    count = own_images * seq
    half = w_qkv.shape[2]
    rows = ln1_gain.shape[0]
    me = jnp.reshape(dp_rank * 2 + tensor_rank, (1,)).astype(jnp.int32)

    vectors = jnp.concatenate(
        [
            jnp.stack([ln1_gain, ln1_bias, qv_bias[0], qv_bias[1]]),
            jnp.stack([proj_bias, ln2_gain, ln2_bias, fc2_bias]),
            fc1_bias.reshape(4, rows),
        ]
    )
    vectors = jnp.pad(vectors, ((0, TILE - vectors.shape[0]), (0, 0))).T
    piece_one = jnp.concatenate([w_qkv[0], w_qkv[1], w_qkv[2], vectors], axis=1).astype(LOW)
    piece_two = jnp.concatenate([w_fc1, w_proj.T], axis=1).astype(LOW)
    piece_three = w_fc2.T.astype(LOW)

    held_one = jnp.stack(along_depth(piece_one, size, range(1, depth)))
    grad_in = out_grad.reshape(count, width)
    out_low = grad_in.astype(LOW)
    out_turned = out_low.T
    held_one, piece_two, out_low, out_turned = lax.optimization_barrier(
        (held_one, piece_two, out_low, out_turned)
    )
    first_one = along_first(held_one, size)
    second_one = along_second(held_one, size)
    far_one = [along_core(held_one, size)]
    deep_two = along_depth(piece_two, size, range(1, depth - 1))
    first_one, second_one, far_own, *deep_two = lax.optimization_barrier(
        (first_one, second_one, *far_one, *deep_two)
    )
    both_one = along_second(first_one, size)
    far_one = [far_own, along_core(second_one, size), along_core(first_one, size)]
    plane_one = [held_one, second_one, first_one]
    deep_two += along_depth(deep_two[0], size, [depth - 1])[1:]
    far_one += [along_core(both_one, size)]
    both_one, piece_three, *deep_two = lax.optimization_barrier((both_one, piece_three, *deep_two))
    pieces_one = plane_one + [both_one] + far_one
    held_two = jnp.stack(deep_two)
    first_two = along_first(held_two, size)
    second_two = along_second(held_two, size)
    far_two = [along_core(held_two, size)]
    deep_three = along_depth(piece_three, size, range(1, depth - 1))

    rows_in = inputs.reshape(count, width)
    own_mask = lax.dynamic_slice_in_dim(key_mask, tensor_rank * own_images, own_images, 0)
    visible = jnp.concatenate(
        [jnp.ones((own_images, seq - key_mask.shape[1]), jnp.int32), own_mask], axis=1
    )
    visible_rows = after(visible, held_one)[:, :, None]
    visible = visible[:, None, :]

    normed_one, turned_one, qkv, table = qkv_call(me, rows_in, pieces_one)
    fc1_full = table[8:12].reshape(4, dp_size, rows).transpose(1, 0, 2).reshape(1, 4 * width)
    qkv, first_two, second_two, *deep_three, far_own = lax.optimization_barrier(
        (qkv, first_two, second_two, *deep_three, *far_two)
    )
    both_two = along_second(first_two, size)
    far_two = [far_own, along_core(second_two, size), along_core(first_two, size)]
    plane_two = [held_two, second_two, first_two]
    deep_three += along_depth(deep_three[0], size, [depth - 1])[1:]
    mixed = attend_call(me, qkv, visible)
    mixed, fc1_full, both_two, *far_two = lax.optimization_barrier(
        (mixed, fc1_full, both_two, *far_two)
    )
    far_two += [along_core(both_two, size)]
    both_two, *deep_three = lax.optimization_barrier((both_two, *deep_three))
    pieces_two = plane_two + [both_two] + far_two
    held_three = jnp.stack(deep_three)
    first_three = along_first(held_three, size)
    second_three = along_second(held_three, size)
    far_three = [along_core(held_three, size)]
    middle, normed_two, turned_two = project_call(me, mixed, rows_in, table, pieces_two)
    hidden, slope = expand_call(me, normed_two, fc1_full, pieces_two)
    hidden, first_three, second_three, far_own = lax.optimization_barrier(
        (hidden, first_three, second_three, *far_three)
    )
    both_three = along_second(first_three, size)
    far_three = [far_own, along_core(second_three, size), along_core(first_three, size)]
    plane_three = [held_three, second_three, first_three]
    fc2 = Scatter(out_turned, hidden, size, depth, "fc2_grad")
    done = fc2.far(me)
    both_three = after(both_three, done)
    far_three += [along_core(both_three, size)]
    pieces_three = plane_three + [both_three] + far_three
    outputs, pre_low, fc1_sum = contract_call(
        me, after(hidden, done), slope, out_low, middle, table, pieces_three
    )
    fc1 = Scatter(turned_two, pre_low, size, depth, "fc1_grad")
    done = fc1.far(me)
    done = fc2.near(done)
    middle_grad, vec_two, middle_low, turned_mid = norm_back_call(
        me, after(pre_low, done), 0, 5, middle, grad_in, table, pieces_two, True, "norm_two_back"
    )
    mixed_grad = mixed_back_call(me, middle_low, pieces_two)
    proj = Scatter(turned_mid, after(mixed, mixed_grad), size, depth, "proj_grad")
    done = proj.far(me)
    done = fc2.second(done)
    done = proj.near(done)
    done = fc1.near(done)
    done = fc2.third(done)
    qkv_low, qkv_sum = attend_back_call(me, qkv, after(mixed_grad, done), visible_rows)
    done = fc1.second(qkv_low, proj.received, *fc2.received, joined=[proj])
    qkv_out = Scatter(turned_one, after(qkv_low, done), size, depth, "qkv_grad")
    done = qkv_out.far(me)
    done = qkv_out.near(done)
    done = fc1.third(done)
    input_grad, vec_one = norm_back_call(
        me,
        after(qkv_low, done),
        0,
        0,
        rows_in,
        middle_grad,
        table,
        pieces_one,
        False,
        "norm_one_back",
    )

    qkv_sum = jnp.sum(qkv_sum, axis=(0, 2)).reshape(2, 3, half)
    sums = jnp.concatenate(
        [
            vec_one[:2],
            qkv_sum[:, 0].reshape(1, width),
            qkv_sum[:, 2].reshape(1, width),
            vec_two[2:3],
            vec_two[:2],
            jnp.sum(grad_in, axis=0, keepdims=True),
            fc1_sum.reshape(4, width),
        ]
    )
    done = qkv_out.second(input_grad, *fc1.received)
    sums = after(sums, done)
    sums = sums + along_core(sums, size)
    done = qkv_out.third(sums)
    sums = after(sums, done)
    for bits in (X_BIT, Y_BIT):
        sums = sums + swap(sums, size, bits)
    sums = after(sums, qkv_out.received[0])
    fc2_grad = fc2.last(sums)
    fc1_grad = fc1.last(sums)
    fc1_grad, proj_grad = fc1_grad[:, : 4 * half], fc1_grad[:, 4 * half :]
    sums = sum(along_depth(sums, size, range(1, depth)))
    qkv_grad = qkv_out.last()
    mine = lax.dynamic_slice_in_dim(sums[:8], dp_rank * rows, rows, 1)
    fc1_mine = lax.dynamic_slice_in_dim(sums[8:].reshape(-1), dp_rank * 4 * rows, 4 * rows, 0)
    return (
        outputs.reshape(inputs.shape),
        input_grad.reshape(inputs.shape),
        mine[0],
        mine[1],
        qkv_grad.reshape(rows, 3, half).transpose(1, 0, 2),
        mine[2:4],
        proj_grad.T,
        mine[4],
        mine[5],
        mine[6],
        fc1_grad,
        fc1_mine,
        fc2_grad.T,
        mine[7],
    )


def solution(mesh):
    placed = (
        P(("dp", "tensor"), None, None),
        P("dp", None),
        P("dp"),
        P("dp"),
        P(None, "dp", "tensor"),
        P(None, "dp"),
        P("tensor", "dp"),
        P("dp"),
        P("dp"),
        P("dp"),
        P("dp", "tensor"),
        P("dp"),
        P("tensor", "dp"),
        P("dp"),
        P(("dp", "tensor"), None, None),
    )
    return jax.shard_map(
        shards,
        mesh=mesh,
        in_specs=placed,
        out_specs=(
            P(("dp", "tensor"), None, None),
            P(("dp", "tensor"), None, None),
            P("dp"),
            P("dp"),
            P(None, "dp", "tensor"),
            P(None, "dp"),
            P("tensor", "dp"),
            P("dp"),
            P("dp"),
            P("dp"),
            P("dp", "tensor"),
            P("dp"),
            P("tensor", "dp"),
            P("dp"),
        ),
        check_vma=False,
    )
```

```python
import jax
import jax.numpy as jnp
from jax import lax
from jax.experimental import pallas as pl
from jax.experimental.pallas import tpu as pltpu
from jax.sharding import PartitionSpec as P

HEAD_DIM = 64
norm_eps = 1e-06
masked_score = -1e30
AXES = ("dp", "tensor")
LOW = jnp.bfloat16
F32 = jnp.float32
TILE = 128
Y_BIT, CORE_BIT, X_BIT, Z_SHIFT = 1, 2, 4, 3
ANY = pl.BlockSpec(memory_space=pltpu.HBM)


def mm(left, right):
    return lax.dot_general(left, right, (((1,), (0,)), ((), ())), preferred_element_type=F32)


def mm_nt(left, right):
    return lax.dot_general(left, right, (((1,), (1,)), ((), ())), preferred_element_type=F32)


def mm_tn(left, right):
    return lax.dot_general(left, right, (((0,), (0,)), ((), ())), preferred_element_type=F32)


def whole(*shape):
    return pl.BlockSpec(shape, lambda t, me: (0,) * len(shape))


def call(body, grid, ins, outs, shapes, scratch, flops, moved, name, room=32, heavy=False):
    return pl.pallas_call(
        body,
        grid_spec=pltpu.PrefetchScalarGridSpec(
            num_scalar_prefetch=1,
            grid=grid,
            in_specs=ins,
            out_specs=outs,
            scratch_shapes=scratch,
        ),
        out_shape=shapes,
        compiler_params=pltpu.CompilerParams(
            dimension_semantics=("arbitrary",) * len(grid), vmem_limit_bytes=room << 20
        ),
        cost_estimate=pl.CostEstimate(
            flops=flops * 100 if heavy else 1, bytes_accessed=moved if heavy else 1, transcendentals=0
        ),
        name=name,
    )


def places(me, core_flip, first, second):
    owner = ((me >> 1) & 1) ^ core_flip
    off_y = jnp.where(owner == 0, first, second)
    off_x = jnp.where(owner == 0, second, first)
    return off_y, off_x


def dp_of(me, core_flip, off_x, off_z):
    core = ((me >> 1) & 1) ^ core_flip
    return (((me >> Z_SHIFT) ^ off_z) << 2) | ((((me >> 2) & 1) ^ off_x) << 1) | core


def fetch(me, pieces, store, sems, start, width):
    for index, piece in enumerate(pieces):
        core_flip, first, second = index >> 2, (index >> 1) & 1, index & 1
        off_y, off_x = places(me, core_flip, first, second)
        y_at = (me & 1) ^ off_y
        depth, rows, _ = piece.shape
        for off_z in range(depth):
            row = pl.multiple_of(dp_of(me, core_flip, off_x, off_z) * rows, rows)
            pltpu.make_async_copy(
                piece.at[off_z, :, pl.ds(start, width)],
                store.at[y_at, pl.ds(row, rows), :],
                sems.at[y_at],
            ).start()


def arrived(store, sems, y_at):
    pltpu.make_async_copy(store.at[y_at], store.at[y_at], sems.at[y_at]).wait()


def normed(rows, gain, shift):
    center = rows - jnp.mean(rows, axis=-1, keepdims=True)
    spread = jnp.mean(center * center, axis=-1, keepdims=True)
    return center * lax.rsqrt(spread + norm_eps) * gain + shift


def qkv_call(me, rows_in, pieces):
    count, width = rows_in.shape
    half = width // 2
    span = 3 * half

    def body(me_ref, x_ref, *refs):
        parts, refs = refs[:8], refs[8:]
        norm_ref, turn_ref, out_ref, table_ref, store, sems, vectors, vector_sems = refs
        step = pl.program_id(0)

        @pl.when(step == 0)
        def _():
            fetch(me_ref[0], parts, vectors, vector_sems, span, TILE)
            fetch(me_ref[0], parts, store, sems, 0, span)
            for y_at in range(2):
                arrived(vectors, vector_sems, y_at)
            table_ref[...] = vectors[0].astype(F32).T[: table_ref.shape[0]]

            @pl.loop(0, count // TILE)
            def _(i):
                at = pl.ds(pl.multiple_of(i * TILE, TILE), TILE)
                value = normed(x_ref[at, :], table_ref[0:1, :], table_ref[1:2, :])
                norm_ref[at, :] = value.astype(LOW)
                turn_ref[:, at] = value.T.astype(LOW)

        for y_at in range(2):

            @pl.when(step == 3 * y_at)
            def _():
                arrived(store, sems, y_at)

        y_at, kind = step // 3, step % 3
        col = pl.multiple_of(kind * half, half)
        own = pl.ds(pl.multiple_of(y_at * half, half), half)
        product = mm(norm_ref[...], store[y_at, :, pl.ds(col, half)])
        bias = jnp.where(kind == 0, table_ref[2:3, own], table_ref[3:4, own])
        bias = jnp.where(kind == 1, 0.0, bias)
        out_ref[...] = (product + bias).astype(LOW)

    return call(
        body,
        (6,),
        [whole(count, width)] + [ANY] * 8,
        [
            whole(count, width),
            whole(width, count),
            pl.BlockSpec((count, half), lambda t, me: (0, t)),
            whole(16, width),
        ],
        [
            jax.ShapeDtypeStruct((count, width), LOW),
            jax.ShapeDtypeStruct((width, count), LOW),
            jax.ShapeDtypeStruct((count, 2 * span), LOW),
            jax.ShapeDtypeStruct((16, width), F32),
        ],
        [
            pltpu.VMEM((2, width, span), LOW),
            pltpu.SemaphoreType.DMA((2,)),
            pltpu.VMEM((2, width, TILE), LOW),
            pltpu.SemaphoreType.DMA((2,)),
        ],
        2 * count * width * 2 * span,
        count * width * 16 + width * span * 4,
        "qkv",
        60,
    )(me, rows_in, *pieces)


def head_halves(shape):
    lane = lax.broadcasted_iota(jnp.int32, shape, 1)
    return lane < HEAD_DIM, lane >= HEAD_DIM


def attend_call(me, qkv, visible):
    images, _, seq = visible.shape
    count, full = qkv.shape
    half = full // 6

    def body(me_ref, qkv_ref, seen_ref, out_ref):
        seen = seen_ref[0] > 0

        @pl.loop(0, half // (2 * TILE))
        def _(pair):
            for part in range(2):
                col = pl.multiple_of((2 * pair + part) * TILE, TILE)
                query = qkv_ref[:, pl.ds(col, TILE)] * jnp.asarray(HEAD_DIM**-0.5, LOW)
                key = qkv_ref[:, pl.ds(half + col, TILE)]
                value = qkv_ref[:, pl.ds(2 * half + col, TILE)]
                lanes = head_halves(query.shape)
                mixed = []
                for keep in lanes:
                    scores = jnp.where(seen, mm_nt(jnp.where(keep, query, 0), key), masked_score)
                    exps = jnp.exp(scores - jnp.max(scores, axis=-1, keepdims=True))
                    total = jnp.sum(exps, axis=-1, keepdims=True)
                    mixed.append(mm(exps.astype(LOW), value) * (1.0 / total))
                out_ref[:, pl.ds(col, TILE)] = jnp.where(lanes[0], mixed[0], mixed[1]).astype(LOW)

    return call(
        body,
        (images, 2),
        [
            pl.BlockSpec((seq, 3 * half), lambda i, y, me: (i, y)),
            pl.BlockSpec((1, 1, seq), lambda i, y, me: (i, 0, 0)),
        ],
        pl.BlockSpec((seq, half), lambda i, y, me: (i, y)),
        jax.ShapeDtypeStruct((count, 2 * half), LOW),
        [],
        4 * count * seq * 2 * half * 4,
        count * full * 3,
        "attend",
    )(me, qkv, visible)


def project_call(me, mixed, rows_in, table, pieces):
    count, width = rows_in.shape
    half = width // 2

    def body(me_ref, mixed_ref, x_ref, table_ref, *refs):
        parts, (mid_ref, norm_ref, turn_ref, store, sems) = refs[:8], refs[8:]
        fetch(me_ref[0], parts, store, sems, 2 * width, half)
        arrived(store, sems, 0)
        mid_ref[...] = mm_nt(mixed_ref[:, :half], store[0])
        arrived(store, sems, 1)
        mid_ref[...] += mm_nt(mixed_ref[:, half:], store[1])

        @pl.loop(0, count // TILE)
        def _(i):
            at = pl.ds(pl.multiple_of(i * TILE, TILE), TILE)
            middle = x_ref[at, :] + (mid_ref[at, :] + table_ref[4:5, :])
            mid_ref[at, :] = middle
            value = normed(middle, table_ref[5:6, :], table_ref[6:7, :])
            norm_ref[at, :] = value.astype(LOW)
            turn_ref[:, at] = value.T.astype(LOW)

    return call(
        body,
        (1,),
        [whole(count, width), whole(count, width), whole(*table.shape)] + [ANY] * 8,
        [whole(count, width), whole(count, width), whole(width, count)],
        [
            jax.ShapeDtypeStruct((count, width), F32),
            jax.ShapeDtypeStruct((count, width), LOW),
            jax.ShapeDtypeStruct((width, count), LOW),
        ],
        [pltpu.VMEM((2, width, half), LOW), pltpu.SemaphoreType.DMA((2,))],
        2 * count * width * width,
        count * width * 14 + width * width * 2,
        "project",
    )(me, mixed, rows_in, table, *pieces)


def expand_call(me, normed_two, bias, pieces):
    count, width = normed_two.shape
    span = bias.shape[1] // 2
    chunk = span // 4

    def body(me_ref, norm_ref, bias_ref, *refs):
        parts, (hid_ref, slope_ref, store, sems) = refs[:8], refs[8:]
        step = pl.program_id(0)

        @pl.when(step == 0)
        def _():
            fetch(me_ref[0], parts, store, sems, 0, span)

        for y_at in range(2):

            @pl.when(step == 4 * y_at)
            def _():
                arrived(store, sems, y_at)

        y_at, col = step // 4, pl.multiple_of(step % 4 * chunk, chunk)
        pre = mm(norm_ref[...], store[y_at, :, pl.ds(col, chunk)]) + bias_ref[...]
        below = 0.5 + 0.5 * lax.erf(pre * 0.5**0.5)
        hid_ref[...] = (pre * below).astype(LOW)
        slope_ref[...] = (below + pre * jnp.exp(pre * pre * -0.5) * 0.3989422804014327).astype(LOW)

    out = pl.BlockSpec((count, chunk), lambda t, me: (0, t))
    return call(
        body,
        (8,),
        [whole(count, width), pl.BlockSpec((1, chunk), lambda t, me: (0, t))] + [ANY] * 8,
        [out, out],
        [jax.ShapeDtypeStruct((count, 2 * span), LOW)] * 2,
        [pltpu.VMEM((2, width, span), LOW), pltpu.SemaphoreType.DMA((2,))],
        2 * count * width * 2 * span,
        count * span * 8 + width * span * 4,
        "expand",
        60,
    )(me, normed_two, bias, *pieces)


def contract_call(me, hidden, slope, out_low, middle, table, pieces):
    count, width = middle.shape
    span = hidden.shape[1] // 2
    chunk = span // 4

    def body(me_ref, hid_ref, slope_ref, low_ref, mid_ref, table_ref, *refs):
        parts, (act_ref, pre_ref, sum_ref, store, sems) = refs[:8], refs[8:]
        step = pl.program_id(0)

        @pl.when(step == 0)
        def _():
            fetch(me_ref[0], parts, store, sems, 0, span)
            act_ref[...] = mid_ref[...] + table_ref[7:8, :]

        for y_at in range(2):

            @pl.when(step == 4 * y_at)
            def _():
                arrived(store, sems, y_at)

        y_at, col = step // 4, pl.multiple_of(step % 4 * chunk, chunk)
        weight = store[y_at, :, pl.ds(col, chunk)]
        act_ref[...] += mm_nt(hid_ref[...], weight)
        pre = mm(low_ref[...], weight) * slope_ref[...].astype(F32)
        pre_ref[...] = pre.astype(LOW)
        sum_ref[...] = jnp.sum(pre, axis=0, keepdims=True)

    part = pl.BlockSpec((count, chunk), lambda t, me: (0, t))
    return call(
        body,
        (8,),
        [part, part, whole(count, width), whole(count, width), whole(*table.shape)] + [ANY] * 8,
        [whole(count, width), part, pl.BlockSpec((1, chunk), lambda t, me: (0, t))],
        [
            jax.ShapeDtypeStruct((count, width), F32),
            jax.ShapeDtypeStruct((count, 2 * span), LOW),
            jax.ShapeDtypeStruct((1, 2 * span), F32),
        ],
        [pltpu.VMEM((2, width, span), LOW), pltpu.SemaphoreType.DMA((2,))],
        4 * count * width * 2 * span,
        count * span * 12 + width * span * 4,
        "contract",
        heavy=True,
    )(me, hidden, slope, out_low, middle, table, *pieces)


def norm_back_call(me, low, start, gain_row, rows_in, base, table, pieces, keep_low, name):
    count, width = rows_in.shape
    span = low.shape[1] // 2
    chunk = span // 2

    def body(me_ref, low_ref, x_ref, base_ref, table_ref, *refs):
        parts, outs = refs[:8], refs[8:]
        if keep_low:
            grad_ref, vec_ref, out_low_ref, turn_ref, store, sems = outs
        else:
            grad_ref, vec_ref, store, sems = outs
        step = pl.program_id(0)

        @pl.when(step == 0)
        def _():
            fetch(me_ref[0], parts, store, sems, start, span)

        for y_at in range(2):

            @pl.when(step == 2 * y_at)
            def _():
                arrived(store, sems, y_at)

        y_at, col = step // 2, pl.multiple_of(step % 2 * chunk, chunk)
        product = mm_nt(low_ref[...], store[y_at, :, pl.ds(col, chunk)])

        @pl.when(step == 0)
        def _():
            grad_ref[...] = product

        @pl.when(step > 0)
        def _():
            grad_ref[...] += product

        @pl.when(step == 3)
        def _():
            vec_ref[...] = jnp.zeros_like(vec_ref)

            @pl.loop(0, count // TILE)
            def _(i):
                at = pl.ds(pl.multiple_of(i * TILE, TILE), TILE)
                back = grad_ref[at, :]
                rows = x_ref[at, :]
                center = rows - jnp.mean(rows, axis=-1, keepdims=True)
                spread = jnp.mean(center * center, axis=-1, keepdims=True)
                scale = lax.rsqrt(spread + norm_eps)
                unit = center * scale
                inner = back * table_ref[gain_row : gain_row + 1, :]
                along = jnp.mean(inner * unit, axis=-1, keepdims=True)
                level = jnp.mean(inner, axis=-1, keepdims=True)
                grad = base_ref[at, :] + scale * (inner - level - unit * along)
                grad_ref[at, :] = grad
                vec_ref[0:1, :] += jnp.sum(back * unit, axis=0, keepdims=True)
                vec_ref[1:2, :] += jnp.sum(back, axis=0, keepdims=True)
                vec_ref[2:3, :] += jnp.sum(grad, axis=0, keepdims=True)
                if keep_low:
                    out_low_ref[at, :] = grad.astype(LOW)
                    turn_ref[:, at] = grad.T.astype(LOW)

    outs = [whole(count, width), whole(8, width)]
    shapes = [jax.ShapeDtypeStruct((count, width), F32), jax.ShapeDtypeStruct((8, width), F32)]
    if keep_low:
        outs += [whole(count, width), whole(width, count)]
        shapes += [
            jax.ShapeDtypeStruct((count, width), LOW),
            jax.ShapeDtypeStruct((width, count), LOW),
        ]
    return call(
        body,
        (4,),
        [
            pl.BlockSpec((count, chunk), lambda t, me: (0, t)),
            whole(count, width),
            whole(count, width),
            whole(*table.shape),
        ]
        + [ANY] * 8,
        outs,
        shapes,
        [pltpu.VMEM((2, width, span), LOW), pltpu.SemaphoreType.DMA((2,))],
        2 * count * width * 2 * span,
        count * width * 16 + width * span * 4 + count * span * 4,
        name,
        32 if keep_low else 60,
    )(me, low, rows_in, base, table, *pieces)


def mixed_back_call(me, middle_low, pieces):
    count, width = middle_low.shape
    half = width // 2

    def body(me_ref, low_ref, *refs):
        parts, (out_ref, store, sems) = refs[:8], refs[8:]
        step = pl.program_id(0)

        @pl.when(step == 0)
        def _():
            fetch(me_ref[0], parts, store, sems, 2 * width, half)

        for y_at in range(2):

            @pl.when(step == y_at)
            def _():
                arrived(store, sems, y_at)

        out_ref[...] = mm(low_ref[...], store[step]).astype(LOW)

    return call(
        body,
        (2,),
        [whole(count, width)] + [ANY] * 8,
        pl.BlockSpec((count, half), lambda t, me: (0, t)),
        jax.ShapeDtypeStruct((count, width), LOW),
        [pltpu.VMEM((2, width, half), LOW), pltpu.SemaphoreType.DMA((2,))],
        2 * count * width * width,
        count * width * 4 + width * width * 2,
        "mixed_back",
    )(me, middle_low, *pieces)


def attend_back_call(me, qkv, grads, visible):
    images, seq, _ = visible.shape
    count, full = qkv.shape
    half = full // 6
    scale = HEAD_DIM**-0.5

    def body(me_ref, qkv_ref, grad_ref, seen_ref, out_ref, sum_ref):
        seen = seen_ref[0] > 0
        @pl.loop(0, half // (2 * TILE))
        def _(pair):
            for part in range(2):
                col = pl.multiple_of((2 * pair + part) * TILE, TILE)
                query = qkv_ref[:, pl.ds(col, TILE)] * jnp.asarray(scale, LOW)
                key = qkv_ref[:, pl.ds(half + col, TILE)]
                value = qkv_ref[:, pl.ds(2 * half + col, TILE)]
                grad = grad_ref[:, pl.ds(col, TILE)]
                lanes = head_halves(query.shape)
                parts = []
                for keep in lanes:
                    scores = jnp.where(seen, mm_nt(jnp.where(keep, key, 0), query), masked_score)
                    exps = jnp.exp(scores - jnp.max(scores, axis=0, keepdims=True))
                    probs = exps * (1.0 / jnp.sum(exps, axis=0, keepdims=True))
                    prob_grad = mm_nt(jnp.where(keep, value, 0), grad)
                    row_dot = jnp.sum(probs * prob_grad, axis=0, keepdims=True)
                    score_grad = (probs * (prob_grad - row_dot)).astype(LOW)
                    parts.append(
                        (
                            mm_tn(key, score_grad).T * scale,
                            mm(score_grad, query),
                            mm(probs.astype(LOW), grad),
                        )
                    )
                for at in range(3):
                    merged = jnp.where(lanes[0], parts[0][at], parts[1][at])
                    put = at * half + col
                    out_ref[:, pl.ds(put, TILE)] = merged.astype(LOW)
                    sum_ref[0, 0, :, pl.ds(put, TILE)] = jnp.sum(merged, axis=0, keepdims=True)

    return call(
        body,
        (images, 2),
        [
            pl.BlockSpec((seq, 3 * half), lambda i, y, me: (i, y)),
            pl.BlockSpec((seq, half), lambda i, y, me: (i, y)),
            pl.BlockSpec((1, seq, 1), lambda i, y, me: (i, 0, 0)),
        ],
        [
            pl.BlockSpec((seq, 3 * half), lambda i, y, me: (i, y)),
            pl.BlockSpec((1, 1, 1, 3 * half), lambda i, y, me: (i, y, 0, 0)),
        ],
        [
            jax.ShapeDtypeStruct((count, full), LOW),
            jax.ShapeDtypeStruct((images, 2, 1, 3 * half), F32),
        ],
        [],
        10 * count * seq * 2 * half * 4,
        count * full * 5,
        "attend_back",
    )(me, qkv, grads, visible)


def weight_grad_call(me, turned, right, depth, core_flip, received, name):
    width, count = turned.shape
    span = right.shape[1] // 2
    chunk = next(c for c in (1024, 768, 512, 384, 256, 128) if span % c == 0)
    parts = span // chunk
    steps = 2 * parts
    rows = width // (4 * depth)
    quarter = width // 4

    def body(me_ref, turn_ref, right_ref, *refs):
        if core_flip:
            (far_ref, lefts, ready, sems) = refs
        else:
            (got_ref, kept_ref, sent_ref, lefts, ready, sems, got, got_sems) = refs
        step = pl.program_id(0)
        slot = step % 2
        owner = ((me_ref[0] >> 1) & 1) ^ core_flip

        def spot(off_y, off_x):
            return jnp.where(owner == 0, off_y, off_x), jnp.where(owner == 0, off_x, off_y)

        def fetched(at, off_x):
            first, second = spot(1 - at // parts, off_x)
            col = pl.multiple_of(at % parts * chunk, chunk)
            return pltpu.make_async_copy(
                got_ref.at[first, second, :, :, pl.ds(col, chunk)],
                got.at[at, off_x],
                got_sems.at[at, off_x],
            )

        def leaving(target, at, off_x):
            col = pl.multiple_of(at % parts * chunk, chunk)
            return pltpu.make_async_copy(
                ready.at[at % 2, off_x],
                target.at[:, :, pl.ds(col, chunk)],
                sems.at[at % 2, off_x],
            )

        @pl.when(step == 0)
        def _():
            if not core_flip:
                for at in range(steps):
                    for off_x in range(2):
                        fetched(at, off_x).start()
            for off_x in range(2):
                for off_z in range(depth):
                    row = pl.multiple_of(dp_of(me_ref[0], core_flip, off_x, off_z) * rows, rows)
                    put = off_x * quarter + off_z * rows
                    lefts[put : put + rows, :] = turn_ref[pl.ds(row, rows), :]

        product = mm(lefts[...], right_ref[...]).reshape(2, depth, rows, chunk)

        @pl.when(step >= 2)
        def _():
            for off_x in range(2):
                some = far_ref.at[0, 0] if core_flip else kept_ref.at[0]
                leaving(some, step, off_x).wait()

        for off_x in range(2):
            total = product[off_x]
            if not core_flip:
                fetched(step, off_x).wait()
                total = total + got[step, off_x].astype(F32)
            ready[slot, off_x] = total.astype(LOW)
            first, second = spot(1 - step // parts, off_x)
            if core_flip:
                leaving(far_ref.at[first, second], step, off_x).start()
            else:
                for at, target in enumerate((kept_ref, sent_ref)):

                    @pl.when(first == at)
                    def _():
                        leaving(target.at[second], step, off_x).start()

        @pl.when(step == steps - 1)
        def _():
            for back in range(min(2, steps)):
                for off_x in range(2):
                    some = far_ref.at[0, 0] if core_flip else kept_ref.at[0]
                    leaving(some, step - back, off_x).wait()

    def right_at(t, me):
        return 0, ((me[0] & 1) ^ (1 - t // parts)) * parts + t % parts

    ins = [whole(width, count), pl.BlockSpec((count, chunk), right_at)]
    scratch = [
        pltpu.VMEM((2 * quarter, count), LOW),
        pltpu.VMEM((2, 2, depth, rows, chunk), LOW),
        pltpu.SemaphoreType.DMA((2, 2)),
    ]
    if core_flip:
        outs = ANY
        shapes = jax.ShapeDtypeStruct((2, 2, depth, rows, span), LOW)
        extra = ()
    else:
        ins = ins + [ANY]
        outs = [ANY, ANY]
        shapes = [jax.ShapeDtypeStruct((2, depth, rows, span), LOW)] * 2
        extra = (received,)
        scratch += [
            pltpu.VMEM((steps, 2, depth, rows, chunk), LOW),
            pltpu.SemaphoreType.DMA((steps, 2)),
        ]
    return call(
        body,
        (steps,),
        ins,
        outs,
        shapes,
        scratch,
        2 * count * width * span,
        count * (width + span * 2) * 2 + width * span * 4,
        name,
    )(me, turned, right, *extra)


def swap(value, size, bits, other=None):
    other = bits if other is None else other
    return lax.ppermute(
        value, AXES, [(i, i ^ (other if i & CORE_BIT else bits)) for i in range(size)]
    )


def after(value, *others):
    return lax.optimization_barrier((value, *others))[0]


def along_depth(piece, size, steps):
    return [piece] + [swap(piece, size, k << Z_SHIFT) for k in steps]


def along_first(value, size):
    return swap(value, size, Y_BIT, X_BIT)


def along_second(value, size):
    return swap(value, size, X_BIT, Y_BIT)


def along_core(value, size):
    return swap(value, size, CORE_BIT)


class Scatter:
    def __init__(self, turned, right, size, depth, name):
        self.size, self.depth, self.name = size, depth, name
        self.turned, self.right = turned, right

    def far(self, me):
        self.me = me
        self.sent = weight_grad_call(
            me, self.turned, self.right, self.depth, 1, None, self.name + "_far"
        )
        self.received = swap(self.sent, self.size, CORE_BIT)
        return self.sent

    def near(self, *others):
        right = after(self.right, *others)
        self.kept, self.sent = weight_grad_call(
            self.me, self.turned, right, self.depth, 0, self.received, self.name + "_near"
        )
        self.received = swap(self.sent, self.size, Y_BIT, X_BIT)
        return self.kept

    def second(self, *others, joined=()):
        kept = after(self.kept, *others)
        total = (kept.astype(F32) + self.received.astype(F32)).astype(LOW)
        for other in joined:
            kept = after(other.kept, *others)
            more = (kept.astype(F32) + other.received.astype(F32)).astype(LOW)
            total = jnp.concatenate([total, more], axis=-1)
        self.kept = total[0]
        self.received = swap(total[1], self.size, X_BIT, Y_BIT)
        return self.kept

    def third(self, *others):
        kept = after(self.kept, *others)
        total = (kept.astype(F32) + self.received.astype(F32)).astype(LOW)
        self.kept = total[0]
        self.received = [
            swap(total[k], self.size, k << Z_SHIFT) for k in range(1, self.depth)
        ]
        return self.kept

    def last(self, *others):
        result = after(self.kept, *others).astype(F32)
        for value in self.received:
            result = result + value.astype(F32)
        return result


def shards(
    inputs,
    key_mask,
    ln1_gain,
    ln1_bias,
    w_qkv,
    qv_bias,
    w_proj,
    proj_bias,
    ln2_gain,
    ln2_bias,
    w_fc1,
    fc1_bias,
    w_fc2,
    fc2_bias,
    out_grad,
):
    tensor_rank = lax.axis_index("tensor")
    dp_rank = lax.axis_index("dp")
    dp_size = lax.axis_size("dp")
    size = 2 * dp_size
    depth = dp_size // 4
    own_images, seq, width = inputs.shape
    count = own_images * seq
    half = w_qkv.shape[2]
    rows = ln1_gain.shape[0]
    me = jnp.reshape(dp_rank * 2 + tensor_rank, (1,)).astype(jnp.int32)

    vectors = jnp.concatenate(
        [
            jnp.stack([ln1_gain, ln1_bias, qv_bias[0], qv_bias[1]]),
            jnp.stack([proj_bias, ln2_gain, ln2_bias, fc2_bias]),
            fc1_bias.reshape(4, rows),
        ]
    )
    vectors = jnp.pad(vectors, ((0, TILE - vectors.shape[0]), (0, 0))).T
    piece_one = jnp.concatenate([w_qkv[0], w_qkv[1], w_qkv[2], vectors], axis=1).astype(LOW)
    piece_two = jnp.concatenate([w_fc1, w_proj.T], axis=1).astype(LOW)
    piece_three = w_fc2.T.astype(LOW)

    held_one = jnp.stack(along_depth(piece_one, size, range(1, depth)))
    grad_in = out_grad.reshape(count, width)
    out_low = grad_in.astype(LOW)
    out_turned = out_low.T
    held_one, piece_two, out_low, out_turned = lax.optimization_barrier(
        (held_one, piece_two, out_low, out_turned)
    )
    first_one = along_first(held_one, size)
    second_one = along_second(held_one, size)
    far_one = [along_core(held_one, size)]
    deep_two = along_depth(piece_two, size, range(1, depth - 1))
    first_one, second_one, far_own, *deep_two = lax.optimization_barrier(
        (first_one, second_one, *far_one, *deep_two)
    )
    both_one = along_second(first_one, size)
    far_one = [far_own, along_core(second_one, size), along_core(first_one, size)]
    plane_one = [held_one, second_one, first_one]
    deep_two += along_depth(deep_two[0], size, [depth - 1])[1:]
    far_one += [along_core(both_one, size)]
    both_one, piece_three, *deep_two = lax.optimization_barrier((both_one, piece_three, *deep_two))
    pieces_one = plane_one + [both_one] + far_one
    held_two = jnp.stack(deep_two)
    first_two = along_first(held_two, size)
    second_two = along_second(held_two, size)
    far_two = [along_core(held_two, size)]
    deep_three = along_depth(piece_three, size, range(1, depth - 1))

    rows_in = inputs.reshape(count, width)
    own_mask = lax.dynamic_slice_in_dim(key_mask, tensor_rank * own_images, own_images, 0)
    visible = jnp.concatenate(
        [jnp.ones((own_images, seq - key_mask.shape[1]), jnp.int32), own_mask], axis=1
    )
    visible_rows = after(visible, held_one)[:, :, None]
    visible = visible[:, None, :]

    normed_one, turned_one, qkv, table = qkv_call(me, rows_in, pieces_one)
    fc1_full = table[8:12].reshape(4, dp_size, rows).transpose(1, 0, 2).reshape(1, 4 * width)
    qkv, first_two, second_two, *deep_three, far_own = lax.optimization_barrier(
        (qkv, first_two, second_two, *deep_three, *far_two)
    )
    both_two = along_second(first_two, size)
    far_two = [far_own, along_core(second_two, size), along_core(first_two, size)]
    plane_two = [held_two, second_two, first_two]
    deep_three += along_depth(deep_three[0], size, [depth - 1])[1:]
    mixed = attend_call(me, qkv, visible)
    mixed, fc1_full, both_two, *far_two = lax.optimization_barrier(
        (mixed, fc1_full, both_two, *far_two)
    )
    far_two += [along_core(both_two, size)]
    both_two, *deep_three = lax.optimization_barrier((both_two, *deep_three))
    pieces_two = plane_two + [both_two] + far_two
    held_three = jnp.stack(deep_three)
    first_three = along_first(held_three, size)
    second_three = along_second(held_three, size)
    far_three = [along_core(held_three, size)]
    middle, normed_two, turned_two = project_call(me, mixed, rows_in, table, pieces_two)
    hidden, slope = expand_call(me, normed_two, fc1_full, pieces_two)
    hidden, first_three, second_three, far_own = lax.optimization_barrier(
        (hidden, first_three, second_three, *far_three)
    )
    both_three = along_second(first_three, size)
    far_three = [far_own, along_core(second_three, size), along_core(first_three, size)]
    plane_three = [held_three, second_three, first_three]
    fc2 = Scatter(out_turned, hidden, size, depth, "fc2_grad")
    done = fc2.far(me)
    both_three = after(both_three, done)
    far_three += [along_core(both_three, size)]
    pieces_three = plane_three + [both_three] + far_three
    outputs, pre_low, fc1_sum = contract_call(
        me, after(hidden, done), slope, out_low, middle, table, pieces_three
    )
    fc1 = Scatter(turned_two, pre_low, size, depth, "fc1_grad")
    done = fc1.far(me)
    done = fc2.near(done)
    middle_grad, vec_two, middle_low, turned_mid = norm_back_call(
        me, after(pre_low, done), 0, 5, middle, grad_in, table, pieces_two, True, "norm_two_back"
    )
    mixed_grad = mixed_back_call(me, middle_low, pieces_two)
    proj = Scatter(turned_mid, after(mixed, mixed_grad), size, depth, "proj_grad")
    done = proj.far(me)
    done = fc2.second(done)
    done = proj.near(done)
    done = fc1.near(done)
    done = fc2.third(done)
    qkv_low, qkv_sum = attend_back_call(me, qkv, after(mixed_grad, done), visible_rows)
    done = fc1.second(qkv_low, proj.received, *fc2.received, joined=[proj])
    qkv_out = Scatter(turned_one, after(qkv_low, done), size, depth, "qkv_grad")
    done = qkv_out.far(me)
    done = qkv_out.near(done)
    input_grad, vec_one = norm_back_call(
        me,
        after(qkv_low, done),
        0,
        0,
        rows_in,
        middle_grad,
        table,
        pieces_one,
        False,
        "norm_one_back",
    )

    qkv_sum = jnp.sum(qkv_sum, axis=(0, 2)).reshape(2, 3, half)
    sums = jnp.concatenate(
        [
            vec_one[:2],
            qkv_sum[:, 0].reshape(1, width),
            qkv_sum[:, 2].reshape(1, width),
            vec_two[2:3],
            vec_two[:2],
            jnp.sum(grad_in, axis=0, keepdims=True),
            fc1_sum.reshape(4, width),
        ]
    )
    done = fc1.third(input_grad)
    done = qkv_out.second(done)
    sums = after(sums, done)
    for bits in (CORE_BIT, X_BIT, Y_BIT):
        sums = sums + swap(sums, size, bits)
    done = qkv_out.third(sums, *fc1.received)
    sums = after(sums, qkv_out.received[0])
    fc2_grad = fc2.last(sums)
    fc1_grad = fc1.last(sums)
    fc1_grad, proj_grad = fc1_grad[:, : 4 * half], fc1_grad[:, 4 * half :]
    sums = sum(along_depth(sums, size, range(1, depth)))
    qkv_grad = qkv_out.last()
    mine = lax.dynamic_slice_in_dim(sums[:8], dp_rank * rows, rows, 1)
    fc1_mine = lax.dynamic_slice_in_dim(sums[8:].reshape(-1), dp_rank * 4 * rows, 4 * rows, 0)
    return (
        outputs.reshape(inputs.shape),
        input_grad.reshape(inputs.shape),
        mine[0],
        mine[1],
        qkv_grad.reshape(rows, 3, half).transpose(1, 0, 2),
        mine[2:4],
        proj_grad.T,
        mine[4],
        mine[5],
        mine[6],
        fc1_grad,
        fc1_mine,
        fc2_grad.T,
        mine[7],
    )


def solution(mesh):
    placed = (
        P(("dp", "tensor"), None, None),
        P("dp", None),
        P("dp"),
        P("dp"),
        P(None, "dp", "tensor"),
        P(None, "dp"),
        P("tensor", "dp"),
        P("dp"),
        P("dp"),
        P("dp"),
        P("dp", "tensor"),
        P("dp"),
        P("tensor", "dp"),
        P("dp"),
        P(("dp", "tensor"), None, None),
    )
    return jax.shard_map(
        shards,
        mesh=mesh,
        in_specs=placed,
        out_specs=(
            P(("dp", "tensor"), None, None),
            P(("dp", "tensor"), None, None),
            P("dp"),
            P("dp"),
            P(None, "dp", "tensor"),
            P(None, "dp"),
            P("tensor", "dp"),
            P("dp"),
            P("dp"),
            P("dp"),
            P("dp", "tensor"),
            P("dp"),
            P("tensor", "dp"),
            P("dp"),
        ),
        check_vma=False,
    )
```
